32 devices in a mesh: dp: 8 (over y, x, core), tensor: 4 (over z).
Axes of the slice: x: 2, y: 2, z: 4, core: 2. Of those that a mesh axis runs over, the one named last changes fastest.
Arguments:
- inputs: bfloat16 [32768, 768], P(('dp', 'tensor')), may hold values from -6 to 6
- cotangent: bfloat16 [32768, 768], P(('dp', 'tensor')), may hold values from -6 to 6
- w_query: bfloat16 [768, 768], P('dp', 'tensor'), may hold values from -0.21875 to 0.21875
- w_key: bfloat16 [768, 768], P('dp', 'tensor'), may hold values from -0.21875 to 0.21875
- w_value: bfloat16 [768, 768], P('dp', 'tensor'), may hold values from -0.21875 to 0.21875
- w_output: bfloat16 [768, 768], P('tensor', 'dp'), may hold values from -2.5 to 2.5
- w_up: bfloat16 [768, 3072], P('dp', 'tensor'), may hold values from -0.21875 to 0.21875
- w_down: bfloat16 [3072, 768], P('tensor', 'dp'), may hold values from -0.109375 to 0.109375
- b_query: float32 [768], P('tensor'), may hold values from -3 to 3
- b_value: float32 [768], P('tensor'), may hold values from -3 to 3
- b_output: float32 [768], replicated, may hold values from -3 to 3
- gain_attn: float32 [768], replicated, may hold values from 0.1 to 1.9
- bias_attn: float32 [768], replicated, may hold values from -3 to 3
- b_up: float32 [3072], P('tensor'), may hold values from -3 to 3
- b_down: float32 [768], replicated, may hold values from -3 to 3
- gain_mlp: float32 [768], replicated, may hold values from 0.1 to 1.9
- bias_mlp: float32 [768], replicated, may hold values from -3 to 3
- random_blocks: int32 [12, 64, 3], P('tensor'), may hold values from 1 to 62, as said below
Outputs:
- layer_out: bfloat16 [32768, 768], P(('dp', 'tensor'))
- grad_input: bfloat16 [32768, 768], P(('dp', 'tensor'))
- grad_w_query: float32 [768, 768], P('dp', 'tensor')
- grad_w_key: float32 [768, 768], P('dp', 'tensor')
- grad_w_value: float32 [768, 768], P('dp', 'tensor')
- grad_w_output: float32 [768, 768], P('tensor', 'dp')
- grad_w_up: float32 [768, 3072], P('dp', 'tensor')
- grad_w_down: float32 [3072, 768], P('tensor', 'dp')
- grad_b_query: float32 [768], P('tensor')
- grad_b_value: float32 [768], P('tensor')
- grad_b_output: float32 [768], replicated
- grad_gain_attn: float32 [768], replicated
- grad_bias_attn: float32 [768], replicated
- grad_b_up: float32 [3072], P('tensor')
- grad_b_down: float32 [768], replicated
- grad_gain_mlp: float32 [768], replicated
- grad_bias_mlp: float32 [768], replicated
The draws below stay inside these ranges and needn't reach their ends.
Inputs may be any that keep to these rules, and one draw needn't show every extreme that they name: random_blocks[h, i] names 3 different blocks of the same sequence, none of them 0, 63, i - 1, i or i + 1.
All inputs are finite; a program needn't handle non-finite values.
Results may differ from the reference program's by a relative error of at most 0.02.
Values may be sent and summed in bfloat16 or wider, within the bound.
No kernel may reach another device: no remote copies, remote signals or barrier semaphores. Data moves between devices by JAX's collectives and lax.ppermute only.
A program may use at most 256 MiB of HBM per device.

```python
import jax
import jax.numpy as jnp
from jax import lax

D = 768
H = 12
HD = 64
FF = 3072
BLOCK = 64
RAND = 3
LENGTH = 4096
TOKENS = 32768


def draw_random_blocks(key, part):
    nblocks = LENGTH // BLOCK
    scores = jax.random.randint(key, (H, nblocks, nblocks), 0, 2 ** 20, dtype=jnp.int32) * nblocks + jnp.arange(nblocks, dtype=jnp.int32)[None, None, :]
    row_index = jnp.arange(nblocks, dtype=jnp.int32)[:, None]
    column = jnp.arange(nblocks, dtype=jnp.int32)[None, :]
    banned = (column == 0) | (column == nblocks - 1) | (jnp.abs(column - row_index) <= 1)
    scores = jnp.where(banned[None], -1, scores)
    return lax.top_k(scores, RAND)[1].astype(jnp.int32)


def steps_of(own_key, dims, pieces, least, high):
    loudness, own = 1.0, jax.random.fold_in(own_key, 6)
    for dim, blocks in pieces:
        steps = jnp.exp(jax.random.uniform(jax.random.fold_in(own, dim), (blocks,), jnp.float32, least / len(pieces), high / len(pieces)))
        loudness = loudness * jnp.repeat(steps, dims[dim] // blocks).reshape([-1 if axis == dim else 1 for axis in range(len(dims))])
    return loudness


def normal_values(key, shape, width, bound, shards=(), kind=jnp.bfloat16):
    values = width * jax.random.normal(key, shape, jnp.float32)
    if shards:
        values = values * steps_of(key, shape, shards, -0.22, 0.18)
    return jnp.clip(values, -bound, bound).astype(kind)


def setup_inputs(seed: int = 0) -> dict:
    splits = jax.random.split(jax.random.key(seed), 19)
    return {
        "inputs": normal_values(splits[0], (TOKENS, D), 1.0, 6.0, ((0, 32),)),
        "cotangent": normal_values(splits[1], (TOKENS, D), 1.0, 6.0, ((0, 32),)),
        "w_query": normal_values(splits[2], (D, D), D ** -0.5, 0.21875, ((0, 8), (1, 4))),
        "w_key": normal_values(splits[3], (D, D), D ** -0.5, 0.21875, ((0, 8), (1, 4))),
        "w_value": normal_values(splits[4], (D, D), D ** -0.5, 0.21875, ((0, 8), (1, 4))),
        "w_output": normal_values(splits[5], (D, D), (max(D // 128, 1)) ** -0.5, 2.5, ((0, 4), (1, 8))),
        "w_up": normal_values(splits[6], (D, FF), D ** -0.5, 0.21875, ((0, 8), (1, 4))),
        "w_down": normal_values(splits[7], (FF, D), FF ** -0.5, 0.109375, ((0, 4), (1, 8))),
        "b_query": normal_values(splits[8], (D,), 0.5, 3.0, ((0, 4),), jnp.float32),
        "b_value": normal_values(splits[9], (D,), 0.5, 3.0, ((0, 4),), jnp.float32),
        "b_output": normal_values(splits[10], (D,), 0.5, 3.0, (), jnp.float32),
        "gain_attn": jnp.clip(1.0 + 0.18 * jax.random.normal(splits[11], (D,), jnp.float32), 0.1, 1.9),
        "bias_attn": normal_values(splits[12], (D,), 0.5, 3.0, (), jnp.float32),
        "b_up": normal_values(splits[13], (FF,), 0.5, 3.0, ((0, 4),), jnp.float32),
        "b_down": normal_values(splits[14], (D,), 0.5, 3.0, (), jnp.float32),
        "gain_mlp": jnp.clip(1.0 + 0.18 * jax.random.normal(splits[15], (D,), jnp.float32), 0.1, 1.9),
        "bias_mlp": normal_values(splits[16], (D,), 0.5, 3.0, (), jnp.float32),
        "random_blocks": draw_random_blocks(jax.random.fold_in(splits[18], 71), 0),
    }


@jax.custom_vjp
def low(v):
    return lax.optimization_barrier(v.astype(jnp.bfloat16)).astype(jnp.float32)

@jax.custom_vjp
def low_back(v):
    return v

def low_keep(v):
    return (low(v), None)

def low_pass(kept, grad):
    return (grad,)

def back_keep(v):
    return (v, None)

def back_low(kept, grad):
    return (low(grad),)
low.defvjp(low_keep, low_pass)
low_back.defvjp(back_keep, back_low)
negative = -1e+30
epsilon = 1e-05

def matmul(left, right):
    return jnp.dot(left, right, preferred_element_type=jnp.float32, precision=lax.Precision.HIGHEST)

def build_keys(random_blocks, nblocks):
    block_index = jnp.arange(nblocks, dtype=jnp.int32)
    fixed_blocks = jnp.stack([jnp.zeros_like(block_index), jnp.full_like(block_index, nblocks - 1), block_index - 1, block_index, block_index + 1], axis=-1)
    fixed_blocks = jnp.clip(fixed_blocks, 0, nblocks - 1)
    always_on = jnp.ones((nblocks,), dtype=bool)
    valid_keys = jnp.stack([always_on, always_on, (block_index - 1 >= 1) & (block_index - 1 <= nblocks - 2), (block_index >= 1) & (block_index <= nblocks - 2), block_index + 1 <= nblocks - 2] + [always_on] * random_blocks.shape[-1], axis=-1)
    head_count = random_blocks.shape[0]
    key_table = jnp.concatenate([jnp.broadcast_to(fixed_blocks[None], (head_count, nblocks, 5)), random_blocks.astype(jnp.int32)], axis=-1)
    return (key_table, valid_keys)

def gather_blocks(source, chosen):
    return jax.vmap(lambda head_source, head_index: head_source[head_index])(source, chosen)

def attention(query_rows, key_rows, value_rows, random_blocks):
    nblocks = LENGTH // BLOCK
    key_table, valid_keys = build_keys(random_blocks, nblocks)
    key_mask = jnp.repeat(valid_keys, BLOCK, axis=1)
    group_blocks = 8

    def rows_to_heads(matrix):
        return matrix.reshape(nblocks, BLOCK, H, HD).transpose(2, 0, 1, 3)
    query_heads = rows_to_heads(query_rows)
    key_heads = rows_to_heads(key_rows)
    value_heads = rows_to_heads(value_rows)

    def one_group(group_id):
        first_block = group_id * group_blocks
        query_part = lax.dynamic_slice_in_dim(query_heads, first_block, group_blocks, 1)
        chosen = lax.dynamic_slice_in_dim(key_table, first_block, group_blocks, 1)
        allowed = lax.dynamic_slice_in_dim(key_mask, first_block, group_blocks, 0)
        key_part = gather_blocks(key_heads, chosen).reshape(H, group_blocks, -1, HD)
        value_part = gather_blocks(value_heads, chosen).reshape(H, group_blocks, -1, HD)
        scores = jnp.einsum('hgqd,hgkd->hgqk', query_part, key_part, precision=lax.Precision.HIGHEST) * HD ** (-0.5)
        scores = low_back(scores)
        scores = jnp.where(allowed[None, :, None, :], scores, negative)
        row_max = lax.optimization_barrier(jnp.max(scores, axis=-1, keepdims=True))
        expo_scores = jnp.exp(scores - row_max)
        softmax_probs = expo_scores / lax.optimization_barrier(jnp.sum(expo_scores, axis=-1, keepdims=True))
        return jnp.einsum('hgqk,hgkd->hgqd', low(softmax_probs), value_part, precision=lax.Precision.HIGHEST)
    blocks = lax.map(jax.checkpoint(one_group), jnp.arange(nblocks // group_blocks))
    return blocks.transpose(0, 2, 3, 1, 4).reshape(LENGTH, H * HD)

def layer_norm(hidden, gain, shift):
    center = hidden - lax.optimization_barrier(jnp.mean(hidden, axis=-1, keepdims=True))
    variance = lax.optimization_barrier(jnp.mean(center * center, axis=-1, keepdims=True))
    return center * lax.rsqrt(variance + epsilon) * gain + shift

def forward(feed_rows, weights, random_blocks):
    w_query, w_key, w_value, w_output, w_up, w_down, b_query, b_value, b_output, gain_attn, bias_attn, b_up, b_down, gain_mlp, bias_mlp = weights
    query_rows = low(low_back(matmul(feed_rows, w_query) + b_query))
    key_rows = low(low_back(matmul(feed_rows, w_key)))
    value_rows = low(low_back(matmul(feed_rows, w_value) + b_value))
    mixed_rows = low(low_back(attention(query_rows, key_rows, value_rows, random_blocks)))
    attn_out = low_back(matmul(mixed_rows, w_output)) + b_output
    normed = layer_norm(feed_rows + attn_out, gain_attn, bias_attn)
    normed_low = low(normed)
    hidden_pre = low_back(matmul(normed_low, w_up) + b_up)
    hidden_low = low(jax.nn.gelu(hidden_pre, approximate=False))
    mlp_out = low_back(matmul(hidden_low, w_down)) + b_down
    return layer_norm(normed + mlp_out, gain_mlp, bias_mlp)

def reference(inputs, cotangent, w_query, w_key, w_value, w_output, w_up, w_down, b_query, b_value, b_output, gain_attn, bias_attn, b_up, b_down, gain_mlp, bias_mlp, random_blocks):
    params = tuple((weight.astype(jnp.float32) for weight in (w_query, w_key, w_value, w_output, w_up, w_down, b_query, b_value, b_output, gain_attn, bias_attn, b_up, b_down, gain_mlp, bias_mlp)))
    sequences = inputs.shape[0] // LENGTH
    seq_inputs = inputs.astype(jnp.float32).reshape(sequences, LENGTH, D)
    seq_cotangent = cotangent.astype(jnp.float32).reshape(sequences, LENGTH, D)

    def one_sequence(totals, seq_pair):
        seq_rows, seq_grad = seq_pair
        result, pullback = jax.vjp(lambda feed_rows, *weights: forward(feed_rows, weights, random_blocks), seq_rows, *params)
        grads = pullback(seq_grad)
        new_totals = tuple((total_item + grad_item for total_item, grad_item in zip(totals, grads[1:])))
        return (new_totals, (result, grads[0]))
    initial = tuple((jnp.zeros_like(weight) for weight in params))
    totals, (outputs, input_grads) = lax.scan(one_sequence, initial, (seq_inputs, seq_cotangent))
    layer_out = outputs.reshape(-1, D).astype(jnp.bfloat16)
    grad_input = input_grads.reshape(-1, D).astype(jnp.bfloat16)
    return (layer_out, grad_input, totals[0], totals[1], totals[2], totals[3], totals[4], totals[5], totals[6], totals[7], totals[8], totals[9], totals[10], totals[11], totals[12], totals[13], totals[14])
```

```python
import functools

import jax
import jax.numpy as jnp
from jax import lax
from jax.experimental import pallas as pl
from jax.experimental.pallas import tpu as pltpu
from jax.sharding import PartitionSpec as P

HD = 64
BLOCK = 64
LENGTH = 4096
NB = LENGTH // BLOCK
GROUP = 4
QROWS = LENGTH // GROUP
QB = QROWS // BLOCK
HEADS = 3
KEYS = 8 * BLOCK
KV = 128 * HEADS
QKV = KV + 256

negative = -1e30
epsilon = 1e-05
both = ("dp", "tensor")
flipped = ("tensor", "dp")
vmem_limit = 56 * 1024 * 1024


def dot_nn(left, right):
    return jnp.dot(left, right, preferred_element_type=jnp.float32)


def dot_tn(left, right):
    return lax.dot_general(
        left, right, (((0,), (0,)), ((), ())), preferred_element_type=jnp.float32
    )


def dot_nt(left, right):
    return lax.dot_general(
        left, right, (((1,), (1,)), ((), ())), preferred_element_type=jnp.float32
    )


def lane_masks(dtype):
    lane = lax.broadcasted_iota(jnp.int32, (1, 128), 1)
    low = (lane < 64).astype(jnp.float32).astype(dtype)
    high = (lane >= 64).astype(jnp.float32).astype(dtype)
    return low, high


def key_bias(block):
    lane = lax.broadcasted_iota(jnp.int32, (1, KEYS), 1)
    entry = lane // BLOCK
    key = jnp.where(entry == 2, block - 1, jnp.where(entry == 3, block, block + 1))
    window = (entry >= 2) & (entry <= 4)
    off = window & ((key < 1) | (key > NB - 2))
    return jnp.where(off, negative, 0.0).astype(jnp.float32)


def gather_keys(table, source, head, block):
    rows = []
    for entry in range(8):
        place = table[(head * NB + block) * 8 + entry]
        rows.append(source[pl.ds(pl.multiple_of(place * BLOCK, BLOCK), BLOCK), head * 128 : head * 128 + 128])
    return jnp.concatenate(rows, axis=0)


def head_queries(first, second, low, high):
    return (first * high, first * low, second)


def forward_kernel(steps, table, place, q_first, q_second, kv0, kv1, kv2, kv3, _, o_ref, p_ref, kv_scr, sems):
    step = pl.program_id(0)

    @pl.when(step == 0)
    def _load():
        copies = [
            pltpu.make_async_copy(
                src.at[:, pl.ds(0, KV)], kv_scr.at[pl.ds(n * QROWS, QROWS)], sems.at[n]
            )
            for n, src in enumerate((kv0, kv1, kv2, kv3))
        ]
        for copy in copies:
            copy.start()
        for copy in copies:
            copy.wait()

    low, high = lane_masks(jnp.bfloat16)
    lane = lax.broadcasted_iota(jnp.int32, (1, 128), 1)
    per = QB // steps
    for sub in range(per):
        local = place[0] * QB + step * per + sub
        bias = key_bias(local ^ (place[1] * QB))
        rows = slice(sub * BLOCK, (sub + 1) * BLOCK)
        queries = head_queries(q_first[rows], q_second[rows], low, high)
        outs = []
        for head in range(HEADS):
            keys = gather_keys(table, kv_scr, head, local)
            scores = dot_nt(queries[head], keys) + bias
            expo = jnp.exp(scores - jnp.max(scores, axis=1, keepdims=True))
            inverse = 1.0 / jnp.sum(expo, axis=1, keepdims=True)
            probs = (expo * inverse).astype(jnp.bfloat16)
            p_ref[sub, head] = probs
            outs.append(dot_nn(probs, keys))
        o_ref[rows, 0:128] = jnp.where(lane < 64, outs[0], outs[1]).astype(jnp.bfloat16)
        o_ref[rows, 128:192] = outs[2][:, 0:64].astype(jnp.bfloat16)


def attend_forward(slot, table, place, qkv, probs):
    steps = 4
    per = QB // steps
    any_spec = pl.BlockSpec(memory_space=pl.ANY)
    p_shape = jax.ShapeDtypeStruct((NB, HEADS, BLOCK, KEYS), jnp.bfloat16)
    operands = [table, place, qkv[slot], qkv[slot], *qkv]
    alias = {}
    kernel = functools.partial(forward_kernel, steps)
    if probs is None:
        probs = jnp.zeros((8, 128), jnp.bfloat16)
    else:
        alias = {8: 1}
    operands.append(probs)
    return pl.pallas_call(
        kernel,
        grid_spec=pltpu.PrefetchScalarGridSpec(
            num_scalar_prefetch=2,
            grid=(steps,),
            in_specs=[
                pl.BlockSpec((per * BLOCK, 128), lambda g, *_: (g, 3)),
                pl.BlockSpec((per * BLOCK, 128), lambda g, *_: (g, 4)),
                any_spec,
                any_spec,
                any_spec,
                any_spec,
                any_spec,
            ],
            out_specs=[
                pl.BlockSpec((per * BLOCK, 192), lambda g, *_: (g, 0)),
                pl.BlockSpec(
                    (per, HEADS, BLOCK, KEYS), lambda g, t, pos: (pos[0] * steps + g, 0, 0, 0)
                ),
            ],
            scratch_shapes=[
                pltpu.VMEM((LENGTH, KV), jnp.bfloat16),
                pltpu.SemaphoreType.DMA((4,)),
            ],
        ),
        out_shape=[jax.ShapeDtypeStruct((QROWS, 192), jnp.bfloat16), p_shape],
        input_output_aliases=alias,
        compiler_params=pltpu.CompilerParams(
            dimension_semantics=("arbitrary",), vmem_limit_bytes=vmem_limit
        ),
        name="attend_forward",
    )(*operands)


def backward_kernel(
    steps, table, p_ref, qkv0, qkv1, qkv2, qkv3, do0, do1, do2, do3, out_ref, qkv_scr, do_scr, acc, sems
):
    step = pl.program_id(0)

    @pl.when(step == 0)
    def _load():
        copies = [
            pltpu.make_async_copy(src, qkv_scr.at[pl.ds(n * QROWS, QROWS)], sems.at[n])
            for n, src in enumerate((qkv0, qkv1, qkv2, qkv3))
        ] + [
            pltpu.make_async_copy(src, do_scr.at[pl.ds(n * QROWS, QROWS)], sems.at[4 + n])
            for n, src in enumerate((do0, do1, do2, do3))
        ]
        for copy in copies:
            copy.start()
        acc[...] = jnp.zeros_like(acc)
        for copy in copies:
            copy.wait()

    low, high = lane_masks(jnp.bfloat16)
    lane = lax.broadcasted_iota(jnp.int32, (1, 128), 1)
    per = NB // steps
    for sub in range(per):
        local = step * per + sub
        rows = pl.ds(pl.multiple_of(local * BLOCK, BLOCK), BLOCK)
        queries = head_queries(
            qkv_scr[rows, KV : KV + 128], qkv_scr[rows, KV + 128 : KV + 256], low, high
        )
        g_first = do_scr[rows, 0:128]
        g_second = do_scr[rows, 128:192]
        grads = (
            g_first * low,
            g_first * high,
            jnp.concatenate([g_second, jnp.zeros_like(g_second)], axis=1),
        )
        backs = []
        for head in range(HEADS):
            keys = gather_keys(table, qkv_scr, head, local)
            probs = p_ref[sub, head]
            wide = probs.astype(jnp.float32)
            weighted = wide * dot_nt(grads[head], keys)
            total = jnp.sum(weighted, axis=1, keepdims=True)
            slopes = (weighted - wide * total).astype(jnp.bfloat16)
            backs.append(dot_nn(slopes, keys) * 0.125)
            stack = jnp.concatenate([slopes, probs], axis=0)
            right = jnp.concatenate([queries[head], grads[head]], axis=0)
            spread = dot_tn(stack, right)
            for entry in range(8):
                spot = table[(head * NB + local) * 8 + entry]
                where = pl.ds(pl.multiple_of(spot * BLOCK, BLOCK), BLOCK)
                acc[where, head * 128 : head * 128 + 128] += spread[
                    entry * BLOCK : (entry + 1) * BLOCK
                ]
        out_ref[rows, KV : KV + 128] = jnp.where(lane < 64, backs[1], backs[0]).astype(jnp.bfloat16)
        out_ref[rows, KV + 128 : KV + 256] = jnp.where(lane < 64, 0.0, backs[2]).astype(
            jnp.bfloat16
        )

    @pl.when(step == steps - 1)
    def _store():
        out_ref[:, 0:KV] = acc[...].astype(jnp.bfloat16)


def attend_backward(table, probs, qkv, grads):
    steps = 16
    per = NB // steps
    any_spec = pl.BlockSpec(memory_space=pl.ANY)
    return pl.pallas_call(
        functools.partial(backward_kernel, steps),
        grid_spec=pltpu.PrefetchScalarGridSpec(
            num_scalar_prefetch=1,
            grid=(steps,),
            in_specs=[pl.BlockSpec((per, HEADS, BLOCK, KEYS), lambda g, *_: (g, 0, 0, 0))]
            + [any_spec] * 8,
            out_specs=pl.BlockSpec((LENGTH, QKV), lambda g, *_: (0, 0)),
            scratch_shapes=[
                pltpu.VMEM((LENGTH, QKV), jnp.bfloat16),
                pltpu.VMEM((LENGTH, 192), jnp.bfloat16),
                pltpu.VMEM((LENGTH, KV), jnp.float32),
                pltpu.SemaphoreType.DMA((8,)),
            ],
        ),
        out_shape=jax.ShapeDtypeStruct((LENGTH, QKV), jnp.bfloat16),
        compiler_params=pltpu.CompilerParams(
            dimension_semantics=("arbitrary",), vmem_limit_bytes=vmem_limit
        ),
        name="attend_backward",
    )(table, probs, *qkv, *grads)


def pack_columns(query, key, value, axis):
    def piece(matrix, head):
        return lax.slice_in_dim(matrix, head * HD, (head + 1) * HD, axis=axis)

    return jnp.concatenate(
        [
            piece(value, 0),
            piece(key, 0),
            piece(key, 1),
            piece(value, 1),
            piece(value, 2),
            piece(key, 2),
            piece(query, 1),
            piece(query, 0),
            piece(query, 2),
        ],
        axis=axis,
    )


def insert_zero(packed, axis):
    head = lax.slice_in_dim(packed, 0, KV + 128, axis=axis)
    tail = lax.slice_in_dim(packed, KV + 128, KV + 192, axis=axis)
    return jnp.concatenate([head, jnp.zeros_like(tail), tail], axis=axis)


def drop_zero(packed, axis):
    head = lax.slice_in_dim(packed, 0, KV + 128, axis=axis)
    tail = lax.slice_in_dim(packed, KV + 192, KV + 256, axis=axis)
    return jnp.concatenate([head, tail], axis=axis)


def unpack_columns(packed, axis):
    def piece(n):
        return lax.slice_in_dim(packed, n * HD, (n + 1) * HD, axis=axis)

    query = jnp.concatenate([piece(7), piece(6), piece(8)], axis=axis)
    key = jnp.concatenate([piece(1), piece(2), piece(5)], axis=axis)
    value = jnp.concatenate([piece(0), piece(3), piece(4)], axis=axis)
    return query, key, value


def layer_stats(hidden):
    center = hidden - jnp.mean(hidden, axis=-1, keepdims=True)
    scale_inv = lax.rsqrt(jnp.mean(center * center, axis=-1, keepdims=True) + epsilon)
    return (center * scale_inv, scale_inv)


def layer_back(grad_out, normal, scale_inv, gain):
    grad_norm = grad_out * gain
    return scale_inv * (
        grad_norm
        - jnp.mean(grad_norm, axis=-1, keepdims=True)
        - normal * jnp.mean(grad_norm * normal, axis=-1, keepdims=True)
    )


def per_device(
    dp_size,
    tensor_size,
    inputs,
    cotangent,
    w_query,
    w_key,
    w_value,
    w_output,
    w_up,
    w_down,
    b_query,
    b_value,
    b_output,
    gain_attn,
    bias_attn,
    b_up,
    b_down,
    gain_mlp,
    bias_mlp,
    random_blocks,
):
    width = inputs.shape[1]
    dp_index = lax.axis_index("dp")
    tensor_index = lax.axis_index("tensor")
    core = dp_index % 2
    rank = 2 * core + tensor_index % 2
    devices = [(d, t) for d in range(dp_size) for t in range(tensor_size)]

    def flat(d, t):
        return d * tensor_size + t

    def stays(d, t):
        return d % 2 == t // 2

    move_pairs = [
        (flat(d, t), flat(d, t) if stays(d, t) else flat(d ^ 1, t ^ 2)) for d, t in devices
    ]
    stay_pairs = [(flat(d, t), flat(d, t ^ 1)) for d, t in devices if stays(d, t)]
    moved_pairs = [(flat(d, t), flat(d, t ^ 1)) for d, t in devices if not stays(d, t)]
    peer_pairs = {
        1: [(flat(d, t), flat(d, t ^ 1)) for d, t in devices],
        2: [(flat(d, t), flat(d ^ 1, t)) for d, t in devices],
        3: [(flat(d, t), flat(d ^ 1, t ^ 1)) for d, t in devices],
    }
    here = core == tensor_index // 2

    packed = pack_columns(w_query, w_key, w_value, 1)
    qkv_all = lax.all_gather(packed, flipped, axis=0, tiled=True).reshape(GROUP, width, 3 * 192)
    rest = jnp.concatenate([w_up, w_down.T, w_output.T], axis=1)
    rest_all = lax.all_gather(rest, flipped, axis=0, tiled=True).reshape(GROUP, width, -1)
    small = jnp.concatenate(
        [b_query, b_value, b_up, random_blocks.astype(jnp.float32).reshape(-1)]
    )
    small_all = lax.all_gather(small, "tensor", axis=0)
    b_up_all = small_all[:, 384 : 384 + b_up.shape[0]].reshape(-1)
    mine = lax.dynamic_index_in_dim(small_all, rank, 0, keepdims=False)
    my_random = mine[384 + b_up.shape[0] :].reshape(HEADS, NB, -1).astype(jnp.int32)

    own = lax.ppermute(inputs, both, move_pairs)
    near_stay = lax.ppermute(inputs, both, stay_pairs)
    near_move = lax.ppermute(own, both, moved_pairs)
    near = jnp.where(here, near_stay, near_move)
    side = lax.ppermute(own, both, peer_pairs[2])
    far = lax.ppermute(near, both, peer_pairs[2])
    rows = (own, near, side, far)
    grad_top = lax.ppermute(cotangent, both, move_pairs)

    w_qkv = insert_zero(lax.dynamic_index_in_dim(qkv_all, rank, 0, keepdims=False), 1)
    b_key = jnp.zeros_like(b_query)
    b_qkv = insert_zero(pack_columns(mine[:192], b_key, mine[192:384], 0), 0)
    scale = jnp.concatenate([jnp.ones((KV,), jnp.float32), jnp.full((256,), 0.125, jnp.float32)])
    qkv = [((dot_nn(part, w_qkv) + b_qkv) * scale).astype(jnp.bfloat16) for part in rows]

    block = jnp.arange(NB, dtype=jnp.int32)
    block = block ^ (rank * QB)
    fixed = jnp.clip(
        jnp.stack(
            [
                jnp.zeros_like(block),
                jnp.full_like(block, NB - 1),
                block - 1,
                block,
                block + 1,
            ],
            axis=-1,
        ),
        0,
        NB - 1,
    )
    local_random = jnp.take(my_random, block, axis=1)
    table = jnp.concatenate(
        [jnp.broadcast_to(fixed[None], (HEADS, NB, 5)), local_random], axis=-1
    )
    table = (table ^ (rank * QB)).reshape(-1)

    probs = None
    outs = [None] * 4
    for slot in (1, 3, 2, 0):
        place = jnp.stack([jnp.int32(slot), rank.astype(jnp.int32)])
        outs[slot], probs = attend_forward(slot, table, place, qkv, probs)
    mixed = jnp.concatenate(
        [outs[0]] + [lax.ppermute(outs[n], both, peer_pairs[n]) for n in (1, 2, 3)], axis=1
    )

    hidden_width = b_up.shape[0]
    up_all = rest_all[:, :, :hidden_width].transpose(1, 0, 2).reshape(width, -1)
    down_all = rest_all[:, :, hidden_width : 2 * hidden_width].transpose(1, 0, 2).reshape(width, -1)
    out_parts = rest_all[:, :, 2 * hidden_width :]
    out_all = jnp.concatenate(
        [
            lax.dynamic_index_in_dim(out_parts, rank ^ n, 0, keepdims=False)
            for n in range(GROUP)
        ],
        axis=1,
    )
    residual = own.astype(jnp.float32) + dot_nt(mixed, out_all) + b_output
    normal_first, scale_first = layer_stats(residual)
    normed = normal_first * gain_attn + bias_attn
    normed_low = normed.astype(jnp.bfloat16)
    hidden_pre = dot_nn(normed_low, up_all) + b_up_all
    cdf = 0.5 * (1.0 + lax.erf(hidden_pre * 0.7071067811865476))
    hidden_low = (hidden_pre * cdf).astype(jnp.bfloat16)
    slope = cdf + hidden_pre * jnp.exp(-0.5 * hidden_pre * hidden_pre) * 0.3989422804014327
    second = normed + dot_nt(hidden_low, down_all) + b_down
    normal_second, scale_second = layer_stats(second)
    layer_out = (normal_second * gain_mlp + bias_mlp).astype(jnp.bfloat16)
    grad_out = grad_top.astype(jnp.float32)
    grad_second = layer_back(grad_out, normal_second, scale_second, gain_mlp)
    grad_second_low = grad_second.astype(jnp.bfloat16)
    grad_hidden = (dot_nn(grad_second_low, down_all) * slope).astype(jnp.bfloat16)
    grad_normed = grad_second + dot_nt(grad_hidden, up_all)
    grad_residual = layer_back(grad_normed, normal_first, scale_first, gain_attn)
    grad_residual_low = grad_residual.astype(jnp.bfloat16)
    grad_mixed = dot_nn(grad_residual_low, out_all).astype(jnp.bfloat16)

    layer_out = lax.ppermute(layer_out, both, move_pairs)
    grad_parts = [grad_mixed[:, n * 192 : (n + 1) * 192] for n in range(GROUP)]
    grads = [grad_parts[0]] + [
        lax.ppermute(grad_parts[n], both, peer_pairs[n]) for n in (1, 2, 3)
    ]

    grad_down = dot_tn(grad_second_low, hidden_low).astype(jnp.bfloat16)
    grad_up = dot_tn(normed_low, grad_hidden).astype(jnp.bfloat16)
    grad_output = dot_tn(grad_residual_low, mixed).astype(jnp.bfloat16)
    grad_output = grad_output.reshape(width, GROUP, -1)
    rest_grad = jnp.concatenate(
        [
            grad_up.reshape(width, GROUP, -1).transpose(1, 0, 2),
            grad_down.reshape(width, GROUP, -1).transpose(1, 0, 2),
            jnp.stack(
                [
                    lax.dynamic_index_in_dim(grad_output, rank ^ n, 1, keepdims=False)
                    for n in range(GROUP)
                ]
            ),
        ],
        axis=2,
    )
    rest_sum = lax.psum_scatter(
        rest_grad.reshape(GROUP * width, -1), flipped, scatter_dimension=0, tiled=True
    ).astype(jnp.float32)
    shard_up = rest_sum[:, :hidden_width]
    shard_down = rest_sum[:, hidden_width : 2 * hidden_width].T
    shard_output = rest_sum[:, 2 * hidden_width :].T
    vectors = jnp.concatenate(
        [
            jnp.sum(grad_residual, axis=0),
            jnp.sum(grad_normed * normal_first, axis=0),
            jnp.sum(grad_normed, axis=0),
            jnp.sum(grad_second, axis=0),
            jnp.sum(grad_out * normal_second, axis=0),
            jnp.sum(grad_out, axis=0),
            jnp.sum(grad_hidden.astype(jnp.float32), axis=0),
        ]
    )
    vectors = lax.psum(vectors, both)

    grad_qkv = attend_backward(table, probs, qkv, grads)
    partial = [
        dot_nt(grad_qkv[n * QROWS : (n + 1) * QROWS], w_qkv8(w_qkv)) for n in range(GROUP)
    ]
    from_side = [
        lax.ppermute(partial[n].astype(jnp.bfloat16), both, peer_pairs[2]) for n in (2, 3)
    ]
    to_near = (partial[1] + from_side[1].astype(jnp.float32)).astype(jnp.bfloat16)
    from_near = lax.ppermute(to_near, both, peer_pairs[1])
    grad_own = (
        grad_residual
        + partial[0]
        + from_side[0].astype(jnp.float32)
        + from_near.astype(jnp.float32)
    ).astype(jnp.bfloat16)
    grad_input = lax.ppermute(grad_own, both, move_pairs)

    all_rows = jnp.concatenate(rows, axis=0)
    grad_w = drop_zero(dot_tn(all_rows, grad_qkv), 1).astype(jnp.bfloat16)
    groups = jnp.arange(GROUP, dtype=jnp.int32)[:, None, None]
    spread_w = jnp.where(groups == rank, grad_w[None], jnp.zeros((), jnp.bfloat16))
    shard_qkv = lax.psum_scatter(
        spread_w.reshape(GROUP * width, -1), flipped, scatter_dimension=0, tiled=True
    ).astype(jnp.float32)
    shard_query, shard_key, shard_value = unpack_columns(shard_qkv, 1)
    shard_query = shard_query
    bias_sum = drop_zero(jnp.sum(grad_qkv.astype(jnp.float32), axis=0), 0)
    bias_query, _, bias_value = unpack_columns(bias_sum, 0)
    bias_pair = jnp.concatenate([bias_query, bias_value])
    bias_pair = lax.psum(
        jnp.where(groups[:, :, 0] == rank, bias_pair[None], 0.0), both
    )
    bias_pair = lax.dynamic_index_in_dim(bias_pair, tensor_index, 0, keepdims=False)
    grad_b_up = lax.dynamic_slice_in_dim(
        vectors[6 * width :], tensor_index * hidden_width, hidden_width, 0
    )
    return (
        layer_out,
        grad_input,
        shard_query,
        shard_key,
        shard_value,
        shard_output,
        shard_up,
        shard_down,
        bias_pair[:192],
        bias_pair[192:],
        vectors[0:width],
        vectors[width : 2 * width],
        vectors[2 * width : 3 * width],
        grad_b_up,
        vectors[3 * width : 4 * width],
        vectors[4 * width : 5 * width],
        vectors[5 * width : 6 * width],
    )


def w_qkv8(w_qkv):
    return w_qkv


def solution(mesh):
    in_specs = (
        P(("dp", "tensor"), None),
        P(("dp", "tensor"), None),
        P("dp", "tensor"),
        P("dp", "tensor"),
        P("dp", "tensor"),
        P("tensor", "dp"),
        P("dp", "tensor"),
        P("tensor", "dp"),
        P("tensor"),
        P("tensor"),
        P(),
        P(),
        P(),
        P("tensor"),
        P(),
        P(),
        P(),
        P("tensor", None, None),
    )
    out_specs = (
        P(("dp", "tensor"), None),
        P(("dp", "tensor"), None),
        P("dp", "tensor"),
        P("dp", "tensor"),
        P("dp", "tensor"),
        P("tensor", "dp"),
        P("dp", "tensor"),
        P("tensor", "dp"),
        P("tensor"),
        P("tensor"),
        P(),
        P(),
        P(),
        P("tensor"),
        P(),
        P(),
        P(),
    )
    body = functools.partial(per_device, mesh.shape["dp"], mesh.shape["tensor"])
    return jax.shard_map(body, mesh=mesh, in_specs=in_specs, out_specs=out_specs, check_vma=False)
```

```python
import functools

import jax
import jax.numpy as jnp
from jax import lax
from jax.experimental import pallas as pl
from jax.experimental.pallas import tpu as pltpu
from jax.sharding import PartitionSpec as P

HD = 64
BLOCK = 64
LENGTH = 4096
NB = LENGTH // BLOCK
GROUP = 4
QROWS = LENGTH // GROUP
QB = QROWS // BLOCK
HEADS = 3
KEYS = 8 * BLOCK
KV = 128 * HEADS
QKV = KV + 256

negative = -1e30
epsilon = 1e-05
both = ("dp", "tensor")
vmem_limit = 56 * 1024 * 1024


def dot_nn(left, right):
    return jnp.dot(left, right, preferred_element_type=jnp.float32)


def dot_tn(left, right):
    return lax.dot_general(
        left, right, (((0,), (0,)), ((), ())), preferred_element_type=jnp.float32
    )


def dot_nt(left, right):
    return lax.dot_general(
        left, right, (((1,), (1,)), ((), ())), preferred_element_type=jnp.float32
    )


def lane_masks(dtype):
    lane = lax.broadcasted_iota(jnp.int32, (1, 128), 1)
    low = (lane < 64).astype(jnp.float32).astype(dtype)
    high = (lane >= 64).astype(jnp.float32).astype(dtype)
    return low, high


def key_bias(block):
    lane = lax.broadcasted_iota(jnp.int32, (1, KEYS), 1)
    entry = lane // BLOCK
    key = jnp.where(entry == 2, block - 1, jnp.where(entry == 3, block, block + 1))
    window = (entry >= 2) & (entry <= 4)
    off = window & ((key < 1) | (key > NB - 2))
    return jnp.where(off, negative, 0.0).astype(jnp.float32)


def gather_keys(table, source, head, block):
    rows = []
    for entry in range(8):
        place = table[(head * NB + block) * 8 + entry]
        rows.append(source[pl.ds(pl.multiple_of(place * BLOCK, BLOCK), BLOCK), head * 128 : head * 128 + 128])
    return jnp.concatenate(rows, axis=0)


def head_queries(first, second, low, high):
    return (first * high, first * low, second)


def forward_kernel(steps, fill, table, place, *refs):
    if fill:
        qkv0, qkv1, qkv2, qkv3, o_ref, p_ref, qkv_scr, s_scr, sems = refs
    else:
        qkv0, qkv1, qkv2, qkv3, _, o_ref, p_ref, qkv_scr, s_scr, sems = refs
    step = pl.program_id(0)

    @pl.when(step == 0)
    def _load():
        copies = [
            pltpu.make_async_copy(src, qkv_scr.at[pl.ds(n * QROWS, QROWS)], sems.at[n])
            for n, src in enumerate((qkv0, qkv1, qkv2, qkv3))
        ]
        for copy in copies:
            copy.start()
        for copy in copies:
            copy.wait()

    low, high = lane_masks(jnp.bfloat16)
    lane = lax.broadcasted_iota(jnp.int32, (1, 128), 1)
    per = QB // steps
    units = [(sub, head) for sub in range(per) for head in range(HEADS)]
    slot = place[1 + step // steps]
    keys = []
    for sub in range(per):
        local = slot * QB + (step % steps) * per + sub
        bias = key_bias(local ^ (place[0] * QB))
        rows = pl.ds(pl.multiple_of(local * BLOCK, BLOCK), BLOCK)
        queries = head_queries(
            qkv_scr[rows, KV : KV + 128], qkv_scr[rows, KV + 128 : KV + 256], low, high
        )
        for head in range(HEADS):
            n = sub * HEADS + head
            keys.append(gather_keys(table, qkv_scr, head, local))
            raw = dot_nt(queries[head], keys[n])
            s_scr[n, :, 0:128] = raw[:, 0:128]
            s_scr[n, :, 128:384] = raw[:, 128:384] + bias[:, 128:384]
            s_scr[n, :, 384:512] = raw[:, 384:512]
    tops = [jnp.max(s_scr[n], axis=1, keepdims=True) for n in range(len(units))]
    sums = []
    for n in range(len(units)):
        expo = jnp.exp(s_scr[n] - tops[n])
        s_scr[n] = expo
        sums.append(jnp.sum(expo, axis=1, keepdims=True))
    for n, (sub, head) in enumerate(units):
        p_ref[sub, head] = (s_scr[n] * (1.0 / sums[n])).astype(jnp.bfloat16)
    for sub in range(per):
        rows = slice(sub * BLOCK, (sub + 1) * BLOCK)
        outs = [dot_nn(p_ref[sub, head], keys[sub * HEADS + head]) for head in range(HEADS)]
        o_ref[0, rows, 0:128] = jnp.where(lane < 64, outs[0], outs[1]).astype(jnp.bfloat16)
        o_ref[0, rows, 128:192] = outs[2][:, 0:64].astype(jnp.bfloat16)


def attend_forward(slots, rank, table, qkv, probs):
    steps = 4
    per = QB // steps
    count = len(slots)
    any_spec = pl.BlockSpec(memory_space=pl.ANY)
    place = jnp.stack([rank.astype(jnp.int32)] + [jnp.int32(slot) for slot in slots])
    operands = [table, place, *qkv]
    alias = {}
    if probs is not None:
        alias = {6: 1}
        operands.append(probs)
    return pl.pallas_call(
        functools.partial(forward_kernel, steps, probs is None),
        grid_spec=pltpu.PrefetchScalarGridSpec(
            num_scalar_prefetch=2,
            grid=(count * steps,),
            in_specs=[any_spec] * (4 + len(alias)),
            out_specs=[
                pl.BlockSpec((1, per * BLOCK, 192), lambda g, *_: (g // steps, g % steps, 0)),
                pl.BlockSpec(
                    (per, HEADS, BLOCK, KEYS),
                    lambda g, t, pos: (pos[1 + g // steps] * steps + g % steps, 0, 0, 0),
                ),
            ],
            scratch_shapes=[
                pltpu.VMEM((LENGTH, QKV), jnp.bfloat16),
                pltpu.VMEM((per * HEADS, BLOCK, KEYS), jnp.float32),
                pltpu.SemaphoreType.DMA((4,)),
            ],
        ),
        out_shape=[
            jax.ShapeDtypeStruct((count, QROWS, 192), jnp.bfloat16),
            jax.ShapeDtypeStruct((NB, HEADS, BLOCK, KEYS), jnp.bfloat16),
        ],
        input_output_aliases=alias,
        compiler_params=pltpu.CompilerParams(
            dimension_semantics=("arbitrary",), vmem_limit_bytes=vmem_limit
        ),
        name="attend_forward",
    )(*operands)


def backward_kernel(
    steps, table, p_ref, qkv0, qkv1, qkv2, qkv3, do0, do1, do2, do3, out_ref, qkv_scr, do_scr, acc, dp_scr, st_scr, sems
):
    step = pl.program_id(0)

    @pl.when(step == 0)
    def _load():
        copies = [
            pltpu.make_async_copy(src, qkv_scr.at[pl.ds(n * QROWS, QROWS)], sems.at[n])
            for n, src in enumerate((qkv0, qkv1, qkv2, qkv3))
        ] + [
            pltpu.make_async_copy(src, do_scr.at[pl.ds(n * QROWS, QROWS)], sems.at[4 + n])
            for n, src in enumerate((do0, do1, do2, do3))
        ]
        for copy in copies:
            copy.start()
        acc[...] = jnp.zeros_like(acc)
        for copy in copies:
            copy.wait()

    low, high = lane_masks(jnp.bfloat16)
    lane = lax.broadcasted_iota(jnp.int32, (1, 128), 1)
    per = NB // steps
    units = [(sub, head) for sub in range(per) for head in range(HEADS)]
    keys, right = [], []
    for sub in range(per):
        local = step * per + sub
        rows = pl.ds(pl.multiple_of(local * BLOCK, BLOCK), BLOCK)
        queries = head_queries(
            qkv_scr[rows, KV : KV + 128], qkv_scr[rows, KV + 128 : KV + 256], low, high
        )
        g_first = do_scr[rows, 0:128]
        g_second = do_scr[rows, 128:192]
        grads = (
            g_first * low,
            g_first * high,
            jnp.concatenate([g_second, jnp.zeros_like(g_second)], axis=1),
        )
        for head in range(HEADS):
            n = sub * HEADS + head
            keys.append(gather_keys(table, qkv_scr, head, local))
            right.append(jnp.concatenate([queries[head], grads[head]], axis=0))
            dp_scr[n] = dot_nt(grads[head], keys[n])
    totals = []
    for n, (sub, head) in enumerate(units):
        weighted = p_ref[sub, head].astype(jnp.float32) * dp_scr[n]
        dp_scr[n] = weighted
        totals.append(jnp.sum(weighted, axis=1, keepdims=True))
    for n, (sub, head) in enumerate(units):
        probs = p_ref[sub, head]
        st_scr[n, 0:BLOCK] = (dp_scr[n] - probs.astype(jnp.float32) * totals[n]).astype(jnp.bfloat16)
        st_scr[n, BLOCK:128] = probs
    for sub in range(per):
        local = step * per + sub
        rows = pl.ds(pl.multiple_of(local * BLOCK, BLOCK), BLOCK)
        backs = [
            dot_nn(st_scr[sub * HEADS + head, 0:BLOCK], keys[sub * HEADS + head]) * 0.125
            for head in range(HEADS)
        ]
        out_ref[rows, KV : KV + 128] = jnp.where(lane < 64, backs[1], backs[0]).astype(jnp.bfloat16)
        out_ref[rows, KV + 128 : KV + 256] = jnp.where(lane < 64, 0.0, backs[2]).astype(
            jnp.bfloat16
        )
    for n, (sub, head) in enumerate(units):
        local = step * per + sub
        spread = dot_tn(st_scr[n], right[n])
        for entry in range(8):
            spot = table[(head * NB + local) * 8 + entry]
            where = pl.ds(pl.multiple_of(spot * BLOCK, BLOCK), BLOCK)
            acc[where, head * 128 : head * 128 + 128] += spread[
                entry * BLOCK : (entry + 1) * BLOCK
            ]

    @pl.when(step == steps - 1)
    def _store():
        out_ref[:, 0:KV] = acc[...].astype(jnp.bfloat16)


def attend_backward(table, probs, qkv, grads):
    steps = 16
    per = NB // steps
    any_spec = pl.BlockSpec(memory_space=pl.ANY)
    return pl.pallas_call(
        functools.partial(backward_kernel, steps),
        grid_spec=pltpu.PrefetchScalarGridSpec(
            num_scalar_prefetch=1,
            grid=(steps,),
            in_specs=[pl.BlockSpec((per, HEADS, BLOCK, KEYS), lambda g, *_: (g, 0, 0, 0))]
            + [any_spec] * 8,
            out_specs=pl.BlockSpec((LENGTH, QKV), lambda g, *_: (0, 0)),
            scratch_shapes=[
                pltpu.VMEM((LENGTH, QKV), jnp.bfloat16),
                pltpu.VMEM((LENGTH, 192), jnp.bfloat16),
                pltpu.VMEM((LENGTH, KV), jnp.float32),
                pltpu.VMEM((per * HEADS, BLOCK, KEYS), jnp.float32),
                pltpu.VMEM((per * HEADS, 128, KEYS), jnp.bfloat16),
                pltpu.SemaphoreType.DMA((8,)),
            ],
        ),
        out_shape=jax.ShapeDtypeStruct((LENGTH, QKV), jnp.bfloat16),
        compiler_params=pltpu.CompilerParams(
            dimension_semantics=("arbitrary",), vmem_limit_bytes=vmem_limit
        ),
        name="attend_backward",
    )(table, probs, *qkv, *grads)


def row_mean(values):
    return jnp.mean(values, axis=1, keepdims=True)


def fold_rows(values):
    total = values[0:8]
    for row in range(8, values.shape[0], 8):
        total = total + values[row : row + 8]
    return total


def token_kernel(
    tile,
    width,
    hidden,
    rank_ref,
    o0,
    o1,
    o2,
    o3,
    x_ref,
    cot_ref,
    vec_ref,
    up_bias_ref,
    weights,
    out_ref,
    n1_ref,
    g_ref,
    du_ref,
    dfr_ref,
    dar_ref,
    da_ref,
    do_ref,
    sum_ref,
    up_sum_ref,
    w_scr,
    acc,
    u_scr,
    slope_scr,
    xhat_scr,
    m1_scr,
    sem,
):
    step = pl.program_id(0)
    parts = GROUP
    small = 32
    cols = 256

    @pl.when(step == 0)
    def _load():
        copy = pltpu.make_async_copy(weights, w_scr, sem)
        copy.start()
        sum_ref[...] = jnp.zeros_like(sum_ref)
        up_sum_ref[...] = jnp.zeros_like(up_sum_ref)
        copy.wait()

    def vector(n):
        return vec_ref[n : n + 1, :]

    def part_rows(n):
        return slice(n * width, (n + 1) * width)

    def out_weight(n):
        place = pl.multiple_of((rank_ref[0] ^ n) * width, width)
        return w_scr[pl.ds(place, width), 2 * hidden :]

    total = dot_nt(o0[...], out_weight(0))
    for n, piece in ((1, o1), (2, o2), (3, o3)):
        total = total + dot_nt(piece[...], out_weight(n))
    acc[...] = total
    first_scale = []
    for row in range(0, tile, small):
        rows = slice(row, row + small)
        resid = acc[rows] + x_ref[rows].astype(jnp.float32) + vector(0)
        center = resid - row_mean(resid)
        scale = lax.rsqrt(row_mean(center * center) + epsilon)
        xhat = center * scale
        normed = xhat * vector(1) + vector(2)
        first_scale.append(scale)
        xhat_scr[rows] = xhat
        m1_scr[rows] = normed
        n1_ref[rows] = normed.astype(jnp.bfloat16)
    for part in range(parts):
        u_scr[part % 2] = dot_nn(n1_ref[...], w_scr[part_rows(part), 0:hidden])
        for row in range(0, tile, small):
            rows = slice(row, row + small)
            for col in range(0, hidden, cols):
                place = slice(col, col + cols)
                wide = slice(part * hidden + col, part * hidden + col + cols)
                pre = u_scr[part % 2, rows, place] + up_bias_ref[:, wide]
                cdf = 0.5 + 0.5 * lax.erf(pre * 0.7071067811865476)
                g_ref[rows, wide] = (pre * cdf).astype(jnp.bfloat16)
                slope_scr[rows, wide] = (
                    cdf + pre * jnp.exp(-0.5 * pre * pre) * 0.3989422804014327
                )
        lift = dot_nt(
            g_ref[:, part * hidden : (part + 1) * hidden],
            w_scr[part_rows(part), hidden : 2 * hidden],
        )
        if part == 0:
            acc[...] = lift
        else:
            acc[...] += lift
    sums = [jnp.zeros((8, width), jnp.float32) for _ in range(6)]
    for row in range(0, tile, small):
        rows = slice(row, row + small)
        second = m1_scr[rows] + acc[rows] + vector(3)
        center = second - row_mean(second)
        scale = lax.rsqrt(row_mean(center * center) + epsilon)
        xhat = center * scale
        out_ref[rows] = (xhat * vector(4) + vector(5)).astype(jnp.bfloat16)
        top = cot_ref[rows].astype(jnp.float32)
        gained = top * vector(4)
        down = scale * (gained - row_mean(gained) - xhat * row_mean(gained * xhat))
        sums[0] = sums[0] + fold_rows(top * xhat)
        sums[1] = sums[1] + fold_rows(top)
        sums[2] = sums[2] + fold_rows(down)
        m1_scr[rows] = down
        dfr_ref[rows] = down.astype(jnp.bfloat16)
    for part in range(parts):
        whole = slice(part * hidden, (part + 1) * hidden)
        u_scr[part % 2] = dot_nn(dfr_ref[...], w_scr[part_rows(part), hidden : 2 * hidden])
        for col in range(0, hidden, cols):
            place = slice(col, col + cols)
            wide = slice(part * hidden + col, part * hidden + col + cols)
            tally = jnp.zeros((8, cols), jnp.float32)
            for row in range(0, tile, small):
                rows = slice(row, row + small)
                low = (u_scr[part % 2, rows, place] * slope_scr[rows, wide]).astype(jnp.bfloat16)
                du_ref[rows, wide] = low
                tally = tally + fold_rows(low.astype(jnp.float32))
            up_sum_ref[:, wide] += tally
        lift = dot_nt(du_ref[:, whole], w_scr[part_rows(part), 0:hidden])
        if part == 0:
            acc[...] = lift
        else:
            acc[...] += lift
    for n, row in enumerate(range(0, tile, small)):
        rows = slice(row, row + small)
        back = m1_scr[rows] + acc[rows]
        xhat = xhat_scr[rows]
        sums[3] = sums[3] + fold_rows(back * xhat)
        sums[4] = sums[4] + fold_rows(back)
        gained = back * vector(1)
        down = first_scale[n] * (gained - row_mean(gained) - xhat * row_mean(gained * xhat))
        sums[5] = sums[5] + fold_rows(down)
        da_ref[rows] = down
        dar_ref[rows] = down.astype(jnp.bfloat16)
    for n in range(6):
        sum_ref[n] += sums[n]
    for n in range(parts):
        do_ref[n] = dot_nn(dar_ref[...], out_weight(n)).astype(jnp.bfloat16)


def token_block(rank, outs, own, cot, vectors, up_bias, weights):
    count, width = own.shape
    total_hidden = up_bias.shape[1]
    hidden = total_hidden // GROUP
    tile = 256

    def rows_of(columns):
        return pl.BlockSpec((tile, columns), lambda g, *_: (g, 0))

    def whole(shape):
        return pl.BlockSpec(shape, lambda g, *_: (0,) * len(shape))

    low = jnp.bfloat16
    head = outs[0].shape[1]
    return pl.pallas_call(
        functools.partial(token_kernel, tile, width, hidden),
        grid_spec=pltpu.PrefetchScalarGridSpec(
            num_scalar_prefetch=1,
            grid=(count // tile,),
            in_specs=[rows_of(head)] * 4
            + [rows_of(width)] * 2
            + [whole(vectors.shape), whole(up_bias.shape), pl.BlockSpec(memory_space=pl.ANY)],
            out_specs=[
                rows_of(width),
                rows_of(width),
                rows_of(total_hidden),
                rows_of(total_hidden),
                rows_of(width),
                rows_of(width),
                rows_of(width),
                pl.BlockSpec((GROUP, tile, head), lambda g, *_: (0, g, 0)),
                whole((6, 8, width)),
                whole((8, total_hidden)),
            ],
            scratch_shapes=[
                pltpu.VMEM(weights.shape, low),
                pltpu.VMEM((tile, width), jnp.float32),
                pltpu.VMEM((2, tile, hidden), jnp.float32),
                pltpu.VMEM((tile, total_hidden), jnp.float32),
                pltpu.VMEM((tile, width), jnp.float32),
                pltpu.VMEM((tile, width), jnp.float32),
                pltpu.SemaphoreType.DMA,
            ],
        ),
        out_shape=[
            jax.ShapeDtypeStruct((count, width), low),
            jax.ShapeDtypeStruct((count, width), low),
            jax.ShapeDtypeStruct((count, total_hidden), low),
            jax.ShapeDtypeStruct((count, total_hidden), low),
            jax.ShapeDtypeStruct((count, width), low),
            jax.ShapeDtypeStruct((count, width), low),
            jax.ShapeDtypeStruct((count, width), jnp.float32),
            jax.ShapeDtypeStruct((GROUP, count, head), low),
            jax.ShapeDtypeStruct((6, 8, width), jnp.float32),
            jax.ShapeDtypeStruct((8, total_hidden), jnp.float32),
        ],
        compiler_params=pltpu.CompilerParams(
            dimension_semantics=("arbitrary",), vmem_limit_bytes=vmem_limit
        ),
        name="token_block",
    )(rank.astype(jnp.int32).reshape(1), *outs, own, cot, vectors, up_bias, weights)


def weight_kernel(width, hidden, rank_ref, n1, dfr, dar, g, du, o0, o1, o2, o3, out_ref, n1_t, dfr_t, dar_t):
    part = pl.program_id(0)

    @pl.when(part == 0)
    def _turn():
        n1_t[...] = n1[...].T
        dfr_t[...] = dfr[...].T
        dar_t[...] = dar[...].T

    out_ref[:, 0:hidden] = dot_nn(n1_t[...], du[...]).astype(jnp.bfloat16)
    out_ref[:, hidden : 2 * hidden] = dot_nn(dfr_t[...], g[...]).astype(jnp.bfloat16)
    for n, piece in enumerate((o0, o1, o2, o3)):

        @pl.when(part == rank_ref[0] ^ n)
        def _out(piece=piece):
            out_ref[:, 2 * hidden :] = dot_nn(dar_t[...], piece[...]).astype(jnp.bfloat16)


def weight_block(rank, n1, dfr, dar, g, du, outs):
    count, width = n1.shape
    hidden = g.shape[1] // GROUP
    head = outs[0].shape[1]
    columns = 2 * hidden + head
    low = jnp.bfloat16

    def whole(shape):
        return pl.BlockSpec(shape, lambda g, *_: (0,) * len(shape))

    return pl.pallas_call(
        functools.partial(weight_kernel, width, hidden),
        grid_spec=pltpu.PrefetchScalarGridSpec(
            num_scalar_prefetch=1,
            grid=(GROUP,),
            in_specs=[whole((count, width))] * 3
            + [pl.BlockSpec((count, hidden), lambda g, *_: (0, g))] * 2
            + [whole((count, head))] * 4,
            out_specs=pl.BlockSpec((width, columns), lambda g, *_: (g, 0)),
            scratch_shapes=[pltpu.VMEM((width, count), low)] * 3,
        ),
        out_shape=jax.ShapeDtypeStruct((GROUP * width, columns), low),
        compiler_params=pltpu.CompilerParams(
            dimension_semantics=("arbitrary",), vmem_limit_bytes=vmem_limit
        ),
        name="weight_block",
    )(rank.astype(jnp.int32).reshape(1), n1, dfr, dar, g, du, *outs)


def pack_columns(query, key, value, axis):
    def piece(matrix, head):
        return lax.slice_in_dim(matrix, head * HD, (head + 1) * HD, axis=axis)

    return jnp.concatenate(
        [
            piece(value, 0),
            piece(key, 0),
            piece(key, 1),
            piece(value, 1),
            piece(value, 2),
            piece(key, 2),
            piece(query, 1),
            piece(query, 0),
            piece(query, 2),
        ],
        axis=axis,
    )


def insert_zero(packed, axis):
    head = lax.slice_in_dim(packed, 0, KV + 128, axis=axis)
    tail = lax.slice_in_dim(packed, KV + 128, KV + 192, axis=axis)
    return jnp.concatenate([head, jnp.zeros_like(tail), tail], axis=axis)


def drop_zero(packed, axis):
    head = lax.slice_in_dim(packed, 0, KV + 128, axis=axis)
    tail = lax.slice_in_dim(packed, KV + 192, KV + 256, axis=axis)
    return jnp.concatenate([head, tail], axis=axis)


def unpack_columns(packed, axis):
    def piece(n):
        return lax.slice_in_dim(packed, n * HD, (n + 1) * HD, axis=axis)

    query = jnp.concatenate([piece(7), piece(6), piece(8)], axis=axis)
    key = jnp.concatenate([piece(1), piece(2), piece(5)], axis=axis)
    value = jnp.concatenate([piece(0), piece(3), piece(4)], axis=axis)
    return query, key, value


def per_device(
    dp_size,
    tensor_size,
    inputs,
    cotangent,
    w_query,
    w_key,
    w_value,
    w_output,
    w_up,
    w_down,
    b_query,
    b_value,
    b_output,
    gain_attn,
    bias_attn,
    b_up,
    b_down,
    gain_mlp,
    bias_mlp,
    random_blocks,
):
    width = inputs.shape[1]
    hidden = b_up.shape[0]
    dp_index = lax.axis_index("dp")
    tensor_index = lax.axis_index("tensor")
    core = dp_index % 2
    half = tensor_index // 2
    rank = 2 * core + tensor_index % 2
    here = core == half
    devices = [(d, t) for d in range(dp_size) for t in range(tensor_size)]
    pair_bits = [bit for bit in range(1, dp_size.bit_length() - 1)]

    def flat(d, t):
        return d * tensor_size + t

    def stays(d, t):
        return d % 2 == t // 2

    def flip(value, d_bits, t_bits, chosen=None):
        pairs = [
            (flat(d, t), flat(d ^ d_bits, t ^ t_bits))
            for d, t in devices
            if chosen is None or chosen(d, t)
        ]
        return lax.ppermute(value, both, pairs)

    def moves(d, t):
        return not stays(d, t)

    def rehome(value):
        return jnp.where(here, value, flip(value, 1, 2, moves))

    def near_of(value):
        return flip(value, 0, 1)

    def side_of(value):
        return flip(value, 1, 0)

    rest = jnp.concatenate([w_up, w_down.T, w_output.T], axis=1)
    rest = lax.all_gather(rest, "tensor", axis=0)
    rest_all = lax.all_gather(rest, "dp", axis=1, tiled=True).reshape(GROUP * width, -1)

    packed = rehome(pack_columns(w_query, w_key, w_value, 1))
    packed = order_halves(half, packed, flip(packed, 0, 2))
    for bit in pair_bits:
        packed = order_halves((dp_index >> bit) % 2, packed, flip(packed, 1 << bit, 0))
    w_qkv = insert_zero(packed, 1)

    small = jnp.concatenate(
        [b_query, b_value, b_up, random_blocks.astype(jnp.float32).reshape(-1)]
    )[None]
    small = jnp.concatenate([small, flip(small, 0, 1)], axis=0)
    small = jnp.concatenate([small, flip(small, 0, 2)], axis=0)
    b_up_all = jnp.concatenate(
        [
            lax.dynamic_index_in_dim(small, tensor_index ^ n, 0)[:, 384 : 384 + hidden]
            for n in range(GROUP)
        ],
        axis=1,
    )
    mine = lax.dynamic_index_in_dim(small, tensor_index ^ rank, 0, keepdims=False)
    my_random = mine[384 + hidden :].reshape(HEADS, NB, -1).astype(jnp.int32)

    own = rehome(inputs)
    near = jnp.where(here, flip(inputs, 0, 1, stays), flip(own, 0, 1, moves))
    side = side_of(own)
    far = side_of(near)
    rows = (own, near, side, far)
    cotangent, _ = lax.optimization_barrier((cotangent, near))
    grad_top = rehome(cotangent)

    b_key = jnp.zeros_like(b_query)
    b_qkv = insert_zero(pack_columns(mine[:192], b_key, mine[192:384], 0), 0)
    scale = jnp.concatenate([jnp.ones((KV,), jnp.float32), jnp.full((256,), 0.125, jnp.float32)])
    qkv = [((dot_nn(part, w_qkv) + b_qkv) * scale).astype(jnp.bfloat16) for part in rows]

    block = jnp.arange(NB, dtype=jnp.int32)
    block = block ^ (rank * QB)
    fixed = jnp.clip(
        jnp.stack(
            [
                jnp.zeros_like(block),
                jnp.full_like(block, NB - 1),
                block - 1,
                block,
                block + 1,
            ],
            axis=-1,
        ),
        0,
        NB - 1,
    )
    local_random = jnp.take(my_random, block, axis=1)
    table = jnp.concatenate(
        [jnp.broadcast_to(fixed[None], (HEADS, NB, 5)), local_random], axis=-1
    )
    table = (table ^ (rank * QB)).reshape(-1)

    remote, probs = attend_forward((1, 3), rank, table, qkv, None)
    local, probs = attend_forward((0, 2), rank, table, qkv, probs)
    outs = (
        local[0],
        near_of(remote[0]),
        side_of(local[1]),
        flip(remote[1], 1, 1),
    )

    vectors = jnp.stack([b_output, gain_attn, bias_attn, b_down, gain_mlp, bias_mlp])
    layer_out, n1, g, du, dfr, dar, da, do, sums, up_sums = token_block(
        rank, outs, own, grad_top, vectors, b_up_all, rest_all
    )
    grads = (do[0], near_of(do[1]), side_of(do[2]), flip(do[3], 1, 1))
    rest_grad = weight_block(rank, n1, dfr, dar, g, du, outs)
    rest_grad, *grads = lax.optimization_barrier((rest_grad, *grads))
    rest_sum = lax.psum_scatter(
        rest_grad.reshape(GROUP, width, -1), "dp", scatter_dimension=1, tiled=True
    )
    rest_sum = lax.psum_scatter(rest_sum, "tensor", scatter_dimension=0, tiled=False).astype(
        jnp.float32
    )
    shard_up = rest_sum[:, :hidden]
    shard_down = rest_sum[:, hidden : 2 * hidden].T
    shard_output = rest_sum[:, 2 * hidden :].T
    layer_out = rehome(layer_out)

    grad_qkv = attend_backward(table, probs, qkv, grads)

    def input_part(n):
        return dot_nt(grad_qkv[n * QROWS : (n + 1) * QROWS], w_qkv)

    low = jnp.bfloat16
    side_far = side_of(input_part(3).astype(low))
    side_own = side_of(input_part(2).astype(low))
    to_near = (input_part(1) + side_far.astype(jnp.float32)).astype(low)
    base = da + input_part(0) + side_own.astype(jnp.float32)
    near_move = flip(to_near, 0, 1, moves)
    to_near, near_move = lax.optimization_barrier((to_near, near_move))
    near_stay = flip(to_near, 0, 1, stays)
    grad_move = (base + near_move.astype(jnp.float32)).astype(low)
    grad_stay = (base + near_stay.astype(jnp.float32)).astype(low)
    grad_input = jnp.where(here, grad_stay, flip(grad_move, 1, 2, moves))

    all_rows = jnp.concatenate(rows, axis=0)
    grad_w = drop_zero(dot_tn(all_rows, grad_qkv), 1).astype(low)
    for bit in reversed(pair_bits):
        grad_w = halve(flip, (dp_index >> bit) % 2, grad_w, 1 << bit, 0)
    grad_w = halve(flip, half, grad_w, 0, 2)
    shard_query, shard_key, shard_value = unpack_columns(
        rehome(grad_w).astype(jnp.float32), 1
    )

    bias_sum = drop_zero(jnp.sum(grad_qkv.astype(jnp.float32), axis=0), 0)
    bias_query, _, bias_value = unpack_columns(bias_sum, 0)
    bias_pair = jnp.concatenate([bias_query, bias_value])
    groups = jnp.arange(GROUP, dtype=jnp.int32)[:, None]
    bias_pair = jnp.where(groups == rank, bias_pair[None], 0.0)
    sums = jnp.concatenate(
        [
            jnp.sum(sums, axis=1).reshape(-1),
            jnp.sum(up_sums, axis=0),
            bias_pair.reshape(-1),
        ]
    ).reshape(-1, 128)
    sums = sums + side_of(sums)
    for bit in pair_bits:
        sums = sums + flip(sums, 1 << bit, 0)
    for bit in (1, 2):
        sums = sums + flip(sums, 0, bit)
    sums = sums.reshape(-1)
    top = sums[: 6 * width].reshape(6, width)
    grad_b_up = lax.dynamic_slice_in_dim(sums, 6 * width + tensor_index * hidden, hidden, 0)
    bias_pair = lax.dynamic_slice_in_dim(
        sums, 6 * width + GROUP * hidden + tensor_index * 384, 384, 0
    )
    return (
        layer_out,
        grad_input,
        shard_query,
        shard_key,
        shard_value,
        shard_output,
        shard_up,
        shard_down,
        bias_pair[:192],
        bias_pair[192:],
        top[5],
        top[3],
        top[4],
        grad_b_up,
        top[2],
        top[0],
        top[1],
    )


def order_halves(bit, own, other):
    return jnp.where(
        bit == 0,
        jnp.concatenate([own, other], axis=0),
        jnp.concatenate([other, own], axis=0),
    )


def halve(flip, bit, value, d_bits, t_bits):
    rows = value.shape[0] // 2
    keep = lax.dynamic_slice_in_dim(value, bit * rows, rows, 0)
    send = lax.dynamic_slice_in_dim(value, (1 - bit) * rows, rows, 0)
    got = flip(send, d_bits, t_bits)
    return (keep.astype(jnp.float32) + got.astype(jnp.float32)).astype(value.dtype)


def solution(mesh):
    in_specs = (
        P(("dp", "tensor"), None),
        P(("dp", "tensor"), None),
        P("dp", "tensor"),
        P("dp", "tensor"),
        P("dp", "tensor"),
        P("tensor", "dp"),
        P("dp", "tensor"),
        P("tensor", "dp"),
        P("tensor"),
        P("tensor"),
        P(),
        P(),
        P(),
        P("tensor"),
        P(),
        P(),
        P(),
        P("tensor", None, None),
    )
    out_specs = (
        P(("dp", "tensor"), None),
        P(("dp", "tensor"), None),
        P("dp", "tensor"),
        P("dp", "tensor"),
        P("dp", "tensor"),
        P("tensor", "dp"),
        P("dp", "tensor"),
        P("tensor", "dp"),
        P("tensor"),
        P("tensor"),
        P(),
        P(),
        P(),
        P("tensor"),
        P(),
        P(),
        P(),
    )
    body = functools.partial(per_device, mesh.shape["dp"], mesh.shape["tensor"])
    return jax.shard_map(body, mesh=mesh, in_specs=in_specs, out_specs=out_specs, check_vma=False)
```

```python
import functools

import jax
import jax.numpy as jnp
from jax import lax
from jax.experimental import pallas as pl
from jax.experimental.pallas import tpu as pltpu
from jax.sharding import PartitionSpec as P

HD = 64
BLOCK = 64
LENGTH = 4096
NB = LENGTH // BLOCK
GROUP = 4
QROWS = LENGTH // GROUP
QB = QROWS // BLOCK
HEADS = 3
KEYS = 8 * BLOCK
KV = 128 * HEADS
QKV = KV + 256

negative = -1e30
epsilon = 1e-05
both = ("dp", "tensor")
vmem_limit = 56 * 1024 * 1024


def dot_nn(left, right):
    return jnp.dot(left, right, preferred_element_type=jnp.float32)


def dot_tn(left, right):
    return lax.dot_general(
        left, right, (((0,), (0,)), ((), ())), preferred_element_type=jnp.float32
    )


def dot_nt(left, right):
    return lax.dot_general(
        left, right, (((1,), (1,)), ((), ())), preferred_element_type=jnp.float32
    )


def lane_masks(dtype):
    lane = lax.broadcasted_iota(jnp.int32, (1, 128), 1)
    low = (lane < 64).astype(jnp.float32).astype(dtype)
    high = (lane >= 64).astype(jnp.float32).astype(dtype)
    return low, high


def key_bias(block):
    lane = lax.broadcasted_iota(jnp.int32, (1, KEYS), 1)
    entry = lane // BLOCK
    key = jnp.where(entry == 2, block - 1, jnp.where(entry == 3, block, block + 1))
    window = (entry >= 2) & (entry <= 4)
    off = window & ((key < 1) | (key > NB - 2))
    return jnp.where(off, negative, 0.0).astype(jnp.float32)


def gather_keys(table, source, head, block):
    rows = []
    for entry in range(8):
        place = table[(head * NB + block) * 8 + entry]
        rows.append(source[pl.ds(pl.multiple_of(place * BLOCK, BLOCK), BLOCK), head * 128 : head * 128 + 128])
    return jnp.concatenate(rows, axis=0)


def head_queries(first, second, low, high):
    return (first * high, first * low, second)


def forward_kernel(steps, count, project, table, place, *refs):
    step = pl.program_id(0)
    last = step == pl.num_programs(0) - 1
    if project:
        x_refs, (w_ref, add_ref, scale_ref), refs = refs[:4], refs[4:7], refs[7:]
        o_refs, (p_ref, qkv_hbm), refs = refs[:count], refs[count : count + 2], refs[count + 2 :]
        qkv_scr, s_scr, o_scr, x_scr, sems = refs
        out_copy = pltpu.make_async_copy(qkv_scr, qkv_hbm, sems.at[4])

        @pl.when(step == 0)
        def _project():
            copies = [
                pltpu.make_async_copy(src, x_scr.at[pl.ds(n * QROWS, QROWS)], sems.at[n])
                for n, src in enumerate(x_refs)
            ]
            for copy in copies:
                copy.start()
            for copy in copies:
                copy.wait()
            chunk = 256

            def body(n, carry):
                rows = pl.ds(pl.multiple_of(n * chunk, chunk), chunk)
                total = dot_nn(x_scr[rows], w_ref[...]) + add_ref[...]
                qkv_scr[rows] = (total.astype(jnp.bfloat16).astype(jnp.float32) * scale_ref[...]).astype(
                    jnp.bfloat16
                )
                return carry

            lax.fori_loop(0, LENGTH // chunk, body, 0)
            out_copy.start()

        @pl.when(last)
        def _written():
            out_copy.wait()

    else:
        qkv_hbm, _ = refs[:2]
        o_refs, refs = refs[2 : 2 + count], refs[2 + count :]
        p_ref, qkv_scr, s_scr, o_scr, sems = refs

        @pl.when(step == 0)
        def _load():
            copy = pltpu.make_async_copy(qkv_hbm, qkv_scr, sems.at[0])
            copy.start()
            copy.wait()

    low, high = lane_masks(jnp.bfloat16)
    lane = lax.broadcasted_iota(jnp.int32, (1, 128), 1)
    per = QB // steps
    units = [(sub, head) for sub in range(per) for head in range(HEADS)]
    slot = place[1 + step // steps]
    keys = []
    for sub in range(per):
        local = slot * QB + (step % steps) * per + sub
        bias = key_bias(local ^ (place[0] * QB))
        rows = pl.ds(pl.multiple_of(local * BLOCK, BLOCK), BLOCK)
        queries = head_queries(
            qkv_scr[rows, KV : KV + 128], qkv_scr[rows, KV + 128 : KV + 256], low, high
        )
        for head in range(HEADS):
            n = sub * HEADS + head
            keys.append(gather_keys(table, qkv_scr, head, local))
            raw = dot_nt(queries[head], keys[n])
            s_scr[n, :, 0:128] = raw[:, 0:128]
            s_scr[n, :, 128:384] = raw[:, 128:384] + bias[:, 128:384]
            s_scr[n, :, 384:512] = raw[:, 384:512]
    tops = [jnp.max(s_scr[n], axis=1, keepdims=True) for n in range(len(units))]
    sums = []
    for n in range(len(units)):
        expo = jnp.exp(s_scr[n] - tops[n])
        s_scr[n] = expo
        sums.append(jnp.sum(expo, axis=1, keepdims=True))
    for n, (sub, head) in enumerate(units):
        p_ref[sub, head] = (s_scr[n] * (1.0 / sums[n])).astype(jnp.bfloat16)
    for sub in range(per):
        rows = slice(sub * BLOCK, (sub + 1) * BLOCK)
        outs = [dot_nn(p_ref[sub, head], keys[sub * HEADS + head]) for head in range(HEADS)]
        o_scr[rows, 0:128] = jnp.where(lane < 64, outs[0], outs[1]).astype(jnp.bfloat16)
        o_scr[rows, 128:192] = outs[2][:, 0:64].astype(jnp.bfloat16)
    for turn, o_ref in enumerate(o_refs):

        @pl.when(step // steps == turn)
        def _out(o_ref=o_ref):
            o_ref[...] = o_scr[...]


def attend_forward(slots, rank, table, rows=None, weights=None, qkv=None, probs=None):
    steps = 4
    per = QB // steps
    count = len(slots)
    project = rows is not None
    any_spec = pl.BlockSpec(memory_space=pl.ANY)
    place = jnp.stack([rank.astype(jnp.int32)] + [jnp.int32(slot) for slot in slots])
    operands = [table, place] + ([*rows, *weights] if project else [qkv, probs])
    in_specs = [any_spec] * (4 if project else 2)
    if project:
        in_specs += [pl.BlockSpec(each.shape, lambda g, *_: (0, 0)) for each in weights]
    qkv_out = [jax.ShapeDtypeStruct((LENGTH, QKV), jnp.bfloat16)] * project
    extra = [pltpu.VMEM((LENGTH, weights[0].shape[0]), jnp.bfloat16)] if project else []
    return pl.pallas_call(
        functools.partial(forward_kernel, steps, count, project),
        grid_spec=pltpu.PrefetchScalarGridSpec(
            num_scalar_prefetch=2,
            grid=(count * steps,),
            in_specs=in_specs,
            out_specs=[
                pl.BlockSpec(
                    (per * BLOCK, 192),
                    lambda g, *_, turn=turn: (jnp.clip(g - turn * steps, 0, steps - 1), 0),
                )
                for turn in range(count)
            ]
            + [
                pl.BlockSpec(
                    (per, HEADS, BLOCK, KEYS),
                    lambda g, t, pos: (pos[1 + g // steps] * steps + g % steps, 0, 0, 0),
                ),
            ]
            + [any_spec] * project,
            scratch_shapes=[
                pltpu.VMEM((LENGTH, QKV), jnp.bfloat16),
                pltpu.VMEM((per * HEADS, BLOCK, KEYS), jnp.float32),
                pltpu.VMEM((per * BLOCK, 192), jnp.bfloat16),
            ]
            + extra
            + [pltpu.SemaphoreType.DMA((5,))],
        ),
        out_shape=[jax.ShapeDtypeStruct((QROWS, 192), jnp.bfloat16)] * count
        + [jax.ShapeDtypeStruct((NB, HEADS, BLOCK, KEYS), jnp.bfloat16)]
        + qkv_out,
        input_output_aliases={} if project else {3: count},
        compiler_params=pltpu.CompilerParams(
            dimension_semantics=("arbitrary",), vmem_limit_bytes=vmem_limit
        ),
        name="attend_forward",
    )(*operands)


def backward_kernel(
    steps,
    table,
    p_ref,
    qkv_hbm,
    do0,
    do1,
    do2,
    do3,
    w_ref,
    da_hbm,
    out_hbm,
    base_hbm,
    near_hbm,
    side_hbm,
    far_hbm,
    sum_ref,
    qkv_scr,
    do_scr,
    acc,
    dp_scr,
    st_scr,
    out_ref,
    da_scr,
    share_scr,
    sems,
):
    step = pl.program_id(0)

    @pl.when(step == 0)
    def _load():
        copies = [pltpu.make_async_copy(qkv_hbm, qkv_scr, sems.at[0])] + [
            pltpu.make_async_copy(src, do_scr.at[pl.ds(n * QROWS, QROWS)], sems.at[4 + n])
            for n, src in enumerate((do0, do1, do2, do3))
        ]
        copies.append(pltpu.make_async_copy(da_hbm, da_scr, sems.at[8]))
        for copy in copies:
            copy.start()
        acc[...] = jnp.zeros_like(acc)
        for copy in copies:
            copy.wait()

    low, high = lane_masks(jnp.bfloat16)
    lane = lax.broadcasted_iota(jnp.int32, (1, 128), 1)
    per = NB // steps
    units = [(sub, head) for sub in range(per) for head in range(HEADS)]
    keys, right = [], []
    for sub in range(per):
        local = step * per + sub
        rows = pl.ds(pl.multiple_of(local * BLOCK, BLOCK), BLOCK)
        queries = head_queries(
            qkv_scr[rows, KV : KV + 128], qkv_scr[rows, KV + 128 : KV + 256], low, high
        )
        g_first = do_scr[rows, 0:128]
        g_second = do_scr[rows, 128:192]
        grads = (
            g_first * low,
            g_first * high,
            jnp.concatenate([g_second, jnp.zeros_like(g_second)], axis=1),
        )
        for head in range(HEADS):
            n = sub * HEADS + head
            keys.append(gather_keys(table, qkv_scr, head, local))
            right.append(jnp.concatenate([queries[head], grads[head]], axis=0))
            dp_scr[n] = dot_nt(grads[head], keys[n])
    totals = []
    for n, (sub, head) in enumerate(units):
        weighted = p_ref[sub, head].astype(jnp.float32) * dp_scr[n]
        dp_scr[n] = weighted
        totals.append(jnp.sum(weighted, axis=1, keepdims=True))
    for n, (sub, head) in enumerate(units):
        probs = p_ref[sub, head]
        st_scr[n, 0:BLOCK] = (dp_scr[n] - probs.astype(jnp.float32) * totals[n]).astype(jnp.bfloat16)
        st_scr[n, BLOCK:128] = probs
    for sub in range(per):
        local = step * per + sub
        rows = pl.ds(pl.multiple_of(local * BLOCK, BLOCK), BLOCK)
        backs = [
            dot_nn(st_scr[sub * HEADS + head, 0:BLOCK], keys[sub * HEADS + head]) * 0.125
            for head in range(HEADS)
        ]
        out_ref[rows, KV : KV + 128] = jnp.where(lane < 64, backs[1], backs[0]).astype(jnp.bfloat16)
        out_ref[rows, KV + 128 : KV + 256] = jnp.where(lane < 64, 0.0, backs[2]).astype(
            jnp.bfloat16
        )
    for n, (sub, head) in enumerate(units):
        local = step * per + sub
        spread = dot_tn(st_scr[n], right[n])
        for entry in range(8):
            spot = table[(head * NB + local) * 8 + entry]
            where = pl.ds(pl.multiple_of(spot * BLOCK, BLOCK), BLOCK)
            acc[where, head * 128 : head * 128 + 128] += spread[
                entry * BLOCK : (entry + 1) * BLOCK
            ]

    @pl.when(step == steps - 1)
    def _store():
        out_ref[:, 0:KV] = acc[...].astype(jnp.bfloat16)
        total = jnp.zeros((8, QKV), jnp.float32)
        for row in range(0, LENGTH, 128):
            total = total + fold_rows(out_ref[row : row + 128].astype(jnp.float32))
        sum_ref[...] = total
        done = [pltpu.make_async_copy(out_ref, out_hbm, sems.at[0])]
        done[0].start()
        chunk = 256

        def share(n, carry):
            source = (3 - n // (QROWS // chunk)) * QROWS + (n % (QROWS // chunk)) * chunk
            rows = pl.ds(pl.multiple_of(source, chunk), chunk)
            place = pl.ds(pl.multiple_of(n * chunk, chunk), chunk)
            share_scr[place] = dot_nt(out_ref[rows], w_ref[...]).astype(jnp.bfloat16)
            return carry

        lax.fori_loop(0, 3 * QROWS // chunk, share, 0)
        for n, share_hbm in enumerate((far_hbm, side_hbm, near_hbm)):
            rows = pl.ds(n * QROWS, QROWS)
            done.append(pltpu.make_async_copy(share_scr.at[rows], share_hbm, sems.at[1 + n]))
            done[-1].start()

        def base(n, carry):
            rows = pl.ds(pl.multiple_of(n * chunk, chunk), chunk)
            da_scr[rows] += dot_nt(out_ref[rows], w_ref[...])
            return carry

        lax.fori_loop(0, QROWS // chunk, base, 0)
        done.append(pltpu.make_async_copy(da_scr, base_hbm, sems.at[4]))
        done[-1].start()
        for copy in done:
            copy.wait()


def attend_backward(table, probs, qkv, grads, w_qkv, da):
    steps = 16
    per = NB // steps
    width = w_qkv.shape[0]
    any_spec = pl.BlockSpec(memory_space=pl.ANY)
    share = jax.ShapeDtypeStruct((QROWS, width), jnp.bfloat16)
    return pl.pallas_call(
        functools.partial(backward_kernel, steps),
        grid_spec=pltpu.PrefetchScalarGridSpec(
            num_scalar_prefetch=1,
            grid=(steps,),
            in_specs=[pl.BlockSpec((per, HEADS, BLOCK, KEYS), lambda g, *_: (g, 0, 0, 0))]
            + [any_spec] * 5
            + [pl.BlockSpec((width, QKV), lambda g, *_: (0, 0)), any_spec],
            out_specs=[any_spec] * 5 + [pl.BlockSpec((8, QKV), lambda g, *_: (0, 0))],
            scratch_shapes=[
                pltpu.VMEM((LENGTH, QKV), jnp.bfloat16),
                pltpu.VMEM((LENGTH, 192), jnp.bfloat16),
                pltpu.VMEM((LENGTH, KV), jnp.float32),
                pltpu.VMEM((per * HEADS, BLOCK, KEYS), jnp.float32),
                pltpu.VMEM((per * HEADS, 128, KEYS), jnp.bfloat16),
                pltpu.VMEM((LENGTH, QKV), jnp.bfloat16),
                pltpu.VMEM((QROWS, width), jnp.float32),
                pltpu.VMEM((3 * QROWS, width), jnp.bfloat16),
                pltpu.SemaphoreType.DMA((9,)),
            ],
        ),
        out_shape=[
            jax.ShapeDtypeStruct((LENGTH, QKV), jnp.bfloat16),
            jax.ShapeDtypeStruct((QROWS, width), jnp.float32),
            share,
            share,
            share,
            jax.ShapeDtypeStruct((8, QKV), jnp.float32),
        ],
        compiler_params=pltpu.CompilerParams(
            dimension_semantics=("arbitrary",), vmem_limit_bytes=vmem_limit
        ),
        cost_estimate=pl.CostEstimate(
            flops=40 * 10**9, transcendentals=0, bytes_accessed=25 * 10**6
        ),
        name="attend_backward",
    )(table, probs, qkv, *grads, w_qkv, da)


def head_weight_kernel(x0, x1, x2, x3, grad_ref, out_ref, x_scr, acc, sems):
    slot = pl.program_id(0)

    @pl.when(slot == 0)
    def _load():
        copies = [
            pltpu.make_async_copy(src, x_scr.at[pl.ds(n * QROWS, QROWS)], sems.at[n])
            for n, src in enumerate((x0, x1, x2, x3))
        ]
        for copy in copies:
            copy.start()
        acc[...] = jnp.zeros_like(acc)
        for copy in copies:
            copy.wait()

    rows = pl.ds(pl.multiple_of(slot * QROWS, QROWS), QROWS)
    acc[...] += dot_tn(x_scr[rows], grad_ref[...])

    @pl.when(slot == pl.num_programs(0) - 1)
    def _store():
        out_ref[:, 0 : KV + 128] = acc[:, 0 : KV + 128].astype(jnp.bfloat16)
        out_ref[:, KV + 128 : KV + 192] = acc[:, KV + 192 : KV + 256].astype(jnp.bfloat16)


def head_weight_block(rows, grad_qkv):
    width = rows[0].shape[1]
    any_spec = pl.BlockSpec(memory_space=pl.ANY)
    return pl.pallas_call(
        head_weight_kernel,
        grid=(GROUP,),
        in_specs=[any_spec] * 4 + [pl.BlockSpec((QROWS, QKV), lambda g: (g, 0))],
        out_specs=pl.BlockSpec((width, QKV - 64), lambda g: (0, 0)),
        scratch_shapes=[
            pltpu.VMEM((LENGTH, width), jnp.bfloat16),
            pltpu.VMEM((width, QKV), jnp.float32),
            pltpu.SemaphoreType.DMA((4,)),
        ],
        out_shape=jax.ShapeDtypeStruct((width, QKV - 64), jnp.bfloat16),
        compiler_params=pltpu.CompilerParams(
            dimension_semantics=("arbitrary",), vmem_limit_bytes=vmem_limit
        ),
        cost_estimate=pl.CostEstimate(
            flops=8 * 10**9, transcendentals=0, bytes_accessed=12 * 10**6
        ),
        name="head_weight_block",
    )(*rows, grad_qkv)


def row_mean(values):
    return jnp.mean(values, axis=1, keepdims=True)


def fold_rows(values):
    total = values[0:8]
    for row in range(8, values.shape[0], 8):
        total = total + values[row : row + 8]
    return total


def token_kernel(
    tile,
    width,
    hidden,
    rank_ref,
    o0,
    o1,
    o2,
    o3,
    x_ref,
    cot_ref,
    vec_ref,
    up_bias_ref,
    weights,
    out_ref,
    n1_ref,
    g_ref,
    du_ref,
    dfr_ref,
    dar_ref,
    da_ref,
    do0,
    do1,
    do2,
    do3,
    total_ref,
    w_scr,
    acc,
    u_scr,
    slope_scr,
    xhat_scr,
    m1_scr,
    sum_ref,
    up_sum_ref,
    sem,
):
    step = pl.program_id(0)
    parts = GROUP
    small = 32
    cols = 256

    @pl.when(step == 0)
    def _load():
        copy = pltpu.make_async_copy(weights, w_scr, sem)
        copy.start()
        sum_ref[...] = jnp.zeros_like(sum_ref)
        up_sum_ref[...] = jnp.zeros_like(up_sum_ref)
        copy.wait()

    def vector(n):
        return vec_ref[n : n + 1, :]

    def part_rows(n):
        return slice(n * width, (n + 1) * width)

    def out_weight(n):
        place = pl.multiple_of((rank_ref[0] ^ n) * width, width)
        return w_scr[pl.ds(place, width), 2 * hidden :]

    total = dot_nt(o0[...], out_weight(0))
    for n, piece in ((1, o1), (2, o2), (3, o3)):
        total = total + dot_nt(piece[...], out_weight(n))
    acc[...] = total
    first_scale = []
    for row in range(0, tile, small):
        rows = slice(row, row + small)
        resid = acc[rows] + x_ref[rows].astype(jnp.float32) + vector(0)
        center = resid - row_mean(resid)
        scale = lax.rsqrt(row_mean(center * center) + epsilon)
        xhat = center * scale
        normed = xhat * vector(1) + vector(2)
        first_scale.append(scale)
        xhat_scr[rows] = xhat
        m1_scr[rows] = normed
        n1_ref[rows] = normed.astype(jnp.bfloat16)
    for part in range(parts):
        u_scr[part % 2] = dot_nn(n1_ref[...], w_scr[part_rows(part), 0:hidden])
        for row in range(0, tile, small):
            rows = slice(row, row + small)
            for col in range(0, hidden, cols):
                place = slice(col, col + cols)
                wide = slice(part * hidden + col, part * hidden + col + cols)
                pre = u_scr[part % 2, rows, place] + up_bias_ref[:, wide]
                cdf = 0.5 + 0.5 * lax.erf(pre * 0.7071067811865476)
                g_ref[rows, wide] = (pre * cdf).astype(jnp.bfloat16)
                slope_scr[rows, wide] = (
                    cdf + pre * jnp.exp(-0.5 * pre * pre) * 0.3989422804014327
                )
        lift = dot_nt(
            g_ref[:, part * hidden : (part + 1) * hidden],
            w_scr[part_rows(part), hidden : 2 * hidden],
        )
        if part == 0:
            acc[...] = lift
        else:
            acc[...] += lift
    sums = [jnp.zeros((8, width), jnp.float32) for _ in range(6)]
    for row in range(0, tile, small):
        rows = slice(row, row + small)
        second = m1_scr[rows] + acc[rows] + vector(3)
        center = second - row_mean(second)
        scale = lax.rsqrt(row_mean(center * center) + epsilon)
        xhat = center * scale
        out_ref[rows] = (xhat * vector(4) + vector(5)).astype(jnp.bfloat16)
        top = cot_ref[rows].astype(jnp.float32)
        gained = top * vector(4)
        down = scale * (gained - row_mean(gained) - xhat * row_mean(gained * xhat))
        sums[0] = sums[0] + fold_rows(top * xhat)
        sums[1] = sums[1] + fold_rows(top)
        sums[2] = sums[2] + fold_rows(down)
        m1_scr[rows] = down
        dfr_ref[rows] = down.astype(jnp.bfloat16)
    for part in range(parts):
        whole = slice(part * hidden, (part + 1) * hidden)
        u_scr[part % 2] = dot_nn(dfr_ref[...], w_scr[part_rows(part), hidden : 2 * hidden])
        for col in range(0, hidden, cols):
            place = slice(col, col + cols)
            wide = slice(part * hidden + col, part * hidden + col + cols)
            tally = jnp.zeros((8, cols), jnp.float32)
            for row in range(0, tile, small):
                rows = slice(row, row + small)
                low = (u_scr[part % 2, rows, place] * slope_scr[rows, wide]).astype(jnp.bfloat16)
                du_ref[rows, wide] = low
                tally = tally + fold_rows(low.astype(jnp.float32))
            up_sum_ref[:, wide] += tally
        lift = dot_nt(du_ref[:, whole], w_scr[part_rows(part), 0:hidden])
        if part == 0:
            acc[...] = lift
        else:
            acc[...] += lift
    for n, row in enumerate(range(0, tile, small)):
        rows = slice(row, row + small)
        back = m1_scr[rows] + acc[rows]
        xhat = xhat_scr[rows]
        sums[3] = sums[3] + fold_rows(back * xhat)
        sums[4] = sums[4] + fold_rows(back)
        gained = back * vector(1)
        down = first_scale[n] * (gained - row_mean(gained) - xhat * row_mean(gained * xhat))
        sums[5] = sums[5] + fold_rows(down)
        da_ref[rows] = down
        dar_ref[rows] = down.astype(jnp.bfloat16)
    for n in range(6):
        sum_ref[n] += sums[n]
    for n, do_ref in enumerate((do0, do1, do2, do3)):
        do_ref[...] = dot_nn(dar_ref[...], out_weight(n)).astype(jnp.bfloat16)

    @pl.when(step == pl.num_programs(0) - 1)
    def _totals():
        for n in range(6):
            total_ref[:, n * width : (n + 1) * width] = jnp.sum(
                sum_ref[n], axis=0, keepdims=True
            )
        total_ref[:, 6 * width :] = jnp.sum(up_sum_ref[...], axis=0, keepdims=True)


def token_block(rank, outs, own, cot, vectors, up_bias, weights):
    count, width = own.shape
    total_hidden = up_bias.shape[1]
    hidden = total_hidden // GROUP
    tile = 256

    def rows_of(columns):
        return pl.BlockSpec((tile, columns), lambda g, *_: (g, 0))

    def whole(shape):
        return pl.BlockSpec(shape, lambda g, *_: (0,) * len(shape))

    low = jnp.bfloat16
    head = outs[0].shape[1]
    return pl.pallas_call(
        functools.partial(token_kernel, tile, width, hidden),
        grid_spec=pltpu.PrefetchScalarGridSpec(
            num_scalar_prefetch=1,
            grid=(count // tile,),
            in_specs=[rows_of(head)] * 4
            + [rows_of(width)] * 2
            + [whole(vectors.shape), whole(up_bias.shape)] + [pl.BlockSpec(memory_space=pl.ANY)],
            out_specs=[
                rows_of(width),
                rows_of(width),
                rows_of(total_hidden),
                rows_of(total_hidden),
                rows_of(width),
                rows_of(width),
                rows_of(width),
                rows_of(head),
                rows_of(head),
                rows_of(head),
                rows_of(head),
                whole((1, 6 * width + total_hidden)),
            ],
            scratch_shapes=[
                pltpu.VMEM(weights.shape, low),
                pltpu.VMEM((tile, width), jnp.float32),
                pltpu.VMEM((2, tile, hidden), jnp.float32),
                pltpu.VMEM((tile, total_hidden), jnp.float32),
                pltpu.VMEM((tile, width), jnp.float32),
                pltpu.VMEM((tile, width), jnp.float32),
                pltpu.VMEM((6, 8, width), jnp.float32),
                pltpu.VMEM((8, total_hidden), jnp.float32),
                pltpu.SemaphoreType.DMA,
            ],
        ),
        out_shape=[
            jax.ShapeDtypeStruct((count, width), low),
            jax.ShapeDtypeStruct((count, width), low),
            jax.ShapeDtypeStruct((count, total_hidden), low),
            jax.ShapeDtypeStruct((count, total_hidden), low),
            jax.ShapeDtypeStruct((count, width), low),
            jax.ShapeDtypeStruct((count, width), low),
            jax.ShapeDtypeStruct((count, width), jnp.float32),
            jax.ShapeDtypeStruct((count, head), low),
            jax.ShapeDtypeStruct((count, head), low),
            jax.ShapeDtypeStruct((count, head), low),
            jax.ShapeDtypeStruct((count, head), low),
            jax.ShapeDtypeStruct((1, 6 * width + total_hidden), jnp.float32),
        ],
        compiler_params=pltpu.CompilerParams(
            dimension_semantics=("arbitrary",), vmem_limit_bytes=vmem_limit
        ),
        cost_estimate=pl.CostEstimate(
            flops=46 * 10**9, transcendentals=0, bytes_accessed=40 * 10**6
        ),
        name="token_block",
    )(rank.astype(jnp.int32).reshape(1), *outs, own, cot, vectors, up_bias, weights)


def weight_kernel(width, hidden, rank_ref, n1, dfr, dar, g, du, o0, o1, o2, o3, out_ref, n1_t, dfr_t, dar_t):
    part = pl.program_id(0)

    @pl.when(part == 0)
    def _turn():
        n1_t[...] = n1[...].T
        dfr_t[...] = dfr[...].T
        dar_t[...] = dar[...].T

    chunk = 256

    def product(n, carry):
        rows = pl.ds(pl.multiple_of(n * chunk, chunk), chunk)
        out_ref[rows, 0:hidden] = dot_nn(n1_t[rows], du[...]).astype(jnp.bfloat16)
        out_ref[rows, hidden : 2 * hidden] = dot_nn(dfr_t[rows], g[...]).astype(jnp.bfloat16)
        return carry

    lax.fori_loop(0, width // chunk, product, 0)
    for n, piece in enumerate((o0, o1, o2, o3)):

        @pl.when(part == rank_ref[0] ^ n)
        def _out(piece=piece):
            out_ref[:, 2 * hidden :] = dot_nn(dar_t[...], piece[...]).astype(jnp.bfloat16)


def weight_block(rank, n1, dfr, dar, g, du, outs):
    count, width = n1.shape
    hidden = g.shape[1] // GROUP
    head = outs[0].shape[1]
    columns = 2 * hidden + head
    low = jnp.bfloat16

    def whole(shape):
        return pl.BlockSpec(shape, lambda g, *_: (0,) * len(shape))

    return pl.pallas_call(
        functools.partial(weight_kernel, width, hidden),
        grid_spec=pltpu.PrefetchScalarGridSpec(
            num_scalar_prefetch=1,
            grid=(GROUP,),
            in_specs=[whole((count, width))] * 3
            + [pl.BlockSpec((count, hidden), lambda g, *_: (0, g))] * 2
            + [whole((count, head))] * 4,
            out_specs=pl.BlockSpec((width, columns), lambda g, *_: (g, 0)),
            scratch_shapes=[pltpu.VMEM((width, count), low)] * 3,
        ),
        out_shape=jax.ShapeDtypeStruct((GROUP * width, columns), low),
        compiler_params=pltpu.CompilerParams(
            dimension_semantics=("arbitrary",), vmem_limit_bytes=vmem_limit
        ),
        cost_estimate=pl.CostEstimate(
            flops=22 * 10**9, transcendentals=0, bytes_accessed=30 * 10**6
        ),
        name="weight_block",
    )(rank.astype(jnp.int32).reshape(1), n1, dfr, dar, g, du, *outs)


def pack_columns(query, key, value, axis):
    def piece(matrix, head):
        return lax.slice_in_dim(matrix, head * HD, (head + 1) * HD, axis=axis)

    return jnp.concatenate(
        [
            piece(value, 0),
            piece(key, 0),
            piece(key, 1),
            piece(value, 1),
            piece(value, 2),
            piece(key, 2),
            piece(query, 1),
            piece(query, 0),
            piece(query, 2),
        ],
        axis=axis,
    )


def insert_zero(packed, axis):
    head = lax.slice_in_dim(packed, 0, KV + 128, axis=axis)
    tail = lax.slice_in_dim(packed, KV + 128, KV + 192, axis=axis)
    return jnp.concatenate([head, jnp.zeros_like(tail), tail], axis=axis)


def drop_zero(packed, axis):
    head = lax.slice_in_dim(packed, 0, KV + 128, axis=axis)
    tail = lax.slice_in_dim(packed, KV + 192, KV + 256, axis=axis)
    return jnp.concatenate([head, tail], axis=axis)


def unpack_columns(packed, axis):
    def piece(n):
        return lax.slice_in_dim(packed, n * HD, (n + 1) * HD, axis=axis)

    query = jnp.concatenate([piece(7), piece(6), piece(8)], axis=axis)
    key = jnp.concatenate([piece(1), piece(2), piece(5)], axis=axis)
    value = jnp.concatenate([piece(0), piece(3), piece(4)], axis=axis)
    return query, key, value


def per_device(
    dp_size,
    tensor_size,
    inputs,
    cotangent,
    w_query,
    w_key,
    w_value,
    w_output,
    w_up,
    w_down,
    b_query,
    b_value,
    b_output,
    gain_attn,
    bias_attn,
    b_up,
    b_down,
    gain_mlp,
    bias_mlp,
    random_blocks,
):
    width = inputs.shape[1]
    hidden = b_up.shape[0]
    low = jnp.bfloat16
    dp_index = lax.axis_index("dp")
    tensor_index = lax.axis_index("tensor")
    core = dp_index % 2
    half = tensor_index // 2
    rank = 2 * core + tensor_index % 2
    here = core == half
    devices = [(d, t) for d in range(dp_size) for t in range(tensor_size)]
    pair_bits = [bit for bit in range(1, dp_size.bit_length() - 1)]

    def flat(d, t):
        return d * tensor_size + t

    def stays(d, t):
        return d % 2 == t // 2

    def flip(value, d_bits, t_bits, chosen=None):
        pairs = [
            (flat(d, t), flat(d ^ d_bits, t ^ t_bits))
            for d, t in devices
            if chosen is None or chosen(d, t)
        ]
        return lax.ppermute(value, both, pairs)

    def moves(d, t):
        return not stays(d, t)

    def rehome(value):
        return jnp.where(here, value, flip(value, 1, 2, moves))

    def near_of(value):
        return flip(value, 0, 1)

    def side_of(value):
        return flip(value, 1, 0)

    rest = jnp.concatenate([w_up, w_down.T, w_output.T], axis=1)
    below = jnp.concatenate(split_three(b_up))
    below = jnp.pad(below, (0, -below.shape[0] % rest.shape[1])).reshape(-1, rest.shape[1])
    rest = lax.all_gather(jnp.concatenate([rest, below], axis=0), "tensor", axis=0)

    packed = pack_columns(w_query, w_key, w_value, 1)
    columns = packed.shape[1]
    floats = jnp.concatenate([b_query, b_value])
    small = jnp.concatenate(split_three(floats) + [random_blocks.astype(low).reshape(-1)])
    small = jnp.pad(small, (0, -small.shape[0] % columns)).reshape(-1, columns)
    packed = jnp.concatenate([order_halves(core, packed, side_of(packed)), small], axis=0)
    packed = jnp.where(here, packed, flip(packed, 0, 2, stays))
    inputs, packed = lax.optimization_barrier((inputs, packed))
    moved = flip(inputs, 1, 2, moves)
    near_stay = flip(inputs, 0, 1, stays)
    small = packed[2 * w_query.shape[0] :].reshape(-1)
    packed = packed[: 2 * w_query.shape[0]]
    for bit in pair_bits:
        packed = order_halves((dp_index >> bit) % 2, packed, flip(packed, 1 << bit, 0))
    w_qkv = insert_zero(packed, 1)
    count = floats.shape[0]
    mine = sum(small[n * count : (n + 1) * count].astype(jnp.float32) for n in range(3))
    my_random = small[3 * count : 3 * count + random_blocks.size]
    my_random = my_random.reshape(HEADS, NB, -1).astype(jnp.int32)
    b_key = jnp.zeros_like(b_query)
    b_qkv = insert_zero(pack_columns(mine[:192], b_key, mine[192:], 0), 0)
    scale = jnp.concatenate([jnp.ones((KV,), jnp.float32), jnp.full((256,), 0.125, jnp.float32)])

    moved, rest, w_qkv, b_qkv = lax.optimization_barrier((moved, rest, w_qkv, b_qkv))
    below = rest[:, w_up.shape[0] :].reshape(GROUP, -1)
    rest_all = lax.all_gather(
        rest[:, : w_up.shape[0]], "dp", axis=1, tiled=True
    ).reshape(GROUP * width, -1)
    b_up_all = sum(
        below[:, n * hidden : (n + 1) * hidden].astype(jnp.float32) for n in range(3)
    ).reshape(1, -1)
    own = jnp.where(here, inputs, moved)
    near_move = flip(own, 0, 1, moves)

    near = jnp.where(here, near_stay, near_move)
    near, own, cotangent = lax.optimization_barrier((near, own, cotangent))
    side, far = side_of(own), side_of(near)
    cot_moved = flip(cotangent, 1, 2, moves)
    rows = (own, near, side, far)
    grad_top = jnp.where(here, cotangent, cot_moved)
    block = jnp.arange(NB, dtype=jnp.int32)
    block = block ^ (rank * QB)
    fixed = jnp.clip(
        jnp.stack(
            [
                jnp.zeros_like(block),
                jnp.full_like(block, NB - 1),
                block - 1,
                block,
                block + 1,
            ],
            axis=-1,
        ),
        0,
        NB - 1,
    )
    local_random = jnp.take(my_random, block, axis=1)
    table = jnp.concatenate(
        [jnp.broadcast_to(fixed[None], (HEADS, NB, 5)), local_random], axis=-1
    )
    table = (table ^ (rank * QB)).reshape(-1)

    weights = (w_qkv, b_qkv[None], scale[None])
    out_near, out_far, out_side, probs, qkv = attend_forward((1, 3, 2), rank, table, rows, weights)
    out_own, probs = attend_forward((0,), rank, table, qkv=qkv, probs=probs)
    outs = (out_own, near_of(out_near), side_of(out_side), flip(out_far, 1, 1))

    vectors = jnp.stack([b_output, gain_attn, bias_attn, b_down, gain_mlp, bias_mlp])
    layer_out, n1, g, du, dfr, dar, da, *do, sums = token_block(
        rank, outs, own, grad_top, vectors, b_up_all, rest_all
    )
    grads = (do[0], near_of(do[1]), side_of(do[2]), flip(do[3], 1, 1))
    rest_grad = weight_block(rank, n1, dfr, dar, g, du, outs)
    sums = sums.reshape(-1)
    sums = sums + flip(sums, 0, 1)
    rest_grad, sums, *grads = lax.optimization_barrier((rest_grad, sums, *grads))
    rest_sum = lax.psum_scatter(
        rest_grad.reshape(GROUP, width, -1), "dp", scatter_dimension=1, tiled=True
    )
    rest_sum = lax.psum_scatter(rest_sum, "tensor", scatter_dimension=0, tiled=False).astype(
        jnp.float32
    )
    shard_up = rest_sum[:, :hidden]
    shard_down = rest_sum[:, hidden : 2 * hidden].T
    shard_output = rest_sum[:, 2 * hidden :].T
    layer_sent = flip(layer_out, 1, 2, moves)

    grad_qkv, base, to_near, to_side, to_far, bias_sum = attend_backward(
        table, probs, qkv, grads, w_qkv, da
    )
    grad_qkv, base, to_near, to_side, to_far, bias_sum, layer_sent = lax.optimization_barrier(
        (grad_qkv, base, to_near, to_side, to_far, bias_sum, layer_sent)
    )
    side_far = side_of(to_far)
    side_own = side_of(to_side)
    bias_query, _, bias_value = unpack_columns(drop_zero(jnp.sum(bias_sum, axis=0), 0), 0)
    sums = jnp.concatenate([sums, bias_query, bias_value])
    sums = sums + flip(sums, 0, 2)
    to_near = (to_near.astype(jnp.float32) + side_far.astype(jnp.float32)).astype(low)
    to_near, sums = lax.optimization_barrier((to_near, sums))
    near_move = flip(to_near, 0, 1, moves)
    base = base + side_own.astype(jnp.float32)
    grad_late, to_near = lax.optimization_barrier((grad_qkv, to_near))
    for bit in pair_bits:
        sums = sums + flip(sums, 1 << bit, 0)
    other = side_of(sums)
    grad_w = head_weight_block(rows, grad_late)
    to_near, near_move, grad_w, base, sums, other = lax.optimization_barrier(
        (to_near, near_move, grad_w, base, sums, other)
    )
    grad_move = (base + near_move.astype(jnp.float32)).astype(low)
    grad_move, to_near, grad_w, base = lax.optimization_barrier(
        (grad_move, to_near, grad_w, base)
    )
    grad_moved = flip(grad_move, 1, 2, moves)
    near_stay = flip(to_near, 0, 1, stays)
    grad_stay = (base + near_stay.astype(jnp.float32)).astype(low)
    grad_moved, grad_stay = lax.optimization_barrier((grad_moved, grad_stay))
    grad_input = jnp.where(here, grad_stay, grad_moved)

    for bit in reversed(pair_bits):
        grad_w = halve(flip, (dp_index >> bit) % 2, grad_w, 1 << bit, 0)
    grad_w, layer_sent = lax.optimization_barrier((grad_w, layer_sent))
    layer_out = jnp.where(here, layer_out, layer_sent)
    grad_w = grad_w.astype(jnp.float32) + flip(grad_w, 0, 2, moves).astype(jnp.float32)
    rows_each = grad_w.shape[0] // 2
    grad_w = grad_w.astype(low)
    keep = lax.dynamic_slice_in_dim(grad_w, core * rows_each, rows_each, 0)
    send = lax.dynamic_slice_in_dim(grad_w, (1 - core) * rows_each, rows_each, 0)
    shard = jnp.where(here, keep, side_of(send)).astype(jnp.float32)
    shard_query, shard_key, shard_value = unpack_columns(shard, 1)

    count = 6 * width + GROUP * hidden
    bias_pair = jnp.where(here, sums[count:], other[count:])
    sums = sums + other
    top = sums[: 6 * width].reshape(6, width)
    grad_b_up = lax.dynamic_slice_in_dim(sums, 6 * width + tensor_index * hidden, hidden, 0)
    return (
        layer_out,
        grad_input,
        shard_query,
        shard_key,
        shard_value,
        shard_output,
        shard_up,
        shard_down,
        bias_pair[:192],
        bias_pair[192:],
        top[5],
        top[3],
        top[4],
        grad_b_up,
        top[2],
        top[0],
        top[1],
    )


def order_halves(bit, own, other):
    return jnp.where(
        bit == 0,
        jnp.concatenate([own, other], axis=0),
        jnp.concatenate([other, own], axis=0),
    )


def split_three(values):
    parts = []
    for _ in range(3):
        part = lax.reduce_precision(values, 8, 7)
        parts.append(part.astype(jnp.bfloat16))
        values = values - part
    return parts


def halve(flip, bit, value, d_bits, t_bits):
    rows = value.shape[0] // 2
    keep = lax.dynamic_slice_in_dim(value, bit * rows, rows, 0)
    send = lax.dynamic_slice_in_dim(value, (1 - bit) * rows, rows, 0)
    got = flip(send, d_bits, t_bits)
    return (keep.astype(jnp.float32) + got.astype(jnp.float32)).astype(value.dtype)


def solution(mesh):
    in_specs = (
        P(("dp", "tensor"), None),
        P(("dp", "tensor"), None),
        P("dp", "tensor"),
        P("dp", "tensor"),
        P("dp", "tensor"),
        P("tensor", "dp"),
        P("dp", "tensor"),
        P("tensor", "dp"),
        P("tensor"),
        P("tensor"),
        P(),
        P(),
        P(),
        P("tensor"),
        P(),
        P(),
        P(),
        P("tensor", None, None),
    )
    out_specs = (
        P(("dp", "tensor"), None),
        P(("dp", "tensor"), None),
        P("dp", "tensor"),
        P("dp", "tensor"),
        P("dp", "tensor"),
        P("tensor", "dp"),
        P("dp", "tensor"),
        P("tensor", "dp"),
        P("tensor"),
        P("tensor"),
        P(),
        P(),
        P(),
        P("tensor"),
        P(),
        P(),
        P(),
    )
    body = functools.partial(per_device, mesh.shape["dp"], mesh.shape["tensor"])
    return jax.shard_map(body, mesh=mesh, in_specs=in_specs, out_specs=out_specs, check_vma=False)
```

```python
import functools

import jax
import jax.numpy as jnp
from jax import lax
from jax.experimental import pallas as pl
from jax.experimental.pallas import tpu as pltpu
from jax.sharding import PartitionSpec as P

HD = 64
BLOCK = 64
LENGTH = 4096
NB = LENGTH // BLOCK
GROUP = 4
QROWS = LENGTH // GROUP
QB = QROWS // BLOCK
HEADS = 3
KEYS = 8 * BLOCK
KV = 128 * HEADS
QKV = KV + 256

negative = -1e30
epsilon = 1e-05
both = ("dp", "tensor")
vmem_limit = 56 * 1024 * 1024


def dot_nn(left, right):
    return jnp.dot(left, right, preferred_element_type=jnp.float32)


def dot_tn(left, right):
    return lax.dot_general(
        left, right, (((0,), (0,)), ((), ())), preferred_element_type=jnp.float32
    )


def dot_nt(left, right):
    return lax.dot_general(
        left, right, (((1,), (1,)), ((), ())), preferred_element_type=jnp.float32
    )


def lane_masks(dtype):
    lane = lax.broadcasted_iota(jnp.int32, (1, 128), 1)
    low = (lane < 64).astype(jnp.float32).astype(dtype)
    high = (lane >= 64).astype(jnp.float32).astype(dtype)
    return low, high


def key_bias(block):
    lane = lax.broadcasted_iota(jnp.int32, (1, KEYS), 1)
    entry = lane // BLOCK
    key = jnp.where(entry == 2, block - 1, jnp.where(entry == 3, block, block + 1))
    window = (entry >= 2) & (entry <= 4)
    off = window & ((key < 1) | (key > NB - 2))
    return jnp.where(off, negative, 0.0).astype(jnp.float32)


def gather_keys(table, source, head, block):
    rows = []
    for entry in range(8):
        place = table[(head * NB + block) * 8 + entry]
        rows.append(source[pl.ds(pl.multiple_of(place * BLOCK, BLOCK), BLOCK), head * 128 : head * 128 + 128])
    return jnp.concatenate(rows, axis=0)


def head_queries(first, second, low, high):
    return (first * high, first * low, second)


def forward_kernel(steps, count, project, table, place, *refs):
    step = pl.program_id(0)
    last = step == pl.num_programs(0) - 1
    if project:
        x_refs, (w_ref, add_ref, scale_ref), refs = refs[:4], refs[4:7], refs[7:]
        o_refs, (p_ref, qkv_hbm), refs = refs[:count], refs[count : count + 2], refs[count + 2 :]
        qkv_scr, s_scr, o_scr, x_scr, sems = refs
        out_copy = pltpu.make_async_copy(qkv_scr, qkv_hbm, sems.at[4])

        @pl.when(step == 0)
        def _project():
            copies = [
                pltpu.make_async_copy(src, x_scr.at[pl.ds(n * QROWS, QROWS)], sems.at[n])
                for n, src in enumerate(x_refs)
            ]
            for copy in copies:
                copy.start()
            for copy in copies:
                copy.wait()
            chunk = 512

            def body(n, carry):
                rows = pl.ds(pl.multiple_of(n * chunk, chunk), chunk)
                total = dot_nn(x_scr[rows], w_ref[...]) + add_ref[...]
                qkv_scr[rows] = (total.astype(jnp.bfloat16).astype(jnp.float32) * scale_ref[...]).astype(
                    jnp.bfloat16
                )
                return carry

            lax.fori_loop(0, LENGTH // chunk, body, 0)
            out_copy.start()

        @pl.when(last)
        def _written():
            out_copy.wait()

    else:
        qkv_hbm, _ = refs[:2]
        o_refs, refs = refs[2 : 2 + count], refs[2 + count :]
        p_ref, qkv_scr, s_scr, o_scr, sems = refs

        @pl.when(step == 0)
        def _load():
            copy = pltpu.make_async_copy(qkv_hbm, qkv_scr, sems.at[0])
            copy.start()
            copy.wait()

    low, high = lane_masks(jnp.bfloat16)
    lane = lax.broadcasted_iota(jnp.int32, (1, 128), 1)
    per = QB // steps
    units = [(sub, head) for sub in range(per) for head in range(HEADS)]
    slot = place[1 + step // steps]
    keys = []
    for sub in range(per):
        local = slot * QB + (step % steps) * per + sub
        bias = key_bias(local ^ (place[0] * QB))
        rows = pl.ds(pl.multiple_of(local * BLOCK, BLOCK), BLOCK)
        queries = head_queries(
            qkv_scr[rows, KV : KV + 128], qkv_scr[rows, KV + 128 : KV + 256], low, high
        )
        for head in range(HEADS):
            n = sub * HEADS + head
            keys.append(gather_keys(table, qkv_scr, head, local))
            raw = dot_nt(queries[head], keys[n])
            s_scr[n, :, 0:128] = raw[:, 0:128]
            s_scr[n, :, 128:384] = raw[:, 128:384] + bias[:, 128:384]
            s_scr[n, :, 384:512] = raw[:, 384:512]
    tops = [jnp.max(s_scr[n], axis=1, keepdims=True) for n in range(len(units))]
    sums = []
    for n in range(len(units)):
        expo = jnp.exp(s_scr[n] - tops[n])
        s_scr[n] = expo
        sums.append(jnp.sum(expo, axis=1, keepdims=True))
    for n, (sub, head) in enumerate(units):
        p_ref[sub, head] = (s_scr[n] * (1.0 / sums[n])).astype(jnp.bfloat16)
    for sub in range(per):
        rows = slice(sub * BLOCK, (sub + 1) * BLOCK)
        outs = [dot_nn(p_ref[sub, head], keys[sub * HEADS + head]) for head in range(HEADS)]
        o_scr[rows, 0:128] = jnp.where(lane < 64, outs[0], outs[1]).astype(jnp.bfloat16)
        o_scr[rows, 128:192] = outs[2][:, 0:64].astype(jnp.bfloat16)
    for turn, o_ref in enumerate(o_refs):

        @pl.when(step // steps == turn)
        def _out(o_ref=o_ref):
            o_ref[...] = o_scr[...]


def attend_forward(slots, rank, table, rows=None, weights=None, qkv=None, probs=None):
    steps = 4
    per = QB // steps
    count = len(slots)
    project = rows is not None
    any_spec = pl.BlockSpec(memory_space=pl.ANY)
    place = jnp.stack([rank.astype(jnp.int32)] + [jnp.int32(slot) for slot in slots])
    operands = [table, place] + ([*rows, *weights] if project else [qkv, probs])
    in_specs = [any_spec] * (4 if project else 2)
    if project:
        in_specs += [pl.BlockSpec(each.shape, lambda g, *_: (0, 0)) for each in weights]
    qkv_out = [jax.ShapeDtypeStruct((LENGTH, QKV), jnp.bfloat16)] * project
    extra = [pltpu.VMEM((LENGTH, weights[0].shape[0]), jnp.bfloat16)] if project else []
    return pl.pallas_call(
        functools.partial(forward_kernel, steps, count, project),
        grid_spec=pltpu.PrefetchScalarGridSpec(
            num_scalar_prefetch=2,
            grid=(count * steps,),
            in_specs=in_specs,
            out_specs=[
                pl.BlockSpec(
                    (per * BLOCK, 192),
                    lambda g, *_, turn=turn: (jnp.clip(g - turn * steps, 0, steps - 1), 0),
                )
                for turn in range(count)
            ]
            + [
                pl.BlockSpec(
                    (per, HEADS, BLOCK, KEYS),
                    lambda g, t, pos: (pos[1 + g // steps] * steps + g % steps, 0, 0, 0),
                ),
            ]
            + [any_spec] * project,
            scratch_shapes=[
                pltpu.VMEM((LENGTH, QKV), jnp.bfloat16),
                pltpu.VMEM((per * HEADS, BLOCK, KEYS), jnp.float32),
                pltpu.VMEM((per * BLOCK, 192), jnp.bfloat16),
            ]
            + extra
            + [pltpu.SemaphoreType.DMA((5,))],
        ),
        out_shape=[jax.ShapeDtypeStruct((QROWS, 192), jnp.bfloat16)] * count
        + [jax.ShapeDtypeStruct((NB, HEADS, BLOCK, KEYS), jnp.bfloat16)]
        + qkv_out,
        input_output_aliases={} if project else {3: count},
        compiler_params=pltpu.CompilerParams(
            dimension_semantics=("arbitrary",), vmem_limit_bytes=vmem_limit
        ),
        name="attend_forward",
    )(*operands)


def backward_kernel(
    steps,
    table,
    p_ref,
    qkv_hbm,
    do0,
    do1,
    do2,
    do3,
    o0,
    o1,
    o2,
    o3,
    w_ref,
    da_hbm,
    out_hbm,
    base_hbm,
    near_hbm,
    side_hbm,
    far_hbm,
    sum_ref,
    qkv_scr,
    do_scr,
    o_scr,
    acc,
    st_scr,
    out_ref,
    da_scr,
    share_scr,
    sems,
):
    step = pl.program_id(0)

    @pl.when(step == 0)
    def _load():
        copies = [pltpu.make_async_copy(qkv_hbm, qkv_scr, sems.at[0])] + [
            pltpu.make_async_copy(src, do_scr.at[pl.ds(n * QROWS, QROWS)], sems.at[4 + n])
            for n, src in enumerate((do0, do1, do2, do3))
        ]
        copies += [
            pltpu.make_async_copy(src, o_scr.at[pl.ds(n * QROWS, QROWS)], sems.at[9 + n])
            for n, src in enumerate((o0, o1, o2, o3))
        ]
        copies.append(pltpu.make_async_copy(da_hbm, da_scr, sems.at[8]))
        for copy in copies:
            copy.start()
        acc[...] = jnp.zeros_like(acc)
        for copy in copies:
            copy.wait()

    low, high = lane_masks(jnp.bfloat16)
    lane = lax.broadcasted_iota(jnp.int32, (1, 128), 1)
    per = NB // steps
    units = [(sub, head) for sub in range(per) for head in range(HEADS)]
    keys, right, wide_low, wide_high = [], [], low.astype(jnp.float32), high.astype(jnp.float32)
    for sub in range(per):
        local = step * per + sub
        rows = pl.ds(pl.multiple_of(local * BLOCK, BLOCK), BLOCK)
        queries = head_queries(
            qkv_scr[rows, KV : KV + 128], qkv_scr[rows, KV + 128 : KV + 256], low, high
        )
        g_first = do_scr[rows, 0:128]
        g_second = do_scr[rows, 128:192]
        first = g_first.astype(jnp.float32) * o_scr[rows, 0:128].astype(jnp.float32)
        second = g_second.astype(jnp.float32) * o_scr[rows, 128:192].astype(jnp.float32)
        totals = (
            jnp.sum(first * wide_low, axis=1, keepdims=True),
            jnp.sum(first * wide_high, axis=1, keepdims=True),
            jnp.sum(second, axis=1, keepdims=True),
        )
        grads = (
            g_first * low,
            g_first * high,
            jnp.concatenate([g_second, jnp.zeros_like(g_second)], axis=1),
        )
        for head in range(HEADS):
            n = sub * HEADS + head
            keys.append(gather_keys(table, qkv_scr, head, local))
            right.append(jnp.concatenate([queries[head], grads[head]], axis=0))
            probs = p_ref[sub, head]
            slopes = probs.astype(jnp.float32) * (dot_nt(grads[head], keys[n]) - totals[head])
            st_scr[n, 0:BLOCK] = slopes.astype(jnp.bfloat16)
            st_scr[n, BLOCK:128] = probs
    for sub in range(per):
        local = step * per + sub
        rows = pl.ds(pl.multiple_of(local * BLOCK, BLOCK), BLOCK)
        backs = [
            dot_nn(st_scr[sub * HEADS + head, 0:BLOCK], keys[sub * HEADS + head]) * 0.125
            for head in range(HEADS)
        ]
        out_ref[rows, KV : KV + 128] = jnp.where(lane < 64, backs[1], backs[0]).astype(jnp.bfloat16)
        out_ref[rows, KV + 128 : KV + 256] = jnp.where(lane < 64, 0.0, backs[2]).astype(
            jnp.bfloat16
        )
    for n, (sub, head) in enumerate(units):
        local = step * per + sub
        spread = dot_tn(st_scr[n], right[n])
        for entry in range(8):
            spot = table[(head * NB + local) * 8 + entry]
            where = pl.ds(pl.multiple_of(spot * BLOCK, BLOCK), BLOCK)
            acc[where, head * 128 : head * 128 + 128] += spread[
                entry * BLOCK : (entry + 1) * BLOCK
            ]

    @pl.when(step == steps - 1)
    def _store():
        out_ref[:, 0:KV] = acc[...].astype(jnp.bfloat16)
        total = jnp.zeros((8, QKV), jnp.float32)
        for row in range(0, LENGTH, 128):
            total = total + fold_rows(out_ref[row : row + 128].astype(jnp.float32))
        sum_ref[...] = total
        done = [pltpu.make_async_copy(out_ref, out_hbm, sems.at[0])]
        done[0].start()
        chunk = 512

        def share(n, carry):
            source = (3 - n // (QROWS // chunk)) * QROWS + (n % (QROWS // chunk)) * chunk
            rows = pl.ds(pl.multiple_of(source, chunk), chunk)
            place = pl.ds(pl.multiple_of(n * chunk, chunk), chunk)
            share_scr[place] = dot_nt(out_ref[rows], w_ref[...]).astype(jnp.bfloat16)
            return carry

        lax.fori_loop(0, 3 * QROWS // chunk, share, 0)
        for n, share_hbm in enumerate((far_hbm, side_hbm, near_hbm)):
            rows = pl.ds(n * QROWS, QROWS)
            done.append(pltpu.make_async_copy(share_scr.at[rows], share_hbm, sems.at[1 + n]))
            done[-1].start()

        def base(n, carry):
            rows = pl.ds(pl.multiple_of(n * chunk, chunk), chunk)
            da_scr[rows] += dot_nt(out_ref[rows], w_ref[...])
            return carry

        lax.fori_loop(0, QROWS // chunk, base, 0)
        done.append(pltpu.make_async_copy(da_scr, base_hbm, sems.at[4]))
        done[-1].start()
        for copy in done:
            copy.wait()


def attend_backward(table, probs, qkv, grads, outs, w_qkv, da):
    steps = 16
    per = NB // steps
    width = w_qkv.shape[0]
    any_spec = pl.BlockSpec(memory_space=pl.ANY)
    share = jax.ShapeDtypeStruct((QROWS, width), jnp.bfloat16)
    return pl.pallas_call(
        functools.partial(backward_kernel, steps),
        grid_spec=pltpu.PrefetchScalarGridSpec(
            num_scalar_prefetch=1,
            grid=(steps,),
            in_specs=[pl.BlockSpec((per, HEADS, BLOCK, KEYS), lambda g, *_: (g, 0, 0, 0))]
            + [any_spec] * 9
            + [pl.BlockSpec((width, QKV), lambda g, *_: (0, 0)), any_spec],
            out_specs=[any_spec] * 5 + [pl.BlockSpec((8, QKV), lambda g, *_: (0, 0))],
            scratch_shapes=[
                pltpu.VMEM((LENGTH, QKV), jnp.bfloat16),
                pltpu.VMEM((LENGTH, 192), jnp.bfloat16),
                pltpu.VMEM((LENGTH, 192), jnp.bfloat16),
                pltpu.VMEM((LENGTH, KV), jnp.float32),
                pltpu.VMEM((per * HEADS, 128, KEYS), jnp.bfloat16),
                pltpu.VMEM((LENGTH, QKV), jnp.bfloat16),
                pltpu.VMEM((QROWS, width), jnp.float32),
                pltpu.VMEM((3 * QROWS, width), jnp.bfloat16),
                pltpu.SemaphoreType.DMA((13,)),
            ],
        ),
        out_shape=[
            jax.ShapeDtypeStruct((LENGTH, QKV), jnp.bfloat16),
            jax.ShapeDtypeStruct((QROWS, width), jnp.float32),
            share,
            share,
            share,
            jax.ShapeDtypeStruct((8, QKV), jnp.float32),
        ],
        compiler_params=pltpu.CompilerParams(
            dimension_semantics=("arbitrary",), vmem_limit_bytes=vmem_limit
        ),
        cost_estimate=pl.CostEstimate(
            flops=40 * 10**9, transcendentals=0, bytes_accessed=25 * 10**6
        ),
        name="attend_backward",
    )(table, probs, qkv, *grads, *outs, w_qkv, da)


def head_weight_kernel(x0, x1, x2, x3, grad_ref, out_ref, x_scr, acc, sems):
    slot = pl.program_id(0)

    @pl.when(slot == 0)
    def _load():
        copies = [
            pltpu.make_async_copy(src, x_scr.at[pl.ds(n * QROWS, QROWS)], sems.at[n])
            for n, src in enumerate((x0, x1, x2, x3))
        ]
        for copy in copies:
            copy.start()
        acc[...] = jnp.zeros_like(acc)
        for copy in copies:
            copy.wait()

    rows = pl.ds(pl.multiple_of(slot * QROWS, QROWS), QROWS)
    acc[...] += dot_tn(x_scr[rows], grad_ref[...])

    @pl.when(slot == pl.num_programs(0) - 1)
    def _store():
        out_ref[:, 0 : KV + 128] = acc[:, 0 : KV + 128].astype(jnp.bfloat16)
        out_ref[:, KV + 128 : KV + 192] = acc[:, KV + 192 : KV + 256].astype(jnp.bfloat16)


def head_weight_block(rows, grad_qkv):
    width = rows[0].shape[1]
    any_spec = pl.BlockSpec(memory_space=pl.ANY)
    return pl.pallas_call(
        head_weight_kernel,
        grid=(GROUP,),
        in_specs=[any_spec] * 4 + [pl.BlockSpec((QROWS, QKV), lambda g: (g, 0))],
        out_specs=pl.BlockSpec((width, QKV - 64), lambda g: (0, 0)),
        scratch_shapes=[
            pltpu.VMEM((LENGTH, width), jnp.bfloat16),
            pltpu.VMEM((width, QKV), jnp.float32),
            pltpu.SemaphoreType.DMA((4,)),
        ],
        out_shape=jax.ShapeDtypeStruct((width, QKV - 64), jnp.bfloat16),
        compiler_params=pltpu.CompilerParams(
            dimension_semantics=("arbitrary",), vmem_limit_bytes=vmem_limit
        ),
        cost_estimate=pl.CostEstimate(
            flops=8 * 10**9, transcendentals=0, bytes_accessed=12 * 10**6
        ),
        name="head_weight_block",
    )(*rows, grad_qkv)


def row_mean(values):
    return jnp.mean(values, axis=1, keepdims=True)


def fold_rows(values):
    total = values[0:8]
    for row in range(8, values.shape[0], 8):
        total = total + values[row : row + 8]
    return total


def token_kernel(
    tile,
    width,
    hidden,
    rank_ref,
    o0,
    o1,
    o2,
    o3,
    x_ref,
    cot_ref,
    vec_ref,
    up_bias_ref,
    weights,
    out_ref,
    n1_ref,
    g_ref,
    du_ref,
    dfr_ref,
    dar_ref,
    da_ref,
    do0,
    do1,
    do2,
    do3,
    total_ref,
    w_scr,
    acc,
    u_scr,
    slope_scr,
    xhat_scr,
    m1_scr,
    sum_ref,
    up_sum_ref,
    sem,
):
    step = pl.program_id(0)
    parts = GROUP
    small = 32
    cols = 256
    spans = ((2 * hidden, weights.shape[1] - 2 * hidden), (0, hidden), (hidden, hidden))
    arrivals = [
        pltpu.make_async_copy(
            weights.at[:, pl.ds(*span)], w_scr.at[:, pl.ds(*span)], sem.at[n]
        )
        for n, span in enumerate(spans)
    ]

    @pl.when(step == 0)
    def _load():
        for copy in arrivals:
            copy.start()
        sum_ref[...] = jnp.zeros_like(sum_ref)
        up_sum_ref[...] = jnp.zeros_like(up_sum_ref)
        arrivals[0].wait()

    def vector(n):
        return vec_ref[n : n + 1, :]

    def part_rows(n):
        return slice(n * width, (n + 1) * width)

    def out_weight(n):
        place = pl.multiple_of((rank_ref[0] ^ n) * width, width)
        return w_scr[pl.ds(place, width), 2 * hidden :]

    total = dot_nt(o0[...], out_weight(0))
    for n, piece in ((1, o1), (2, o2), (3, o3)):
        total = total + dot_nt(piece[...], out_weight(n))
    acc[...] = total
    first_scale = []
    for row in range(0, tile, small):
        rows = slice(row, row + small)
        resid = acc[rows] + x_ref[rows].astype(jnp.float32) + vector(0)
        center = resid - row_mean(resid)
        scale = lax.rsqrt(row_mean(center * center) + epsilon)
        xhat = center * scale
        normed = xhat * vector(1) + vector(2)
        first_scale.append(scale)
        xhat_scr[rows] = xhat
        m1_scr[rows] = normed
        n1_ref[rows] = normed.astype(jnp.bfloat16)

    @pl.when(step == 0)
    def _arrived():
        arrivals[1].wait()
        arrivals[2].wait()

    for part in range(parts):
        u_scr[part % 2] = dot_nn(n1_ref[...], w_scr[part_rows(part), 0:hidden])
        for row in range(0, tile, small):
            rows = slice(row, row + small)
            for col in range(0, hidden, cols):
                place = slice(col, col + cols)
                wide = slice(part * hidden + col, part * hidden + col + cols)
                pre = u_scr[part % 2, rows, place] + up_bias_ref[:, wide]
                cdf = 0.5 + 0.5 * lax.erf(pre * 0.7071067811865476)
                g_ref[rows, wide] = (pre * cdf).astype(jnp.bfloat16)
                slope_scr[rows, wide] = (
                    cdf + pre * jnp.exp(-0.5 * pre * pre) * 0.3989422804014327
                )
        lift = dot_nt(
            g_ref[:, part * hidden : (part + 1) * hidden],
            w_scr[part_rows(part), hidden : 2 * hidden],
        )
        if part == 0:
            acc[...] = lift
        else:
            acc[...] += lift
    sums = [jnp.zeros((8, width), jnp.float32) for _ in range(6)]
    for row in range(0, tile, small):
        rows = slice(row, row + small)
        second = m1_scr[rows] + acc[rows] + vector(3)
        center = second - row_mean(second)
        scale = lax.rsqrt(row_mean(center * center) + epsilon)
        xhat = center * scale
        out_ref[rows] = (xhat * vector(4) + vector(5)).astype(jnp.bfloat16)
        top = cot_ref[rows].astype(jnp.float32)
        gained = top * vector(4)
        down = scale * (gained - row_mean(gained) - xhat * row_mean(gained * xhat))
        sums[0] = sums[0] + fold_rows(top * xhat)
        sums[1] = sums[1] + fold_rows(top)
        sums[2] = sums[2] + fold_rows(down)
        m1_scr[rows] = down
        dfr_ref[rows] = down.astype(jnp.bfloat16)
    for part in range(parts):
        whole = slice(part * hidden, (part + 1) * hidden)
        u_scr[part % 2] = dot_nn(dfr_ref[...], w_scr[part_rows(part), hidden : 2 * hidden])
        for col in range(0, hidden, cols):
            place = slice(col, col + cols)
            wide = slice(part * hidden + col, part * hidden + col + cols)
            tally = jnp.zeros((8, cols), jnp.float32)
            for row in range(0, tile, small):
                rows = slice(row, row + small)
                low = (u_scr[part % 2, rows, place] * slope_scr[rows, wide]).astype(jnp.bfloat16)
                du_ref[rows, wide] = low
                tally = tally + fold_rows(low.astype(jnp.float32))
            up_sum_ref[:, wide] += tally
        lift = dot_nt(du_ref[:, whole], w_scr[part_rows(part), 0:hidden])
        if part == 0:
            acc[...] = lift
        else:
            acc[...] += lift
    for n, row in enumerate(range(0, tile, small)):
        rows = slice(row, row + small)
        back = m1_scr[rows] + acc[rows]
        xhat = xhat_scr[rows]
        sums[3] = sums[3] + fold_rows(back * xhat)
        sums[4] = sums[4] + fold_rows(back)
        gained = back * vector(1)
        down = first_scale[n] * (gained - row_mean(gained) - xhat * row_mean(gained * xhat))
        sums[5] = sums[5] + fold_rows(down)
        da_ref[rows] = down
        dar_ref[rows] = down.astype(jnp.bfloat16)
    for n in range(6):
        sum_ref[n] += sums[n]
    for n, do_ref in enumerate((do0, do1, do2, do3)):
        do_ref[...] = dot_nn(dar_ref[...], out_weight(n)).astype(jnp.bfloat16)

    @pl.when(step == pl.num_programs(0) - 1)
    def _totals():
        for n in range(6):
            total_ref[:, n * width : (n + 1) * width] = jnp.sum(
                sum_ref[n], axis=0, keepdims=True
            )
        total_ref[:, 6 * width :] = jnp.sum(up_sum_ref[...], axis=0, keepdims=True)


def token_block(rank, outs, own, cot, vectors, up_bias, weights):
    count, width = own.shape
    total_hidden = up_bias.shape[1]
    hidden = total_hidden // GROUP
    tile = 256

    def rows_of(columns):
        return pl.BlockSpec((tile, columns), lambda g, *_: (g, 0))

    def whole(shape):
        return pl.BlockSpec(shape, lambda g, *_: (0,) * len(shape))

    low = jnp.bfloat16
    head = outs[0].shape[1]
    return pl.pallas_call(
        functools.partial(token_kernel, tile, width, hidden),
        grid_spec=pltpu.PrefetchScalarGridSpec(
            num_scalar_prefetch=1,
            grid=(count // tile,),
            in_specs=[rows_of(head)] * 4
            + [rows_of(width)] * 2
            + [whole(vectors.shape), whole(up_bias.shape)] + [pl.BlockSpec(memory_space=pl.ANY)],
            out_specs=[
                rows_of(width),
                rows_of(width),
                rows_of(total_hidden),
                rows_of(total_hidden),
                rows_of(width),
                rows_of(width),
                rows_of(width),
                rows_of(head),
                rows_of(head),
                rows_of(head),
                rows_of(head),
                whole((1, 6 * width + total_hidden)),
            ],
            scratch_shapes=[
                pltpu.VMEM(weights.shape, low),
                pltpu.VMEM((tile, width), jnp.float32),
                pltpu.VMEM((2, tile, hidden), jnp.float32),
                pltpu.VMEM((tile, total_hidden), jnp.float32),
                pltpu.VMEM((tile, width), jnp.float32),
                pltpu.VMEM((tile, width), jnp.float32),
                pltpu.VMEM((6, 8, width), jnp.float32),
                pltpu.VMEM((8, total_hidden), jnp.float32),
                pltpu.SemaphoreType.DMA((3,)),
            ],
        ),
        out_shape=[
            jax.ShapeDtypeStruct((count, width), low),
            jax.ShapeDtypeStruct((count, width), low),
            jax.ShapeDtypeStruct((count, total_hidden), low),
            jax.ShapeDtypeStruct((count, total_hidden), low),
            jax.ShapeDtypeStruct((count, width), low),
            jax.ShapeDtypeStruct((count, width), low),
            jax.ShapeDtypeStruct((count, width), jnp.float32),
            jax.ShapeDtypeStruct((count, head), low),
            jax.ShapeDtypeStruct((count, head), low),
            jax.ShapeDtypeStruct((count, head), low),
            jax.ShapeDtypeStruct((count, head), low),
            jax.ShapeDtypeStruct((1, 6 * width + total_hidden), jnp.float32),
        ],
        compiler_params=pltpu.CompilerParams(
            dimension_semantics=("arbitrary",), vmem_limit_bytes=vmem_limit
        ),
        cost_estimate=pl.CostEstimate(
            flops=46 * 10**9, transcendentals=0, bytes_accessed=40 * 10**6
        ),
        name="token_block",
    )(rank.astype(jnp.int32).reshape(1), *outs, own, cot, vectors, up_bias, weights)


def weight_kernel(width, hidden, rank_ref, n1, dfr, dar, g, du, o0, o1, o2, o3, out_ref, n1_t, dfr_t, dar_t):
    part = pl.program_id(0)

    @pl.when(part == 0)
    def _turn():
        n1_t[...] = n1[...].T
        dfr_t[...] = dfr[...].T
        dar_t[...] = dar[...].T

    chunk = 256

    def product(n, carry):
        rows = pl.ds(pl.multiple_of(n * chunk, chunk), chunk)
        out_ref[rows, 0:hidden] = dot_nn(n1_t[rows], du[...]).astype(jnp.bfloat16)
        out_ref[rows, hidden : 2 * hidden] = dot_nn(dfr_t[rows], g[...]).astype(jnp.bfloat16)
        return carry

    lax.fori_loop(0, width // chunk, product, 0)
    for n, piece in enumerate((o0, o1, o2, o3)):

        @pl.when(part == rank_ref[0] ^ n)
        def _out(piece=piece):
            out_ref[:, 2 * hidden :] = dot_nn(dar_t[...], piece[...]).astype(jnp.bfloat16)


def weight_block(rank, n1, dfr, dar, g, du, outs):
    count, width = n1.shape
    hidden = g.shape[1] // GROUP
    head = outs[0].shape[1]
    columns = 2 * hidden + head
    low = jnp.bfloat16

    def whole(shape):
        return pl.BlockSpec(shape, lambda g, *_: (0,) * len(shape))

    return pl.pallas_call(
        functools.partial(weight_kernel, width, hidden),
        grid_spec=pltpu.PrefetchScalarGridSpec(
            num_scalar_prefetch=1,
            grid=(GROUP,),
            in_specs=[whole((count, width))] * 3
            + [pl.BlockSpec((count, hidden), lambda g, *_: (0, g))] * 2
            + [whole((count, head))] * 4,
            out_specs=pl.BlockSpec((width, columns), lambda g, *_: (g, 0)),
            scratch_shapes=[pltpu.VMEM((width, count), low)] * 3,
        ),
        out_shape=jax.ShapeDtypeStruct((GROUP * width, columns), low),
        compiler_params=pltpu.CompilerParams(
            dimension_semantics=("arbitrary",), vmem_limit_bytes=vmem_limit
        ),
        cost_estimate=pl.CostEstimate(
            flops=22 * 10**9, transcendentals=0, bytes_accessed=30 * 10**6
        ),
        name="weight_block",
    )(rank.astype(jnp.int32).reshape(1), n1, dfr, dar, g, du, *outs)


def pack_columns(query, key, value, axis):
    def piece(matrix, head):
        return lax.slice_in_dim(matrix, head * HD, (head + 1) * HD, axis=axis)

    return jnp.concatenate(
        [
            piece(value, 0),
            piece(key, 0),
            piece(key, 1),
            piece(value, 1),
            piece(value, 2),
            piece(key, 2),
            piece(query, 1),
            piece(query, 0),
            piece(query, 2),
        ],
        axis=axis,
    )


def insert_zero(packed, axis):
    head = lax.slice_in_dim(packed, 0, KV + 128, axis=axis)
    tail = lax.slice_in_dim(packed, KV + 128, KV + 192, axis=axis)
    return jnp.concatenate([head, jnp.zeros_like(tail), tail], axis=axis)


def drop_zero(packed, axis):
    head = lax.slice_in_dim(packed, 0, KV + 128, axis=axis)
    tail = lax.slice_in_dim(packed, KV + 192, KV + 256, axis=axis)
    return jnp.concatenate([head, tail], axis=axis)


def unpack_columns(packed, axis):
    def piece(n):
        return lax.slice_in_dim(packed, n * HD, (n + 1) * HD, axis=axis)

    query = jnp.concatenate([piece(7), piece(6), piece(8)], axis=axis)
    key = jnp.concatenate([piece(1), piece(2), piece(5)], axis=axis)
    value = jnp.concatenate([piece(0), piece(3), piece(4)], axis=axis)
    return query, key, value


def per_device(
    dp_size,
    tensor_size,
    inputs,
    cotangent,
    w_query,
    w_key,
    w_value,
    w_output,
    w_up,
    w_down,
    b_query,
    b_value,
    b_output,
    gain_attn,
    bias_attn,
    b_up,
    b_down,
    gain_mlp,
    bias_mlp,
    random_blocks,
):
    width = inputs.shape[1]
    hidden = b_up.shape[0]
    low = jnp.bfloat16
    dp_index = lax.axis_index("dp")
    tensor_index = lax.axis_index("tensor")
    core = dp_index % 2
    half = tensor_index // 2
    rank = 2 * core + tensor_index % 2
    here = core == half
    devices = [(d, t) for d in range(dp_size) for t in range(tensor_size)]
    pair_bits = [bit for bit in range(1, dp_size.bit_length() - 1)]

    def flat(d, t):
        return d * tensor_size + t

    def stays(d, t):
        return d % 2 == t // 2

    def flip(value, d_bits, t_bits, chosen=None):
        pairs = [
            (flat(d, t), flat(d ^ d_bits, t ^ t_bits))
            for d, t in devices
            if chosen is None or chosen(d, t)
        ]
        return lax.ppermute(value, both, pairs)

    def moves(d, t):
        return not stays(d, t)

    def rehome(value):
        return jnp.where(here, value, flip(value, 1, 2, moves))

    def near_of(value):
        return flip(value, 0, 1)

    def side_of(value):
        return flip(value, 1, 0)

    rest = jnp.concatenate([w_up, w_down.T, w_output.T], axis=1)
    below = jnp.concatenate(split_three(b_up))
    below = jnp.pad(below, (0, -below.shape[0] % rest.shape[1])).reshape(-1, rest.shape[1])
    rest = lax.all_gather(jnp.concatenate([rest, below], axis=0), "tensor", axis=0)

    packed = pack_columns(w_query, w_key, w_value, 1)
    columns = packed.shape[1]
    floats = jnp.concatenate([b_query, b_value])
    small = jnp.concatenate(split_three(floats) + [random_blocks.astype(low).reshape(-1)])
    small = jnp.pad(small, (0, -small.shape[0] % columns)).reshape(-1, columns)
    packed = jnp.concatenate([order_halves(core, packed, side_of(packed)), small], axis=0)
    packed = jnp.where(here, packed, flip(packed, 0, 2, stays))
    inputs, packed = lax.optimization_barrier((inputs, packed))
    moved = flip(inputs, 1, 2, moves)
    near_stay = flip(inputs, 0, 1, stays)
    small = packed[2 * w_query.shape[0] :].reshape(-1)
    packed = packed[: 2 * w_query.shape[0]]
    for bit in pair_bits:
        packed = order_halves((dp_index >> bit) % 2, packed, flip(packed, 1 << bit, 0))
    w_qkv = insert_zero(packed, 1)
    count = floats.shape[0]
    mine = sum(small[n * count : (n + 1) * count].astype(jnp.float32) for n in range(3))
    my_random = small[3 * count : 3 * count + random_blocks.size]
    my_random = my_random.reshape(HEADS, NB, -1).astype(jnp.int32)
    b_key = jnp.zeros_like(b_query)
    b_qkv = insert_zero(pack_columns(mine[:192], b_key, mine[192:], 0), 0)
    scale = jnp.concatenate([jnp.ones((KV,), jnp.float32), jnp.full((256,), 0.125, jnp.float32)])

    moved, rest, w_qkv, b_qkv = lax.optimization_barrier((moved, rest, w_qkv, b_qkv))
    below = rest[:, w_up.shape[0] :].reshape(GROUP, -1)
    rest_all = lax.all_gather(
        rest[:, : w_up.shape[0]], "dp", axis=1, tiled=True
    ).reshape(GROUP * width, -1)
    b_up_all = sum(
        below[:, n * hidden : (n + 1) * hidden].astype(jnp.float32) for n in range(3)
    ).reshape(1, -1)
    own = jnp.where(here, inputs, moved)
    near_move = flip(own, 0, 1, moves)

    near = jnp.where(here, near_stay, near_move)
    near, own, cotangent = lax.optimization_barrier((near, own, cotangent))
    side, far = side_of(own), side_of(near)
    cot_moved = flip(cotangent, 1, 2, moves)
    rows = (own, near, side, far)
    grad_top = jnp.where(here, cotangent, cot_moved)
    block = jnp.arange(NB, dtype=jnp.int32)
    block = block ^ (rank * QB)
    fixed = jnp.clip(
        jnp.stack(
            [
                jnp.zeros_like(block),
                jnp.full_like(block, NB - 1),
                block - 1,
                block,
                block + 1,
            ],
            axis=-1,
        ),
        0,
        NB - 1,
    )
    local_random = jnp.take(my_random, block, axis=1)
    table = jnp.concatenate(
        [jnp.broadcast_to(fixed[None], (HEADS, NB, 5)), local_random], axis=-1
    )
    table = (table ^ (rank * QB)).reshape(-1)

    weights = (w_qkv, b_qkv[None], scale[None])
    out_near, out_far, out_side, probs, qkv = attend_forward((1, 3, 2), rank, table, rows, weights)
    out_own, probs = attend_forward((0,), rank, table, qkv=qkv, probs=probs)
    outs = (out_own, near_of(out_near), side_of(out_side), flip(out_far, 1, 1))

    vectors = jnp.stack([b_output, gain_attn, bias_attn, b_down, gain_mlp, bias_mlp])
    layer_out, n1, g, du, dfr, dar, da, *do, sums = token_block(
        rank, outs, own, grad_top, vectors, b_up_all, rest_all
    )
    grads = (do[0], near_of(do[1]), side_of(do[2]), flip(do[3], 1, 1))
    rest_grad = weight_block(rank, n1, dfr, dar, g, du, outs)
    sums = sums.reshape(-1)
    sums = sums + flip(sums, 0, 1)
    rest_grad, sums, *grads = lax.optimization_barrier((rest_grad, sums, *grads))
    rest_sum = lax.psum_scatter(
        rest_grad.reshape(GROUP, width, -1), "dp", scatter_dimension=1, tiled=True
    )
    layer_sent = flip(layer_out, 1, 2, moves)

    grad_qkv, base, to_near, to_side, to_far, bias_sum = attend_backward(
        table, probs, qkv, grads, (out_own, out_near, out_side, out_far), w_qkv, da
    )
    grad_qkv, base, to_near, to_side, to_far, bias_sum, layer_sent = lax.optimization_barrier(
        (grad_qkv, base, to_near, to_side, to_far, bias_sum, layer_sent)
    )
    side_far = side_of(to_far)
    side_own = side_of(to_side)
    bias_query, _, bias_value = unpack_columns(drop_zero(jnp.sum(bias_sum, axis=0), 0), 0)
    sums = jnp.concatenate([sums, bias_query, bias_value])
    sums = sums + flip(sums, 0, 2)
    to_near = (to_near.astype(jnp.float32) + side_far.astype(jnp.float32)).astype(low)
    to_near, sums = lax.optimization_barrier((to_near, sums))
    near_got = near_of(to_near)
    base = base + side_own.astype(jnp.float32)
    grad_late, to_near = lax.optimization_barrier((grad_qkv, to_near))
    for bit in pair_bits:
        sums = sums + flip(sums, 1 << bit, 0)
    other = side_of(sums)
    grad_late, sums = lax.optimization_barrier((grad_late, sums))
    grad_w = head_weight_block(rows, grad_late)
    rest_sum, base, grad_w = lax.optimization_barrier((rest_sum, base, grad_w))
    rest_sum = lax.psum_scatter(rest_sum, "tensor", scatter_dimension=0, tiled=False).astype(
        jnp.float32
    )
    for bit in reversed(pair_bits[2:]):
        grad_w = halve(flip, (dp_index >> bit) % 2, grad_w, 1 << bit, 0)
    place = (dp_index // 2) % 4
    rows_each = grad_w.shape[0] // 4
    total = lax.dynamic_slice_in_dim(grad_w, place * rows_each, rows_each, 0).astype(jnp.float32)
    for n in (3, 1, 2):
        send = lax.dynamic_slice_in_dim(grad_w, (place ^ n) * rows_each, rows_each, 0)
        total = total + flip(send, 2 * n, 0).astype(jnp.float32)
    grad_w = total.astype(low)
    near_got, grad_w, base, sums, other, layer_sent = lax.optimization_barrier(
        (near_got, grad_w, base, sums, other, layer_sent)
    )
    grad_own = (base + near_got.astype(jnp.float32)).astype(low)
    grad_own, grad_w, layer_sent = lax.optimization_barrier((grad_own, grad_w, layer_sent))
    grad_moved = flip(grad_own, 1, 2, moves)

    grad_got = flip(grad_w, 0, 2, moves)
    grad_w = grad_w.astype(jnp.float32) + grad_got.astype(jnp.float32)
    rows_each = grad_w.shape[0] // 2
    grad_w = grad_w.astype(low)
    keep = lax.dynamic_slice_in_dim(grad_w, core * rows_each, rows_each, 0)
    send = lax.dynamic_slice_in_dim(grad_w, (1 - core) * rows_each, rows_each, 0)
    side_got = side_of(send)
    grad_moved, side_got, rest_sum = lax.optimization_barrier((grad_moved, side_got, rest_sum))
    shard = jnp.where(here, keep, side_got).astype(jnp.float32)
    shard_query, shard_key, shard_value = unpack_columns(shard, 1)
    shard_up = rest_sum[:, :hidden]
    shard_down = rest_sum[:, hidden : 2 * hidden].T
    shard_output = rest_sum[:, 2 * hidden :].T
    layer_out = jnp.where(here, layer_out, layer_sent)
    grad_input = jnp.where(here, grad_own, grad_moved)

    count = 6 * width + GROUP * hidden
    bias_pair = jnp.where(here, sums[count:], other[count:])
    sums = sums + other
    top = sums[: 6 * width].reshape(6, width)
    grad_b_up = lax.dynamic_slice_in_dim(sums, 6 * width + tensor_index * hidden, hidden, 0)
    return (
        layer_out,
        grad_input,
        shard_query,
        shard_key,
        shard_value,
        shard_output,
        shard_up,
        shard_down,
        bias_pair[:192],
        bias_pair[192:],
        top[5],
        top[3],
        top[4],
        grad_b_up,
        top[2],
        top[0],
        top[1],
    )


def order_halves(bit, own, other):
    return jnp.where(
        bit == 0,
        jnp.concatenate([own, other], axis=0),
        jnp.concatenate([other, own], axis=0),
    )


def split_three(values):
    parts = []
    for _ in range(3):
        part = lax.reduce_precision(values, 8, 7)
        parts.append(part.astype(jnp.bfloat16))
        values = values - part
    return parts


def halve(flip, bit, value, d_bits, t_bits):
    rows = value.shape[0] // 2
    keep = lax.dynamic_slice_in_dim(value, bit * rows, rows, 0)
    send = lax.dynamic_slice_in_dim(value, (1 - bit) * rows, rows, 0)
    got = flip(send, d_bits, t_bits)
    return (keep.astype(jnp.float32) + got.astype(jnp.float32)).astype(value.dtype)


def solution(mesh):
    in_specs = (
        P(("dp", "tensor"), None),
        P(("dp", "tensor"), None),
        P("dp", "tensor"),
        P("dp", "tensor"),
        P("dp", "tensor"),
        P("tensor", "dp"),
        P("dp", "tensor"),
        P("tensor", "dp"),
        P("tensor"),
        P("tensor"),
        P(),
        P(),
        P(),
        P("tensor"),
        P(),
        P(),
        P(),
        P("tensor", None, None),
    )
    out_specs = (
        P(("dp", "tensor"), None),
        P(("dp", "tensor"), None),
        P("dp", "tensor"),
        P("dp", "tensor"),
        P("dp", "tensor"),
        P("tensor", "dp"),
        P("dp", "tensor"),
        P("tensor", "dp"),
        P("tensor"),
        P("tensor"),
        P(),
        P(),
        P(),
        P("tensor"),
        P(),
        P(),
        P(),
    )
    body = functools.partial(per_device, mesh.shape["dp"], mesh.shape["tensor"])
    return jax.shard_map(body, mesh=mesh, in_specs=in_specs, out_specs=out_specs, check_vma=False)
```

```python
import functools

import jax
import jax.numpy as jnp
from jax import lax
from jax.experimental import pallas as pl
from jax.experimental.pallas import tpu as pltpu
from jax.sharding import PartitionSpec as P

HD = 64
BLOCK = 64
LENGTH = 4096
NB = LENGTH // BLOCK
GROUP = 4
QROWS = LENGTH // GROUP
QB = QROWS // BLOCK
HEADS = 3
KEYS = 8 * BLOCK
KV = 128 * HEADS
QKV = KV + 256

negative = -1e30
epsilon = 1e-05
both = ("dp", "tensor")
vmem_limit = 56 * 1024 * 1024


def dot_nn(left, right):
    return jnp.dot(left, right, preferred_element_type=jnp.float32)


def dot_tn(left, right):
    return lax.dot_general(
        left, right, (((0,), (0,)), ((), ())), preferred_element_type=jnp.float32
    )


def dot_nt(left, right):
    return lax.dot_general(
        left, right, (((1,), (1,)), ((), ())), preferred_element_type=jnp.float32
    )


def lane_masks(dtype):
    lane = lax.broadcasted_iota(jnp.int32, (1, 128), 1)
    low = (lane < 64).astype(jnp.float32).astype(dtype)
    high = (lane >= 64).astype(jnp.float32).astype(dtype)
    return low, high


def key_bias(block):
    lane = lax.broadcasted_iota(jnp.int32, (1, KEYS), 1)
    entry = lane // BLOCK
    key = jnp.where(entry == 2, block - 1, jnp.where(entry == 3, block, block + 1))
    window = (entry >= 2) & (entry <= 4)
    off = window & ((key < 1) | (key > NB - 2))
    return jnp.where(off, negative, 0.0).astype(jnp.float32)


def gather_keys(table, source, head, block):
    rows = []
    for entry in range(8):
        place = table[(head * NB + block) * 8 + entry]
        rows.append(source[pl.ds(pl.multiple_of(place * BLOCK, BLOCK), BLOCK), head * 128 : head * 128 + 128])
    return jnp.concatenate(rows, axis=0)


def head_queries(first, second, low, high):
    return (first * high, first * low, second)


def forward_kernel(steps, count, project, table, place, *refs):
    step = pl.program_id(0)
    last = step == pl.num_programs(0) - 1
    if project:
        x_refs, (w_ref, add_ref, scale_ref), refs = refs[:4], refs[4:7], refs[7:]
        o_refs, (p_ref, qkv_hbm), refs = refs[:count], refs[count : count + 2], refs[count + 2 :]
        qkv_scr, s_scr, o_scr, x_scr, sems = refs
        out_copy = pltpu.make_async_copy(qkv_scr, qkv_hbm, sems.at[4])

        @pl.when(step == 0)
        def _project():
            copies = [
                pltpu.make_async_copy(src, x_scr.at[pl.ds(n * QROWS, QROWS)], sems.at[n])
                for n, src in enumerate(x_refs)
            ]
            for copy in copies:
                copy.start()
            for copy in copies:
                copy.wait()
            chunk = 512

            def body(n, carry):
                rows = pl.ds(pl.multiple_of(n * chunk, chunk), chunk)
                total = dot_nn(x_scr[rows], w_ref[...]) + add_ref[...]
                qkv_scr[rows] = (total.astype(jnp.bfloat16).astype(jnp.float32) * scale_ref[...]).astype(
                    jnp.bfloat16
                )
                return carry

            lax.fori_loop(0, LENGTH // chunk, body, 0)
            out_copy.start()

        @pl.when(last)
        def _written():
            out_copy.wait()

    else:
        qkv_hbm, _ = refs[:2]
        o_refs, refs = refs[2 : 2 + count], refs[2 + count :]
        p_ref, qkv_scr, s_scr, o_scr, sems = refs

        @pl.when(step == 0)
        def _load():
            copy = pltpu.make_async_copy(qkv_hbm, qkv_scr, sems.at[0])
            copy.start()
            copy.wait()

    low, high = lane_masks(jnp.bfloat16)
    lane = lax.broadcasted_iota(jnp.int32, (1, 128), 1)
    per = QB // steps
    units = [(sub, head) for sub in range(per) for head in range(HEADS)]
    slot = place[1 + step // steps]
    keys = []
    for sub in range(per):
        local = slot * QB + (step % steps) * per + sub
        bias = key_bias(local ^ (place[0] * QB))
        rows = pl.ds(pl.multiple_of(local * BLOCK, BLOCK), BLOCK)
        queries = head_queries(
            qkv_scr[rows, KV : KV + 128], qkv_scr[rows, KV + 128 : KV + 256], low, high
        )
        for head in range(HEADS):
            n = sub * HEADS + head
            keys.append(gather_keys(table, qkv_scr, head, local))
            raw = dot_nt(queries[head], keys[n])
            s_scr[n, :, 0:128] = raw[:, 0:128]
            s_scr[n, :, 128:384] = raw[:, 128:384] + bias[:, 128:384]
            s_scr[n, :, 384:512] = raw[:, 384:512]
    tops = [jnp.max(s_scr[n], axis=1, keepdims=True) for n in range(len(units))]
    sums = []
    for n in range(len(units)):
        expo = jnp.exp(s_scr[n] - tops[n])
        s_scr[n] = expo
        sums.append(jnp.sum(expo, axis=1, keepdims=True))
    for n, (sub, head) in enumerate(units):
        p_ref[sub, head] = (s_scr[n] * (1.0 / sums[n])).astype(jnp.bfloat16)
    for sub in range(per):
        rows = slice(sub * BLOCK, (sub + 1) * BLOCK)
        outs = [dot_nn(p_ref[sub, head], keys[sub * HEADS + head]) for head in range(HEADS)]
        o_scr[rows, 0:128] = jnp.where(lane < 64, outs[0], outs[1]).astype(jnp.bfloat16)
        o_scr[rows, 128:192] = outs[2][:, 0:64].astype(jnp.bfloat16)
    for turn, o_ref in enumerate(o_refs):

        @pl.when(step // steps == turn)
        def _out(o_ref=o_ref):
            o_ref[...] = o_scr[...]


def attend_forward(slots, rank, table, rows=None, weights=None, qkv=None, probs=None):
    steps = 4
    per = QB // steps
    count = len(slots)
    project = rows is not None
    any_spec = pl.BlockSpec(memory_space=pl.ANY)
    place = jnp.stack([rank.astype(jnp.int32)] + [jnp.int32(slot) for slot in slots])
    operands = [table, place] + ([*rows, *weights] if project else [qkv, probs])
    in_specs = [any_spec] * (4 if project else 2)
    if project:
        in_specs += [pl.BlockSpec(each.shape, lambda g, *_: (0, 0)) for each in weights]
    qkv_out = [jax.ShapeDtypeStruct((LENGTH, QKV), jnp.bfloat16)] * project
    extra = [pltpu.VMEM((LENGTH, weights[0].shape[0]), jnp.bfloat16)] if project else []
    return pl.pallas_call(
        functools.partial(forward_kernel, steps, count, project),
        grid_spec=pltpu.PrefetchScalarGridSpec(
            num_scalar_prefetch=2,
            grid=(count * steps,),
            in_specs=in_specs,
            out_specs=[
                pl.BlockSpec(
                    (per * BLOCK, 192),
                    lambda g, *_, turn=turn: (jnp.clip(g - turn * steps, 0, steps - 1), 0),
                )
                for turn in range(count)
            ]
            + [
                pl.BlockSpec(
                    (per, HEADS, BLOCK, KEYS),
                    lambda g, t, pos: (pos[1 + g // steps] * steps + g % steps, 0, 0, 0),
                ),
            ]
            + [any_spec] * project,
            scratch_shapes=[
                pltpu.VMEM((LENGTH, QKV), jnp.bfloat16),
                pltpu.VMEM((per * HEADS, BLOCK, KEYS), jnp.float32),
                pltpu.VMEM((per * BLOCK, 192), jnp.bfloat16),
            ]
            + extra
            + [pltpu.SemaphoreType.DMA((5,))],
        ),
        out_shape=[jax.ShapeDtypeStruct((QROWS, 192), jnp.bfloat16)] * count
        + [jax.ShapeDtypeStruct((NB, HEADS, BLOCK, KEYS), jnp.bfloat16)]
        + qkv_out,
        input_output_aliases={} if project else {3: count},
        compiler_params=pltpu.CompilerParams(
            dimension_semantics=("arbitrary",), vmem_limit_bytes=vmem_limit
        ),
        name="attend_forward",
    )(*operands)


def backward_kernel(
    steps,
    table,
    p_ref,
    qkv_hbm,
    do0,
    do1,
    do2,
    do3,
    o0,
    o1,
    o2,
    o3,
    w_ref,
    da_hbm,
    out_hbm,
    base_hbm,
    near_hbm,
    side_hbm,
    far_hbm,
    sum_ref,
    qkv_scr,
    do_scr,
    o_scr,
    acc,
    st_scr,
    out_ref,
    da_scr,
    share_scr,
    sems,
):
    step = pl.program_id(0)

    @pl.when(step == 0)
    def _load():
        copies = [pltpu.make_async_copy(qkv_hbm, qkv_scr, sems.at[0])] + [
            pltpu.make_async_copy(src, do_scr.at[pl.ds(n * QROWS, QROWS)], sems.at[4 + n])
            for n, src in enumerate((do0, do1, do2, do3))
        ]
        copies += [
            pltpu.make_async_copy(src, o_scr.at[pl.ds(n * QROWS, QROWS)], sems.at[9 + n])
            for n, src in enumerate((o0, o1, o2, o3))
        ]
        copies.append(pltpu.make_async_copy(da_hbm, da_scr, sems.at[8]))
        for copy in copies:
            copy.start()
        acc[...] = jnp.zeros_like(acc)
        for copy in copies:
            copy.wait()

    low, high = lane_masks(jnp.bfloat16)
    lane = lax.broadcasted_iota(jnp.int32, (1, 128), 1)
    per = NB // steps
    units = [(sub, head) for sub in range(per) for head in range(HEADS)]
    keys, right, wide_low, wide_high = [], [], low.astype(jnp.float32), high.astype(jnp.float32)
    for sub in range(per):
        local = step * per + sub
        rows = pl.ds(pl.multiple_of(local * BLOCK, BLOCK), BLOCK)
        queries = head_queries(
            qkv_scr[rows, KV : KV + 128], qkv_scr[rows, KV + 128 : KV + 256], low, high
        )
        g_first = do_scr[rows, 0:128]
        g_second = do_scr[rows, 128:192]
        first = g_first.astype(jnp.float32) * o_scr[rows, 0:128].astype(jnp.float32)
        second = g_second.astype(jnp.float32) * o_scr[rows, 128:192].astype(jnp.float32)
        totals = (
            jnp.sum(first * wide_low, axis=1, keepdims=True),
            jnp.sum(first * wide_high, axis=1, keepdims=True),
            jnp.sum(second, axis=1, keepdims=True),
        )
        grads = (
            g_first * low,
            g_first * high,
            jnp.concatenate([g_second, jnp.zeros_like(g_second)], axis=1),
        )
        for head in range(HEADS):
            n = sub * HEADS + head
            keys.append(gather_keys(table, qkv_scr, head, local))
            right.append(jnp.concatenate([queries[head], grads[head]], axis=0))
            probs = p_ref[sub, head]
            slopes = probs.astype(jnp.float32) * (dot_nt(grads[head], keys[n]) - totals[head])
            st_scr[n, 0:BLOCK] = slopes.astype(jnp.bfloat16)
            st_scr[n, BLOCK:128] = probs
    for sub in range(per):
        local = step * per + sub
        rows = pl.ds(pl.multiple_of(local * BLOCK, BLOCK), BLOCK)
        backs = [
            dot_nn(st_scr[sub * HEADS + head, 0:BLOCK], keys[sub * HEADS + head]) * 0.125
            for head in range(HEADS)
        ]
        out_ref[rows, KV : KV + 128] = jnp.where(lane < 64, backs[1], backs[0]).astype(jnp.bfloat16)
        out_ref[rows, KV + 128 : KV + 256] = jnp.where(lane < 64, 0.0, backs[2]).astype(
            jnp.bfloat16
        )
    for n, (sub, head) in enumerate(units):
        local = step * per + sub
        spread = dot_tn(st_scr[n], right[n])
        for entry in range(8):
            spot = table[(head * NB + local) * 8 + entry]
            where = pl.ds(pl.multiple_of(spot * BLOCK, BLOCK), BLOCK)
            acc[where, head * 128 : head * 128 + 128] += spread[
                entry * BLOCK : (entry + 1) * BLOCK
            ]

    @pl.when(step == steps - 1)
    def _store():
        out_ref[:, 0:KV] = acc[...].astype(jnp.bfloat16)
        total = jnp.zeros((8, QKV), jnp.float32)
        for row in range(0, LENGTH, 128):
            total = total + fold_rows(out_ref[row : row + 128].astype(jnp.float32))
        sum_ref[...] = total
        done = [pltpu.make_async_copy(out_ref, out_hbm, sems.at[0])]
        done[0].start()
        chunk = 512

        def share(n, carry):
            source = (3 - n // (QROWS // chunk)) * QROWS + (n % (QROWS // chunk)) * chunk
            rows = pl.ds(pl.multiple_of(source, chunk), chunk)
            place = pl.ds(pl.multiple_of(n * chunk, chunk), chunk)
            share_scr[place] = dot_nt(out_ref[rows], w_ref[...]).astype(jnp.bfloat16)
            return carry

        lax.fori_loop(0, 3 * QROWS // chunk, share, 0)
        for n, share_hbm in enumerate((far_hbm, side_hbm, near_hbm)):
            rows = pl.ds(n * QROWS, QROWS)
            done.append(pltpu.make_async_copy(share_scr.at[rows], share_hbm, sems.at[1 + n]))
            done[-1].start()

        def base(n, carry):
            rows = pl.ds(pl.multiple_of(n * chunk, chunk), chunk)
            da_scr[rows] += dot_nt(out_ref[rows], w_ref[...])
            return carry

        lax.fori_loop(0, QROWS // chunk, base, 0)
        done.append(pltpu.make_async_copy(da_scr, base_hbm, sems.at[4]))
        done[-1].start()
        for copy in done:
            copy.wait()


def attend_backward(table, probs, qkv, grads, outs, w_qkv, da):
    steps = 16
    per = NB // steps
    width = w_qkv.shape[0]
    any_spec = pl.BlockSpec(memory_space=pl.ANY)
    share = jax.ShapeDtypeStruct((QROWS, width), jnp.bfloat16)
    return pl.pallas_call(
        functools.partial(backward_kernel, steps),
        grid_spec=pltpu.PrefetchScalarGridSpec(
            num_scalar_prefetch=1,
            grid=(steps,),
            in_specs=[pl.BlockSpec((per, HEADS, BLOCK, KEYS), lambda g, *_: (g, 0, 0, 0))]
            + [any_spec] * 9
            + [pl.BlockSpec((width, QKV), lambda g, *_: (0, 0)), any_spec],
            out_specs=[any_spec] * 5 + [pl.BlockSpec((8, QKV), lambda g, *_: (0, 0))],
            scratch_shapes=[
                pltpu.VMEM((LENGTH, QKV), jnp.bfloat16),
                pltpu.VMEM((LENGTH, 192), jnp.bfloat16),
                pltpu.VMEM((LENGTH, 192), jnp.bfloat16),
                pltpu.VMEM((LENGTH, KV), jnp.float32),
                pltpu.VMEM((per * HEADS, 128, KEYS), jnp.bfloat16),
                pltpu.VMEM((LENGTH, QKV), jnp.bfloat16),
                pltpu.VMEM((QROWS, width), jnp.float32),
                pltpu.VMEM((3 * QROWS, width), jnp.bfloat16),
                pltpu.SemaphoreType.DMA((13,)),
            ],
        ),
        out_shape=[
            jax.ShapeDtypeStruct((LENGTH, QKV), jnp.bfloat16),
            jax.ShapeDtypeStruct((QROWS, width), jnp.float32),
            share,
            share,
            share,
            jax.ShapeDtypeStruct((8, QKV), jnp.float32),
        ],
        compiler_params=pltpu.CompilerParams(
            dimension_semantics=("arbitrary",), vmem_limit_bytes=vmem_limit
        ),
        cost_estimate=pl.CostEstimate(
            flops=40 * 10**9, transcendentals=0, bytes_accessed=25 * 10**6
        ),
        name="attend_backward",
    )(table, probs, qkv, *grads, *outs, w_qkv, da)


def head_weight_kernel(x0, x1, x2, x3, grad_ref, out_ref, x_scr, acc, sems):
    slot = pl.program_id(0)

    @pl.when(slot == 0)
    def _load():
        copies = [
            pltpu.make_async_copy(src, x_scr.at[pl.ds(n * QROWS, QROWS)], sems.at[n])
            for n, src in enumerate((x0, x1, x2, x3))
        ]
        for copy in copies:
            copy.start()
        acc[...] = jnp.zeros_like(acc)
        for copy in copies:
            copy.wait()

    rows = pl.ds(pl.multiple_of(slot * QROWS, QROWS), QROWS)
    acc[...] += dot_tn(x_scr[rows], grad_ref[...])

    @pl.when(slot == pl.num_programs(0) - 1)
    def _store():
        out_ref[:, 0 : KV + 128] = acc[:, 0 : KV + 128].astype(jnp.bfloat16)
        out_ref[:, KV + 128 : KV + 192] = acc[:, KV + 192 : KV + 256].astype(jnp.bfloat16)


def head_weight_block(rows, grad_qkv):
    width = rows[0].shape[1]
    any_spec = pl.BlockSpec(memory_space=pl.ANY)
    return pl.pallas_call(
        head_weight_kernel,
        grid=(GROUP,),
        in_specs=[any_spec] * 4 + [pl.BlockSpec((QROWS, QKV), lambda g: (g, 0))],
        out_specs=pl.BlockSpec((width, QKV - 64), lambda g: (0, 0)),
        scratch_shapes=[
            pltpu.VMEM((LENGTH, width), jnp.bfloat16),
            pltpu.VMEM((width, QKV), jnp.float32),
            pltpu.SemaphoreType.DMA((4,)),
        ],
        out_shape=jax.ShapeDtypeStruct((width, QKV - 64), jnp.bfloat16),
        compiler_params=pltpu.CompilerParams(
            dimension_semantics=("arbitrary",), vmem_limit_bytes=vmem_limit
        ),
        cost_estimate=pl.CostEstimate(
            flops=8 * 10**9, transcendentals=0, bytes_accessed=12 * 10**6
        ),
        name="head_weight_block",
    )(*rows, grad_qkv)


def row_mean(values):
    return jnp.mean(values, axis=1, keepdims=True)


def fold_rows(values):
    total = values[0:8]
    for row in range(8, values.shape[0], 8):
        total = total + values[row : row + 8]
    return total


def token_kernel(
    tile,
    width,
    hidden,
    rank_ref,
    o0,
    o1,
    o2,
    o3,
    x_ref,
    cot_ref,
    vec_ref,
    up_bias_ref,
    weights,
    out_ref,
    n1_ref,
    g_ref,
    du_ref,
    dfr_ref,
    dar_ref,
    da_ref,
    do0,
    do1,
    do2,
    do3,
    total_ref,
    w_scr,
    acc,
    u_scr,
    slope_scr,
    xhat_scr,
    m1_scr,
    sum_ref,
    up_sum_ref,
    sem,
):
    step = pl.program_id(0)
    parts = GROUP
    small = 32
    cols = 256
    spans = ((2 * hidden, weights.shape[1] - 2 * hidden), (0, hidden), (hidden, hidden))
    arrivals = [
        pltpu.make_async_copy(
            weights.at[:, pl.ds(*span)], w_scr.at[:, pl.ds(*span)], sem.at[n]
        )
        for n, span in enumerate(spans)
    ]

    @pl.when(step == 0)
    def _load():
        for copy in arrivals:
            copy.start()
        sum_ref[...] = jnp.zeros_like(sum_ref)
        up_sum_ref[...] = jnp.zeros_like(up_sum_ref)
        arrivals[0].wait()

    def vector(n):
        return vec_ref[n : n + 1, :]

    def part_rows(n):
        return slice(n * width, (n + 1) * width)

    def out_weight(n):
        place = pl.multiple_of((rank_ref[0] ^ n) * width, width)
        return w_scr[pl.ds(place, width), 2 * hidden :]

    total = dot_nt(o0[...], out_weight(0))
    for n, piece in ((1, o1), (2, o2), (3, o3)):
        total = total + dot_nt(piece[...], out_weight(n))
    acc[...] = total
    first_scale = []
    for row in range(0, tile, small):
        rows = slice(row, row + small)
        resid = acc[rows] + x_ref[rows].astype(jnp.float32) + vector(0)
        center = resid - row_mean(resid)
        scale = lax.rsqrt(row_mean(center * center) + epsilon)
        xhat = center * scale
        normed = xhat * vector(1) + vector(2)
        first_scale.append(scale)
        xhat_scr[rows] = xhat
        m1_scr[rows] = normed
        n1_ref[rows] = normed.astype(jnp.bfloat16)

    @pl.when(step == 0)
    def _arrived():
        arrivals[1].wait()
        arrivals[2].wait()

    for part in range(parts):
        u_scr[part % 2] = dot_nn(n1_ref[...], w_scr[part_rows(part), 0:hidden])
        for row in range(0, tile, small):
            rows = slice(row, row + small)
            for col in range(0, hidden, cols):
                place = slice(col, col + cols)
                wide = slice(part * hidden + col, part * hidden + col + cols)
                pre = u_scr[part % 2, rows, place] + up_bias_ref[:, wide]
                cdf = 0.5 + 0.5 * lax.erf(pre * 0.7071067811865476)
                g_ref[rows, wide] = (pre * cdf).astype(jnp.bfloat16)
                slope_scr[rows, wide] = (
                    cdf + pre * jnp.exp(-0.5 * pre * pre) * 0.3989422804014327
                )
        lift = dot_nt(
            g_ref[:, part * hidden : (part + 1) * hidden],
            w_scr[part_rows(part), hidden : 2 * hidden],
        )
        if part == 0:
            acc[...] = lift
        else:
            acc[...] += lift
    sums = [jnp.zeros((8, width), jnp.float32) for _ in range(6)]
    for row in range(0, tile, small):
        rows = slice(row, row + small)
        second = m1_scr[rows] + acc[rows] + vector(3)
        center = second - row_mean(second)
        scale = lax.rsqrt(row_mean(center * center) + epsilon)
        xhat = center * scale
        out_ref[rows] = (xhat * vector(4) + vector(5)).astype(jnp.bfloat16)
        top = cot_ref[rows].astype(jnp.float32)
        gained = top * vector(4)
        down = scale * (gained - row_mean(gained) - xhat * row_mean(gained * xhat))
        sums[0] = sums[0] + fold_rows(top * xhat)
        sums[1] = sums[1] + fold_rows(top)
        sums[2] = sums[2] + fold_rows(down)
        m1_scr[rows] = down
        dfr_ref[rows] = down.astype(jnp.bfloat16)
    for part in range(parts):
        whole = slice(part * hidden, (part + 1) * hidden)
        u_scr[part % 2] = dot_nn(dfr_ref[...], w_scr[part_rows(part), hidden : 2 * hidden])
        for col in range(0, hidden, cols):
            place = slice(col, col + cols)
            wide = slice(part * hidden + col, part * hidden + col + cols)
            tally = jnp.zeros((8, cols), jnp.float32)
            for row in range(0, tile, small):
                rows = slice(row, row + small)
                low = (u_scr[part % 2, rows, place] * slope_scr[rows, wide]).astype(jnp.bfloat16)
                du_ref[rows, wide] = low
                tally = tally + fold_rows(low.astype(jnp.float32))
            up_sum_ref[:, wide] += tally
        lift = dot_nt(du_ref[:, whole], w_scr[part_rows(part), 0:hidden])
        if part == 0:
            acc[...] = lift
        else:
            acc[...] += lift
    for n, row in enumerate(range(0, tile, small)):
        rows = slice(row, row + small)
        back = m1_scr[rows] + acc[rows]
        xhat = xhat_scr[rows]
        sums[3] = sums[3] + fold_rows(back * xhat)
        sums[4] = sums[4] + fold_rows(back)
        gained = back * vector(1)
        down = first_scale[n] * (gained - row_mean(gained) - xhat * row_mean(gained * xhat))
        sums[5] = sums[5] + fold_rows(down)
        da_ref[rows] = down
        dar_ref[rows] = down.astype(jnp.bfloat16)
    for n in range(6):
        sum_ref[n] += sums[n]
    for n, do_ref in enumerate((do0, do1, do2, do3)):
        do_ref[...] = dot_nn(dar_ref[...], out_weight(n)).astype(jnp.bfloat16)

    @pl.when(step == pl.num_programs(0) - 1)
    def _totals():
        for n in range(6):
            total_ref[:, n * width : (n + 1) * width] = jnp.sum(
                sum_ref[n], axis=0, keepdims=True
            )
        total_ref[:, 6 * width :] = jnp.sum(up_sum_ref[...], axis=0, keepdims=True)


def token_block(rank, outs, own, cot, vectors, up_bias, weights):
    count, width = own.shape
    total_hidden = up_bias.shape[1]
    hidden = total_hidden // GROUP
    tile = 256

    def rows_of(columns):
        return pl.BlockSpec((tile, columns), lambda g, *_: (g, 0))

    def whole(shape):
        return pl.BlockSpec(shape, lambda g, *_: (0,) * len(shape))

    low = jnp.bfloat16
    head = outs[0].shape[1]
    return pl.pallas_call(
        functools.partial(token_kernel, tile, width, hidden),
        grid_spec=pltpu.PrefetchScalarGridSpec(
            num_scalar_prefetch=1,
            grid=(count // tile,),
            in_specs=[rows_of(head)] * 4
            + [rows_of(width)] * 2
            + [whole(vectors.shape), whole(up_bias.shape)] + [pl.BlockSpec(memory_space=pl.ANY)],
            out_specs=[
                rows_of(width),
                rows_of(width),
                rows_of(total_hidden),
                rows_of(total_hidden),
                rows_of(width),
                rows_of(width),
                rows_of(width),
                rows_of(head),
                rows_of(head),
                rows_of(head),
                rows_of(head),
                whole((1, 6 * width + total_hidden)),
            ],
            scratch_shapes=[
                pltpu.VMEM(weights.shape, low),
                pltpu.VMEM((tile, width), jnp.float32),
                pltpu.VMEM((2, tile, hidden), jnp.float32),
                pltpu.VMEM((tile, total_hidden), jnp.float32),
                pltpu.VMEM((tile, width), jnp.float32),
                pltpu.VMEM((tile, width), jnp.float32),
                pltpu.VMEM((6, 8, width), jnp.float32),
                pltpu.VMEM((8, total_hidden), jnp.float32),
                pltpu.SemaphoreType.DMA((3,)),
            ],
        ),
        out_shape=[
            jax.ShapeDtypeStruct((count, width), low),
            jax.ShapeDtypeStruct((count, width), low),
            jax.ShapeDtypeStruct((count, total_hidden), low),
            jax.ShapeDtypeStruct((count, total_hidden), low),
            jax.ShapeDtypeStruct((count, width), low),
            jax.ShapeDtypeStruct((count, width), low),
            jax.ShapeDtypeStruct((count, width), jnp.float32),
            jax.ShapeDtypeStruct((count, head), low),
            jax.ShapeDtypeStruct((count, head), low),
            jax.ShapeDtypeStruct((count, head), low),
            jax.ShapeDtypeStruct((count, head), low),
            jax.ShapeDtypeStruct((1, 6 * width + total_hidden), jnp.float32),
        ],
        compiler_params=pltpu.CompilerParams(
            dimension_semantics=("arbitrary",), vmem_limit_bytes=vmem_limit
        ),
        cost_estimate=pl.CostEstimate(
            flops=46 * 10**9, transcendentals=0, bytes_accessed=40 * 10**6
        ),
        name="token_block",
    )(rank.astype(jnp.int32).reshape(1), *outs, own, cot, vectors, up_bias, weights)


def weight_kernel(width, hidden, rank_ref, n1, dfr, dar, g, du, o0, o1, o2, o3, out_ref, n1_t, dfr_t, dar_t):
    part = pl.program_id(0)

    @pl.when(part == 0)
    def _turn():
        n1_t[...] = n1[...].T
        dfr_t[...] = dfr[...].T
        dar_t[...] = dar[...].T

    chunk = 256

    def product(n, carry):
        rows = pl.ds(pl.multiple_of(n * chunk, chunk), chunk)
        out_ref[rows, 0:hidden] = dot_nn(n1_t[rows], du[...]).astype(jnp.bfloat16)
        out_ref[rows, hidden : 2 * hidden] = dot_nn(dfr_t[rows], g[...]).astype(jnp.bfloat16)
        return carry

    lax.fori_loop(0, width // chunk, product, 0)
    for n, piece in enumerate((o0, o1, o2, o3)):

        @pl.when(part == rank_ref[0] ^ n)
        def _out(piece=piece):
            out_ref[:, 2 * hidden :] = dot_nn(dar_t[...], piece[...]).astype(jnp.bfloat16)


def weight_block(rank, n1, dfr, dar, g, du, outs):
    count, width = n1.shape
    hidden = g.shape[1] // GROUP
    head = outs[0].shape[1]
    columns = 2 * hidden + head
    low = jnp.bfloat16

    def whole(shape):
        return pl.BlockSpec(shape, lambda g, *_: (0,) * len(shape))

    return pl.pallas_call(
        functools.partial(weight_kernel, width, hidden),
        grid_spec=pltpu.PrefetchScalarGridSpec(
            num_scalar_prefetch=1,
            grid=(GROUP,),
            in_specs=[whole((count, width))] * 3
            + [pl.BlockSpec((count, hidden), lambda g, *_: (0, g))] * 2
            + [whole((count, head))] * 4,
            out_specs=pl.BlockSpec((width, columns), lambda g, *_: (g, 0)),
            scratch_shapes=[pltpu.VMEM((width, count), low)] * 3,
        ),
        out_shape=jax.ShapeDtypeStruct((GROUP * width, columns), low),
        compiler_params=pltpu.CompilerParams(
            dimension_semantics=("arbitrary",), vmem_limit_bytes=vmem_limit
        ),
        cost_estimate=pl.CostEstimate(
            flops=22 * 10**9, transcendentals=0, bytes_accessed=30 * 10**6
        ),
        name="weight_block",
    )(rank.astype(jnp.int32).reshape(1), n1, dfr, dar, g, du, *outs)


def pack_columns(query, key, value, axis):
    def piece(matrix, head):
        return lax.slice_in_dim(matrix, head * HD, (head + 1) * HD, axis=axis)

    return jnp.concatenate(
        [
            piece(value, 0),
            piece(key, 0),
            piece(key, 1),
            piece(value, 1),
            piece(value, 2),
            piece(key, 2),
            piece(query, 1),
            piece(query, 0),
            piece(query, 2),
        ],
        axis=axis,
    )


def insert_zero(packed, axis):
    head = lax.slice_in_dim(packed, 0, KV + 128, axis=axis)
    tail = lax.slice_in_dim(packed, KV + 128, KV + 192, axis=axis)
    return jnp.concatenate([head, jnp.zeros_like(tail), tail], axis=axis)


def drop_zero(packed, axis):
    head = lax.slice_in_dim(packed, 0, KV + 128, axis=axis)
    tail = lax.slice_in_dim(packed, KV + 192, KV + 256, axis=axis)
    return jnp.concatenate([head, tail], axis=axis)


def unpack_columns(packed, axis):
    def piece(n):
        return lax.slice_in_dim(packed, n * HD, (n + 1) * HD, axis=axis)

    query = jnp.concatenate([piece(7), piece(6), piece(8)], axis=axis)
    key = jnp.concatenate([piece(1), piece(2), piece(5)], axis=axis)
    value = jnp.concatenate([piece(0), piece(3), piece(4)], axis=axis)
    return query, key, value


def per_device(
    dp_size,
    tensor_size,
    inputs,
    cotangent,
    w_query,
    w_key,
    w_value,
    w_output,
    w_up,
    w_down,
    b_query,
    b_value,
    b_output,
    gain_attn,
    bias_attn,
    b_up,
    b_down,
    gain_mlp,
    bias_mlp,
    random_blocks,
):
    width = inputs.shape[1]
    hidden = b_up.shape[0]
    low = jnp.bfloat16
    dp_index = lax.axis_index("dp")
    tensor_index = lax.axis_index("tensor")
    core = dp_index % 2
    half = tensor_index // 2
    rank = 2 * core + tensor_index % 2
    here = core == half
    devices = [(d, t) for d in range(dp_size) for t in range(tensor_size)]
    pair_bits = [bit for bit in range(1, dp_size.bit_length() - 1)]

    def flat(d, t):
        return d * tensor_size + t

    def stays(d, t):
        return d % 2 == t // 2

    def flip(value, d_bits, t_bits, chosen=None):
        pairs = [
            (flat(d, t), flat(d ^ d_bits, t ^ t_bits))
            for d, t in devices
            if chosen is None or chosen(d, t)
        ]
        return lax.ppermute(value, both, pairs)

    def moves(d, t):
        return not stays(d, t)

    def rehome(value):
        return jnp.where(here, value, flip(value, 1, 2, moves))

    def near_of(value):
        return flip(value, 0, 1)

    def side_of(value):
        return flip(value, 1, 0)

    rest = jnp.concatenate([w_up, w_down.T, w_output.T], axis=1)
    below = jnp.concatenate(split_three(b_up))
    below = jnp.pad(below, (0, -below.shape[0] % rest.shape[1])).reshape(-1, rest.shape[1])
    rest = jnp.concatenate([rest, below], axis=0)

    packed = pack_columns(w_query, w_key, w_value, 1)
    columns = packed.shape[1]
    floats = jnp.concatenate([b_query, b_value])
    small = jnp.concatenate(split_three(floats) + [random_blocks.astype(low).reshape(-1)])
    small = jnp.pad(small, (0, -small.shape[0] % columns)).reshape(-1, columns)
    packed = jnp.concatenate([order_halves(core, packed, side_of(packed)), small], axis=0)
    packed_got = flip(packed, 0, 2, stays)

    moved = flip(inputs, 1, 2, moves)
    near_stay = flip(inputs, 0, 1, stays)
    moved, near_stay, packed_got, rest = lax.optimization_barrier(
        (moved, near_stay, packed_got, rest)
    )
    own = jnp.where(here, inputs, moved)
    near_move = flip(own, 0, 1, moves)
    own, packed_got = lax.optimization_barrier((own, packed_got))
    rest = lax.all_gather(rest, "tensor", axis=0)
    packed = jnp.where(here, packed, packed_got)
    small = packed[2 * w_query.shape[0] :].reshape(-1)
    packed = packed[: 2 * w_query.shape[0]]
    for bit in pair_bits:
        packed = order_halves((dp_index >> bit) % 2, packed, flip(packed, 1 << bit, 0))
    w_qkv = insert_zero(packed, 1)
    count = floats.shape[0]
    mine = sum(small[n * count : (n + 1) * count].astype(jnp.float32) for n in range(3))
    my_random = small[3 * count : 3 * count + random_blocks.size]
    my_random = my_random.reshape(HEADS, NB, -1).astype(jnp.int32)
    b_key = jnp.zeros_like(b_query)
    b_qkv = insert_zero(pack_columns(mine[:192], b_key, mine[192:], 0), 0)
    scale = jnp.concatenate([jnp.ones((KV,), jnp.float32), jnp.full((256,), 0.125, jnp.float32)])
    near = jnp.where(here, near_stay, near_move)
    near, own, cotangent, w_qkv, b_qkv = lax.optimization_barrier(
        (near, own, cotangent, w_qkv, b_qkv)
    )
    side, far = side_of(own), side_of(near)
    cot_moved = flip(cotangent, 1, 2, moves)
    side, far, rest = lax.optimization_barrier((side, far, rest))
    below = rest[:, w_up.shape[0] :].reshape(GROUP, -1)
    rest_all = lax.all_gather(
        rest[:, : w_up.shape[0]], "dp", axis=1, tiled=True
    ).reshape(GROUP * width, -1)
    b_up_all = sum(
        below[:, n * hidden : (n + 1) * hidden].astype(jnp.float32) for n in range(3)
    ).reshape(1, -1)
    rows = (own, near, side, far)
    grad_top = jnp.where(here, cotangent, cot_moved)
    block = jnp.arange(NB, dtype=jnp.int32)
    block = block ^ (rank * QB)
    fixed = jnp.clip(
        jnp.stack(
            [
                jnp.zeros_like(block),
                jnp.full_like(block, NB - 1),
                block - 1,
                block,
                block + 1,
            ],
            axis=-1,
        ),
        0,
        NB - 1,
    )
    local_random = jnp.take(my_random, block, axis=1)
    table = jnp.concatenate(
        [jnp.broadcast_to(fixed[None], (HEADS, NB, 5)), local_random], axis=-1
    )
    table = (table ^ (rank * QB)).reshape(-1)

    weights = (w_qkv, b_qkv[None], scale[None])
    out_near, out_far, out_side, probs, qkv = attend_forward((1, 3, 2), rank, table, rows, weights)
    out_own, probs = attend_forward((0,), rank, table, qkv=qkv, probs=probs)
    outs = (out_own, near_of(out_near), side_of(out_side), flip(out_far, 1, 1))

    vectors = jnp.stack([b_output, gain_attn, bias_attn, b_down, gain_mlp, bias_mlp])
    layer_out, n1, g, du, dfr, dar, da, *do, sums = token_block(
        rank, outs, own, grad_top, vectors, b_up_all, rest_all
    )
    grads = (do[0], near_of(do[1]), side_of(do[2]), flip(do[3], 1, 1))
    rest_grad = weight_block(rank, n1, dfr, dar, g, du, outs)
    sums = sums.reshape(-1)
    sums = sums + flip(sums, 0, 1)
    rest_grad, sums, *grads = lax.optimization_barrier((rest_grad, sums, *grads))
    rest_sum = lax.psum_scatter(
        rest_grad.reshape(GROUP, width, -1), "dp", scatter_dimension=1, tiled=True
    )
    layer_sent = flip(layer_out, 1, 2, moves)

    grad_qkv, base, to_near, to_side, to_far, bias_sum = attend_backward(
        table, probs, qkv, grads, (out_own, out_near, out_side, out_far), w_qkv, da
    )
    grad_qkv, base, to_near, to_side, to_far, bias_sum, layer_sent = lax.optimization_barrier(
        (grad_qkv, base, to_near, to_side, to_far, bias_sum, layer_sent)
    )
    side_far = side_of(to_far)
    side_own = side_of(to_side)
    bias_query, _, bias_value = unpack_columns(drop_zero(jnp.sum(bias_sum, axis=0), 0), 0)
    sums = jnp.concatenate([sums, bias_query, bias_value])
    sums = sums + flip(sums, 0, 2)
    to_near = (to_near.astype(jnp.float32) + side_far.astype(jnp.float32)).astype(low)
    to_near, sums = lax.optimization_barrier((to_near, sums))
    near_got = near_of(to_near)
    base = base + side_own.astype(jnp.float32)
    grad_late, to_near = lax.optimization_barrier((grad_qkv, to_near))
    for bit in pair_bits:
        sums = sums + flip(sums, 1 << bit, 0)
    other = side_of(sums)
    grad_late, sums = lax.optimization_barrier((grad_late, sums))
    grad_w = head_weight_block(rows, grad_late)
    rest_sum, base, grad_w = lax.optimization_barrier((rest_sum, base, grad_w))
    rest_sum = lax.psum_scatter(rest_sum, "tensor", scatter_dimension=0, tiled=False).astype(
        jnp.float32
    )
    for bit in reversed(pair_bits[2:]):
        grad_w = halve(flip, (dp_index >> bit) % 2, grad_w, 1 << bit, 0)
    place = (dp_index // 2) % 4
    rows_each = grad_w.shape[0] // 4
    total = lax.dynamic_slice_in_dim(grad_w, place * rows_each, rows_each, 0).astype(jnp.float32)
    for n in (3, 1, 2):
        send = lax.dynamic_slice_in_dim(grad_w, (place ^ n) * rows_each, rows_each, 0)
        total = total + flip(send, 2 * n, 0).astype(jnp.float32)
    grad_w = total.astype(low)
    near_got, grad_w, base, sums, other, layer_sent = lax.optimization_barrier(
        (near_got, grad_w, base, sums, other, layer_sent)
    )
    grad_own = (base + near_got.astype(jnp.float32)).astype(low)
    grad_own, grad_w, layer_sent = lax.optimization_barrier((grad_own, grad_w, layer_sent))
    grad_moved = flip(grad_own, 1, 2, moves)

    grad_got = flip(grad_w, 0, 2, moves)
    grad_w = grad_w.astype(jnp.float32) + grad_got.astype(jnp.float32)
    rows_each = grad_w.shape[0] // 2
    grad_w = grad_w.astype(low)
    keep = lax.dynamic_slice_in_dim(grad_w, core * rows_each, rows_each, 0)
    send = lax.dynamic_slice_in_dim(grad_w, (1 - core) * rows_each, rows_each, 0)
    side_got = side_of(send)
    grad_moved, side_got, rest_sum = lax.optimization_barrier((grad_moved, side_got, rest_sum))
    shard = jnp.where(here, keep, side_got).astype(jnp.float32)
    shard_query, shard_key, shard_value = unpack_columns(shard, 1)
    shard_up = rest_sum[:, :hidden]
    shard_down = rest_sum[:, hidden : 2 * hidden].T
    shard_output = rest_sum[:, 2 * hidden :].T
    layer_out = jnp.where(here, layer_out, layer_sent)
    grad_input = jnp.where(here, grad_own, grad_moved)

    count = 6 * width + GROUP * hidden
    bias_pair = jnp.where(here, sums[count:], other[count:])
    sums = sums + other
    top = sums[: 6 * width].reshape(6, width)
    grad_b_up = lax.dynamic_slice_in_dim(sums, 6 * width + tensor_index * hidden, hidden, 0)
    return (
        layer_out,
        grad_input,
        shard_query,
        shard_key,
        shard_value,
        shard_output,
        shard_up,
        shard_down,
        bias_pair[:192],
        bias_pair[192:],
        top[5],
        top[3],
        top[4],
        grad_b_up,
        top[2],
        top[0],
        top[1],
    )


def order_halves(bit, own, other):
    return jnp.where(
        bit == 0,
        jnp.concatenate([own, other], axis=0),
        jnp.concatenate([other, own], axis=0),
    )


def split_three(values):
    parts = []
    for _ in range(3):
        part = lax.reduce_precision(values, 8, 7)
        parts.append(part.astype(jnp.bfloat16))
        values = values - part
    return parts


def halve(flip, bit, value, d_bits, t_bits):
    rows = value.shape[0] // 2
    keep = lax.dynamic_slice_in_dim(value, bit * rows, rows, 0)
    send = lax.dynamic_slice_in_dim(value, (1 - bit) * rows, rows, 0)
    got = flip(send, d_bits, t_bits)
    return (keep.astype(jnp.float32) + got.astype(jnp.float32)).astype(value.dtype)


def solution(mesh):
    in_specs = (
        P(("dp", "tensor"), None),
        P(("dp", "tensor"), None),
        P("dp", "tensor"),
        P("dp", "tensor"),
        P("dp", "tensor"),
        P("tensor", "dp"),
        P("dp", "tensor"),
        P("tensor", "dp"),
        P("tensor"),
        P("tensor"),
        P(),
        P(),
        P(),
        P("tensor"),
        P(),
        P(),
        P(),
        P("tensor", None, None),
    )
    out_specs = (
        P(("dp", "tensor"), None),
        P(("dp", "tensor"), None),
        P("dp", "tensor"),
        P("dp", "tensor"),
        P("dp", "tensor"),
        P("tensor", "dp"),
        P("dp", "tensor"),
        P("tensor", "dp"),
        P("tensor"),
        P("tensor"),
        P(),
        P(),
        P(),
        P("tensor"),
        P(),
        P(),
        P(),
    )
    body = functools.partial(per_device, mesh.shape["dp"], mesh.shape["tensor"])
    return jax.shard_map(body, mesh=mesh, in_specs=in_specs, out_specs=out_specs, check_vma=False)
```

```python
import functools

import jax
import jax.numpy as jnp
from jax import lax
from jax.experimental import pallas as pl
from jax.experimental.pallas import tpu as pltpu
from jax.sharding import PartitionSpec as P

HD = 64
BLOCK = 64
LENGTH = 4096
NB = LENGTH // BLOCK
GROUP = 4
QROWS = LENGTH // GROUP
QB = QROWS // BLOCK
HEADS = 3
KEYS = 8 * BLOCK
KV = 128 * HEADS
QKV = KV + 256

negative = -1e30
epsilon = 1e-05
both = ("dp", "tensor")
vmem_limit = 56 * 1024 * 1024


def dot_nn(left, right):
    return jnp.dot(left, right, preferred_element_type=jnp.float32)


def dot_tn(left, right):
    return lax.dot_general(
        left, right, (((0,), (0,)), ((), ())), preferred_element_type=jnp.float32
    )


def dot_nt(left, right):
    return lax.dot_general(
        left, right, (((1,), (1,)), ((), ())), preferred_element_type=jnp.float32
    )


def lane_masks(dtype):
    lane = lax.broadcasted_iota(jnp.int32, (1, 128), 1)
    low = (lane < 64).astype(jnp.float32).astype(dtype)
    high = (lane >= 64).astype(jnp.float32).astype(dtype)
    return low, high


def key_bias(block):
    lane = lax.broadcasted_iota(jnp.int32, (1, KEYS), 1)
    entry = lane // BLOCK
    key = jnp.where(entry == 2, block - 1, jnp.where(entry == 3, block, block + 1))
    window = (entry >= 2) & (entry <= 4)
    off = window & ((key < 1) | (key > NB - 2))
    return jnp.where(off, negative, 0.0).astype(jnp.float32)


def gather_keys(table, source, head, block):
    rows = []
    for entry in range(8):
        place = table[(head * NB + block) * 8 + entry]
        rows.append(source[pl.ds(pl.multiple_of(place * BLOCK, BLOCK), BLOCK), head * 128 : head * 128 + 128])
    return jnp.concatenate(rows, axis=0)


def head_queries(first, second, low, high):
    return (first * high, first * low, second)


def forward_kernel(steps, count, project, table, place, *refs):
    step = pl.program_id(0)
    last = step == pl.num_programs(0) - 1
    if project:
        x_refs, (w_ref, add_ref, scale_ref), refs = refs[:4], refs[4:7], refs[7:]
        o_refs, (p_ref, qkv_hbm), refs = refs[:count], refs[count : count + 2], refs[count + 2 :]
        qkv_scr, s_scr, o_scr, x_scr, sems = refs
        out_copy = pltpu.make_async_copy(qkv_scr, qkv_hbm, sems.at[4])

        @pl.when(step == 0)
        def _project():
            copies = [
                pltpu.make_async_copy(src, x_scr.at[pl.ds(n * QROWS, QROWS)], sems.at[n])
                for n, src in enumerate(x_refs)
            ]
            for copy in copies:
                copy.start()
            for copy in copies:
                copy.wait()
            chunk = 512

            def body(n, carry):
                rows = pl.ds(pl.multiple_of(n * chunk, chunk), chunk)
                total = dot_nn(x_scr[rows], w_ref[...]) + add_ref[...]
                qkv_scr[rows] = (total.astype(jnp.bfloat16).astype(jnp.float32) * scale_ref[...]).astype(
                    jnp.bfloat16
                )
                return carry

            lax.fori_loop(0, LENGTH // chunk, body, 0)
            out_copy.start()

        @pl.when(last)
        def _written():
            out_copy.wait()

    else:
        qkv_hbm, _ = refs[:2]
        o_refs, refs = refs[2 : 2 + count], refs[2 + count :]
        p_ref, qkv_scr, s_scr, o_scr, sems = refs

        @pl.when(step == 0)
        def _load():
            copy = pltpu.make_async_copy(qkv_hbm, qkv_scr, sems.at[0])
            copy.start()
            copy.wait()

    low, high = lane_masks(jnp.bfloat16)
    lane = lax.broadcasted_iota(jnp.int32, (1, 128), 1)
    per = QB // steps
    units = [(sub, head) for sub in range(per) for head in range(HEADS)]
    slot = place[1 + step // steps]
    keys = []
    for sub in range(per):
        local = slot * QB + (step % steps) * per + sub
        bias = key_bias(local ^ (place[0] * QB))
        rows = pl.ds(pl.multiple_of(local * BLOCK, BLOCK), BLOCK)
        queries = head_queries(
            qkv_scr[rows, KV : KV + 128], qkv_scr[rows, KV + 128 : KV + 256], low, high
        )
        for head in range(HEADS):
            n = sub * HEADS + head
            keys.append(gather_keys(table, qkv_scr, head, local))
            raw = dot_nt(queries[head], keys[n])
            s_scr[n, :, 0:128] = raw[:, 0:128]
            s_scr[n, :, 128:384] = raw[:, 128:384] + bias[:, 128:384]
            s_scr[n, :, 384:512] = raw[:, 384:512]
    tops = [jnp.max(s_scr[n], axis=1, keepdims=True) for n in range(len(units))]
    sums = []
    for n in range(len(units)):
        expo = jnp.exp(s_scr[n] - tops[n])
        s_scr[n] = expo
        sums.append(jnp.sum(expo, axis=1, keepdims=True))
    for n, (sub, head) in enumerate(units):
        p_ref[sub, head] = (s_scr[n] * (1.0 / sums[n])).astype(jnp.bfloat16)
    for sub in range(per):
        rows = slice(sub * BLOCK, (sub + 1) * BLOCK)
        outs = [dot_nn(p_ref[sub, head], keys[sub * HEADS + head]) for head in range(HEADS)]
        o_scr[rows, 0:128] = jnp.where(lane < 64, outs[0], outs[1]).astype(jnp.bfloat16)
        o_scr[rows, 128:192] = outs[2][:, 0:64].astype(jnp.bfloat16)
    for turn, o_ref in enumerate(o_refs):

        @pl.when(step // steps == turn)
        def _out(o_ref=o_ref):
            o_ref[...] = o_scr[...]


def attend_forward(slots, rank, table, rows=None, weights=None, qkv=None, probs=None):
    steps = 4
    per = QB // steps
    count = len(slots)
    project = rows is not None
    any_spec = pl.BlockSpec(memory_space=pl.ANY)
    place = jnp.stack([rank.astype(jnp.int32)] + [jnp.int32(slot) for slot in slots])
    operands = [table, place] + ([*rows, *weights] if project else [qkv, probs])
    in_specs = [any_spec] * (4 if project else 2)
    if project:
        in_specs += [pl.BlockSpec(each.shape, lambda g, *_: (0, 0)) for each in weights]
    qkv_out = [jax.ShapeDtypeStruct((LENGTH, QKV), jnp.bfloat16)] * project
    extra = [pltpu.VMEM((LENGTH, weights[0].shape[0]), jnp.bfloat16)] if project else []
    return pl.pallas_call(
        functools.partial(forward_kernel, steps, count, project),
        grid_spec=pltpu.PrefetchScalarGridSpec(
            num_scalar_prefetch=2,
            grid=(count * steps,),
            in_specs=in_specs,
            out_specs=[
                pl.BlockSpec(
                    (per * BLOCK, 192),
                    lambda g, *_, turn=turn: (jnp.clip(g - turn * steps, 0, steps - 1), 0),
                )
                for turn in range(count)
            ]
            + [
                pl.BlockSpec(
                    (per, HEADS, BLOCK, KEYS),
                    lambda g, t, pos: (pos[1 + g // steps] * steps + g % steps, 0, 0, 0),
                ),
            ]
            + [any_spec] * project,
            scratch_shapes=[
                pltpu.VMEM((LENGTH, QKV), jnp.bfloat16),
                pltpu.VMEM((per * HEADS, BLOCK, KEYS), jnp.float32),
                pltpu.VMEM((per * BLOCK, 192), jnp.bfloat16),
            ]
            + extra
            + [pltpu.SemaphoreType.DMA((5,))],
        ),
        out_shape=[jax.ShapeDtypeStruct((QROWS, 192), jnp.bfloat16)] * count
        + [jax.ShapeDtypeStruct((NB, HEADS, BLOCK, KEYS), jnp.bfloat16)]
        + qkv_out,
        input_output_aliases={} if project else {3: count},
        compiler_params=pltpu.CompilerParams(
            dimension_semantics=("arbitrary",), vmem_limit_bytes=vmem_limit
        ),
        name="attend_forward",
    )(*operands)


def backward_kernel(
    steps,
    table,
    p_ref,
    qkv_hbm,
    do0,
    do1,
    do2,
    do3,
    o0,
    o1,
    o2,
    o3,
    w_ref,
    da_hbm,
    out_hbm,
    base_hbm,
    near_hbm,
    side_hbm,
    far_hbm,
    sum_ref,
    qkv_scr,
    do_scr,
    o_scr,
    acc,
    st_scr,
    out_ref,
    da_scr,
    share_scr,
    sems,
):
    step = pl.program_id(0)

    @pl.when(step == 0)
    def _load():
        copies = [pltpu.make_async_copy(qkv_hbm, qkv_scr, sems.at[0])] + [
            pltpu.make_async_copy(src, do_scr.at[pl.ds(n * QROWS, QROWS)], sems.at[4 + n])
            for n, src in enumerate((do0, do1, do2, do3))
        ]
        copies += [
            pltpu.make_async_copy(src, o_scr.at[pl.ds(n * QROWS, QROWS)], sems.at[9 + n])
            for n, src in enumerate((o0, o1, o2, o3))
        ]
        copies.append(pltpu.make_async_copy(da_hbm, da_scr, sems.at[8]))
        for copy in copies:
            copy.start()
        acc[...] = jnp.zeros_like(acc)
        for copy in copies:
            copy.wait()

    low, high = lane_masks(jnp.bfloat16)
    lane = lax.broadcasted_iota(jnp.int32, (1, 128), 1)
    per = NB // steps
    units = [(sub, head) for sub in range(per) for head in range(HEADS)]
    keys, right, wide_low, wide_high = [], [], low.astype(jnp.float32), high.astype(jnp.float32)
    for sub in range(per):
        local = step * per + sub
        rows = pl.ds(pl.multiple_of(local * BLOCK, BLOCK), BLOCK)
        queries = head_queries(
            qkv_scr[rows, KV : KV + 128], qkv_scr[rows, KV + 128 : KV + 256], low, high
        )
        g_first = do_scr[rows, 0:128]
        g_second = do_scr[rows, 128:192]
        first = g_first.astype(jnp.float32) * o_scr[rows, 0:128].astype(jnp.float32)
        second = g_second.astype(jnp.float32) * o_scr[rows, 128:192].astype(jnp.float32)
        totals = (
            jnp.sum(first * wide_low, axis=1, keepdims=True),
            jnp.sum(first * wide_high, axis=1, keepdims=True),
            jnp.sum(second, axis=1, keepdims=True),
        )
        grads = (
            g_first * low,
            g_first * high,
            jnp.concatenate([g_second, jnp.zeros_like(g_second)], axis=1),
        )
        for head in range(HEADS):
            n = sub * HEADS + head
            keys.append(gather_keys(table, qkv_scr, head, local))
            right.append(jnp.concatenate([queries[head], grads[head]], axis=0))
            probs = p_ref[sub, head]
            slopes = probs.astype(jnp.float32) * (dot_nt(grads[head], keys[n]) - totals[head])
            st_scr[n, 0:BLOCK] = slopes.astype(jnp.bfloat16)
            st_scr[n, BLOCK:128] = probs
    for sub in range(per):
        local = step * per + sub
        rows = pl.ds(pl.multiple_of(local * BLOCK, BLOCK), BLOCK)
        backs = [
            dot_nn(st_scr[sub * HEADS + head, 0:BLOCK], keys[sub * HEADS + head]) * 0.125
            for head in range(HEADS)
        ]
        out_ref[rows, KV : KV + 128] = jnp.where(lane < 64, backs[1], backs[0]).astype(jnp.bfloat16)
        out_ref[rows, KV + 128 : KV + 256] = jnp.where(lane < 64, 0.0, backs[2]).astype(
            jnp.bfloat16
        )
    for n, (sub, head) in enumerate(units):
        local = step * per + sub
        spread = dot_tn(st_scr[n], right[n])
        for entry in range(8):
            spot = table[(head * NB + local) * 8 + entry]
            where = pl.ds(pl.multiple_of(spot * BLOCK, BLOCK), BLOCK)
            acc[where, head * 128 : head * 128 + 128] += spread[
                entry * BLOCK : (entry + 1) * BLOCK
            ]

    @pl.when(step == steps - 1)
    def _store():
        out_ref[:, 0:KV] = acc[...].astype(jnp.bfloat16)
        total = jnp.zeros((8, QKV), jnp.float32)
        for row in range(0, LENGTH, 128):
            total = total + fold_rows(out_ref[row : row + 128].astype(jnp.float32))
        sum_ref[...] = total
        done = [pltpu.make_async_copy(out_ref, out_hbm, sems.at[0])]
        done[0].start()
        chunk = 512

        def share(n, carry):
            source = (3 - n // (QROWS // chunk)) * QROWS + (n % (QROWS // chunk)) * chunk
            rows = pl.ds(pl.multiple_of(source, chunk), chunk)
            place = pl.ds(pl.multiple_of(n * chunk, chunk), chunk)
            share_scr[place] = dot_nt(out_ref[rows], w_ref[...]).astype(jnp.bfloat16)
            return carry

        lax.fori_loop(0, 3 * QROWS // chunk, share, 0)
        for n, share_hbm in enumerate((far_hbm, side_hbm, near_hbm)):
            rows = pl.ds(n * QROWS, QROWS)
            done.append(pltpu.make_async_copy(share_scr.at[rows], share_hbm, sems.at[1 + n]))
            done[-1].start()

        def base(n, carry):
            rows = pl.ds(pl.multiple_of(n * chunk, chunk), chunk)
            da_scr[rows] += dot_nt(out_ref[rows], w_ref[...])
            return carry

        lax.fori_loop(0, QROWS // chunk, base, 0)
        done.append(pltpu.make_async_copy(da_scr, base_hbm, sems.at[4]))
        done[-1].start()
        for copy in done:
            copy.wait()


def attend_backward(table, probs, qkv, grads, outs, w_qkv, da):
    steps = 16
    per = NB // steps
    width = w_qkv.shape[0]
    any_spec = pl.BlockSpec(memory_space=pl.ANY)
    share = jax.ShapeDtypeStruct((QROWS, width), jnp.bfloat16)
    return pl.pallas_call(
        functools.partial(backward_kernel, steps),
        grid_spec=pltpu.PrefetchScalarGridSpec(
            num_scalar_prefetch=1,
            grid=(steps,),
            in_specs=[pl.BlockSpec((per, HEADS, BLOCK, KEYS), lambda g, *_: (g, 0, 0, 0))]
            + [any_spec] * 9
            + [pl.BlockSpec((width, QKV), lambda g, *_: (0, 0)), any_spec],
            out_specs=[any_spec] * 5 + [pl.BlockSpec((8, QKV), lambda g, *_: (0, 0))],
            scratch_shapes=[
                pltpu.VMEM((LENGTH, QKV), jnp.bfloat16),
                pltpu.VMEM((LENGTH, 192), jnp.bfloat16),
                pltpu.VMEM((LENGTH, 192), jnp.bfloat16),
                pltpu.VMEM((LENGTH, KV), jnp.float32),
                pltpu.VMEM((per * HEADS, 128, KEYS), jnp.bfloat16),
                pltpu.VMEM((LENGTH, QKV), jnp.bfloat16),
                pltpu.VMEM((QROWS, width), jnp.float32),
                pltpu.VMEM((3 * QROWS, width), jnp.bfloat16),
                pltpu.SemaphoreType.DMA((13,)),
            ],
        ),
        out_shape=[
            jax.ShapeDtypeStruct((LENGTH, QKV), jnp.bfloat16),
            jax.ShapeDtypeStruct((QROWS, width), jnp.float32),
            share,
            share,
            share,
            jax.ShapeDtypeStruct((8, QKV), jnp.float32),
        ],
        compiler_params=pltpu.CompilerParams(
            dimension_semantics=("arbitrary",), vmem_limit_bytes=vmem_limit
        ),
        cost_estimate=pl.CostEstimate(
            flops=40 * 10**9, transcendentals=0, bytes_accessed=25 * 10**6
        ),
        name="attend_backward",
    )(table, probs, qkv, *grads, *outs, w_qkv, da)


def head_weight_kernel(x0, x1, x2, x3, grad_ref, out_ref, x_scr, acc, sems):
    slot = pl.program_id(0)

    @pl.when(slot == 0)
    def _load():
        copies = [
            pltpu.make_async_copy(src, x_scr.at[pl.ds(n * QROWS, QROWS)], sems.at[n])
            for n, src in enumerate((x0, x1, x2, x3))
        ]
        for copy in copies:
            copy.start()
        acc[...] = jnp.zeros_like(acc)
        for copy in copies:
            copy.wait()

    rows = pl.ds(pl.multiple_of(slot * QROWS, QROWS), QROWS)
    acc[...] += dot_tn(x_scr[rows], grad_ref[...])

    @pl.when(slot == pl.num_programs(0) - 1)
    def _store():
        out_ref[:, 0 : KV + 128] = acc[:, 0 : KV + 128].astype(jnp.bfloat16)
        out_ref[:, KV + 128 : KV + 192] = acc[:, KV + 192 : KV + 256].astype(jnp.bfloat16)


def head_weight_block(rows, grad_qkv):
    width = rows[0].shape[1]
    any_spec = pl.BlockSpec(memory_space=pl.ANY)
    return pl.pallas_call(
        head_weight_kernel,
        grid=(GROUP,),
        in_specs=[any_spec] * 4 + [pl.BlockSpec((QROWS, QKV), lambda g: (g, 0))],
        out_specs=pl.BlockSpec((width, QKV - 64), lambda g: (0, 0)),
        scratch_shapes=[
            pltpu.VMEM((LENGTH, width), jnp.bfloat16),
            pltpu.VMEM((width, QKV), jnp.float32),
            pltpu.SemaphoreType.DMA((4,)),
        ],
        out_shape=jax.ShapeDtypeStruct((width, QKV - 64), jnp.bfloat16),
        compiler_params=pltpu.CompilerParams(
            dimension_semantics=("arbitrary",), vmem_limit_bytes=vmem_limit
        ),
        cost_estimate=pl.CostEstimate(
            flops=8 * 10**9, transcendentals=0, bytes_accessed=12 * 10**6
        ),
        name="head_weight_block",
    )(*rows, grad_qkv)


def row_mean(values):
    return jnp.mean(values, axis=1, keepdims=True)


def fold_rows(values):
    total = values[0:8]
    for row in range(8, values.shape[0], 8):
        total = total + values[row : row + 8]
    return total


def token_kernel(
    tile,
    width,
    hidden,
    rank_ref,
    o0,
    o1,
    o2,
    o3,
    x_ref,
    cot_ref,
    vec_ref,
    up_bias_ref,
    weights,
    out_ref,
    n1_ref,
    g_ref,
    du_ref,
    dfr_ref,
    dar_ref,
    da_ref,
    do0,
    do1,
    do2,
    do3,
    total_ref,
    w_scr,
    acc,
    u_scr,
    slope_scr,
    xhat_scr,
    m1_scr,
    sum_ref,
    up_sum_ref,
    sem,
):
    step = pl.program_id(0)
    parts = GROUP
    small = 32
    cols = 256
    spans = ((2 * hidden, weights.shape[1] - 2 * hidden), (0, hidden), (hidden, hidden))
    arrivals = [
        pltpu.make_async_copy(
            weights.at[:, pl.ds(*span)], w_scr.at[:, pl.ds(*span)], sem.at[n]
        )
        for n, span in enumerate(spans)
    ]

    @pl.when(step == 0)
    def _load():
        for copy in arrivals:
            copy.start()
        sum_ref[...] = jnp.zeros_like(sum_ref)
        up_sum_ref[...] = jnp.zeros_like(up_sum_ref)
        arrivals[0].wait()

    def vector(n):
        return vec_ref[n : n + 1, :]

    def part_rows(n):
        return slice(n * width, (n + 1) * width)

    def out_weight(n):
        place = pl.multiple_of((rank_ref[0] ^ n) * width, width)
        return w_scr[pl.ds(place, width), 2 * hidden :]

    total = dot_nt(o0[...], out_weight(0))
    for n, piece in ((1, o1), (2, o2), (3, o3)):
        total = total + dot_nt(piece[...], out_weight(n))
    acc[...] = total
    first_scale = []
    for row in range(0, tile, small):
        rows = slice(row, row + small)
        resid = acc[rows] + x_ref[rows].astype(jnp.float32) + vector(0)
        center = resid - row_mean(resid)
        scale = lax.rsqrt(row_mean(center * center) + epsilon)
        xhat = center * scale
        normed = xhat * vector(1) + vector(2)
        first_scale.append(scale)
        xhat_scr[rows] = xhat
        m1_scr[rows] = normed
        n1_ref[rows] = normed.astype(jnp.bfloat16)

    @pl.when(step == 0)
    def _arrived():
        arrivals[1].wait()
        arrivals[2].wait()

    for part in range(parts):
        u_scr[part % 2] = dot_nn(n1_ref[...], w_scr[part_rows(part), 0:hidden])
        for row in range(0, tile, small):
            rows = slice(row, row + small)
            for col in range(0, hidden, cols):
                place = slice(col, col + cols)
                wide = slice(part * hidden + col, part * hidden + col + cols)
                pre = u_scr[part % 2, rows, place] + up_bias_ref[:, wide]
                cdf = 0.5 + 0.5 * lax.erf(pre * 0.7071067811865476)
                g_ref[rows, wide] = (pre * cdf).astype(jnp.bfloat16)
                slope_scr[rows, wide] = (
                    cdf + pre * jnp.exp(-0.5 * pre * pre) * 0.3989422804014327
                )
        lift = dot_nt(
            g_ref[:, part * hidden : (part + 1) * hidden],
            w_scr[part_rows(part), hidden : 2 * hidden],
        )
        if part == 0:
            acc[...] = lift
        else:
            acc[...] += lift
    sums = [jnp.zeros((8, width), jnp.float32) for _ in range(6)]
    for row in range(0, tile, small):
        rows = slice(row, row + small)
        second = m1_scr[rows] + acc[rows] + vector(3)
        center = second - row_mean(second)
        scale = lax.rsqrt(row_mean(center * center) + epsilon)
        xhat = center * scale
        out_ref[rows] = (xhat * vector(4) + vector(5)).astype(jnp.bfloat16)
        top = cot_ref[rows].astype(jnp.float32)
        gained = top * vector(4)
        down = scale * (gained - row_mean(gained) - xhat * row_mean(gained * xhat))
        sums[0] = sums[0] + fold_rows(top * xhat)
        sums[1] = sums[1] + fold_rows(top)
        sums[2] = sums[2] + fold_rows(down)
        m1_scr[rows] = down
        dfr_ref[rows] = down.astype(jnp.bfloat16)
    for part in range(parts):
        whole = slice(part * hidden, (part + 1) * hidden)
        u_scr[part % 2] = dot_nn(dfr_ref[...], w_scr[part_rows(part), hidden : 2 * hidden])
        for col in range(0, hidden, cols):
            place = slice(col, col + cols)
            wide = slice(part * hidden + col, part * hidden + col + cols)
            tally = jnp.zeros((8, cols), jnp.float32)
            for row in range(0, tile, small):
                rows = slice(row, row + small)
                low = (u_scr[part % 2, rows, place] * slope_scr[rows, wide]).astype(jnp.bfloat16)
                du_ref[rows, wide] = low
                tally = tally + fold_rows(low.astype(jnp.float32))
            up_sum_ref[:, wide] += tally
        lift = dot_nt(du_ref[:, whole], w_scr[part_rows(part), 0:hidden])
        if part == 0:
            acc[...] = lift
        else:
            acc[...] += lift
    for n, row in enumerate(range(0, tile, small)):
        rows = slice(row, row + small)
        back = m1_scr[rows] + acc[rows]
        xhat = xhat_scr[rows]
        sums[3] = sums[3] + fold_rows(back * xhat)
        sums[4] = sums[4] + fold_rows(back)
        gained = back * vector(1)
        down = first_scale[n] * (gained - row_mean(gained) - xhat * row_mean(gained * xhat))
        sums[5] = sums[5] + fold_rows(down)
        da_ref[rows] = down
        dar_ref[rows] = down.astype(jnp.bfloat16)
    for n in range(6):
        sum_ref[n] += sums[n]
    for n, do_ref in enumerate((do0, do1, do2, do3)):
        do_ref[...] = dot_nn(dar_ref[...], out_weight(n)).astype(jnp.bfloat16)

    @pl.when(step == pl.num_programs(0) - 1)
    def _totals():
        for n in range(6):
            total_ref[:, n * width : (n + 1) * width] = jnp.sum(
                sum_ref[n], axis=0, keepdims=True
            )
        total_ref[:, 6 * width :] = jnp.sum(up_sum_ref[...], axis=0, keepdims=True)


def token_block(rank, outs, own, cot, vectors, up_bias, weights):
    count, width = own.shape
    total_hidden = up_bias.shape[1]
    hidden = total_hidden // GROUP
    tile = 256

    def rows_of(columns):
        return pl.BlockSpec((tile, columns), lambda g, *_: (g, 0))

    def whole(shape):
        return pl.BlockSpec(shape, lambda g, *_: (0,) * len(shape))

    low = jnp.bfloat16
    head = outs[0].shape[1]
    return pl.pallas_call(
        functools.partial(token_kernel, tile, width, hidden),
        grid_spec=pltpu.PrefetchScalarGridSpec(
            num_scalar_prefetch=1,
            grid=(count // tile,),
            in_specs=[rows_of(head)] * 4
            + [rows_of(width)] * 2
            + [whole(vectors.shape), whole(up_bias.shape)] + [pl.BlockSpec(memory_space=pl.ANY)],
            out_specs=[
                rows_of(width),
                rows_of(width),
                rows_of(total_hidden),
                rows_of(total_hidden),
                rows_of(width),
                rows_of(width),
                rows_of(width),
                rows_of(head),
                rows_of(head),
                rows_of(head),
                rows_of(head),
                whole((1, 6 * width + total_hidden)),
            ],
            scratch_shapes=[
                pltpu.VMEM(weights.shape, low),
                pltpu.VMEM((tile, width), jnp.float32),
                pltpu.VMEM((2, tile, hidden), jnp.float32),
                pltpu.VMEM((tile, total_hidden), jnp.float32),
                pltpu.VMEM((tile, width), jnp.float32),
                pltpu.VMEM((tile, width), jnp.float32),
                pltpu.VMEM((6, 8, width), jnp.float32),
                pltpu.VMEM((8, total_hidden), jnp.float32),
                pltpu.SemaphoreType.DMA((3,)),
            ],
        ),
        out_shape=[
            jax.ShapeDtypeStruct((count, width), low),
            jax.ShapeDtypeStruct((count, width), low),
            jax.ShapeDtypeStruct((count, total_hidden), low),
            jax.ShapeDtypeStruct((count, total_hidden), low),
            jax.ShapeDtypeStruct((count, width), low),
            jax.ShapeDtypeStruct((count, width), low),
            jax.ShapeDtypeStruct((count, width), jnp.float32),
            jax.ShapeDtypeStruct((count, head), low),
            jax.ShapeDtypeStruct((count, head), low),
            jax.ShapeDtypeStruct((count, head), low),
            jax.ShapeDtypeStruct((count, head), low),
            jax.ShapeDtypeStruct((1, 6 * width + total_hidden), jnp.float32),
        ],
        compiler_params=pltpu.CompilerParams(
            dimension_semantics=("arbitrary",), vmem_limit_bytes=vmem_limit
        ),
        cost_estimate=pl.CostEstimate(
            flops=46 * 10**9, transcendentals=0, bytes_accessed=40 * 10**6
        ),
        name="token_block",
    )(rank.astype(jnp.int32).reshape(1), *outs, own, cot, vectors, up_bias, weights)


def weight_kernel(width, hidden, rank_ref, n1, dfr, dar, g, du, o0, o1, o2, o3, out_ref, n1_t, dfr_t, dar_t):
    part = pl.program_id(0)

    @pl.when(part == 0)
    def _turn():
        n1_t[...] = n1[...].T
        dfr_t[...] = dfr[...].T
        dar_t[...] = dar[...].T

    chunk = 256

    def product(n, carry):
        rows = pl.ds(pl.multiple_of(n * chunk, chunk), chunk)
        out_ref[rows, 0:hidden] = dot_nn(n1_t[rows], du[...]).astype(jnp.bfloat16)
        out_ref[rows, hidden : 2 * hidden] = dot_nn(dfr_t[rows], g[...]).astype(jnp.bfloat16)
        return carry

    lax.fori_loop(0, width // chunk, product, 0)
    for n, piece in enumerate((o0, o1, o2, o3)):

        @pl.when(part == rank_ref[0] ^ n)
        def _out(piece=piece):
            out_ref[:, 2 * hidden :] = dot_nn(dar_t[...], piece[...]).astype(jnp.bfloat16)


def weight_block(rank, n1, dfr, dar, g, du, outs):
    count, width = n1.shape
    hidden = g.shape[1] // GROUP
    head = outs[0].shape[1]
    columns = 2 * hidden + head
    low = jnp.bfloat16

    def whole(shape):
        return pl.BlockSpec(shape, lambda g, *_: (0,) * len(shape))

    return pl.pallas_call(
        functools.partial(weight_kernel, width, hidden),
        grid_spec=pltpu.PrefetchScalarGridSpec(
            num_scalar_prefetch=1,
            grid=(GROUP,),
            in_specs=[whole((count, width))] * 3
            + [pl.BlockSpec((count, hidden), lambda g, *_: (0, g))] * 2
            + [whole((count, head))] * 4,
            out_specs=pl.BlockSpec((width, columns), lambda g, *_: (g, 0)),
            scratch_shapes=[pltpu.VMEM((width, count), low)] * 3,
        ),
        out_shape=jax.ShapeDtypeStruct((GROUP * width, columns), low),
        compiler_params=pltpu.CompilerParams(
            dimension_semantics=("arbitrary",), vmem_limit_bytes=vmem_limit
        ),
        cost_estimate=pl.CostEstimate(
            flops=22 * 10**9, transcendentals=0, bytes_accessed=30 * 10**6
        ),
        name="weight_block",
    )(rank.astype(jnp.int32).reshape(1), n1, dfr, dar, g, du, *outs)


def pack_columns(query, key, value, axis):
    def piece(matrix, head):
        return lax.slice_in_dim(matrix, head * HD, (head + 1) * HD, axis=axis)

    return jnp.concatenate(
        [
            piece(value, 0),
            piece(key, 0),
            piece(key, 1),
            piece(value, 1),
            piece(value, 2),
            piece(key, 2),
            piece(query, 1),
            piece(query, 0),
            piece(query, 2),
        ],
        axis=axis,
    )


def insert_zero(packed, axis):
    head = lax.slice_in_dim(packed, 0, KV + 128, axis=axis)
    tail = lax.slice_in_dim(packed, KV + 128, KV + 192, axis=axis)
    return jnp.concatenate([head, jnp.zeros_like(tail), tail], axis=axis)


def drop_zero(packed, axis):
    head = lax.slice_in_dim(packed, 0, KV + 128, axis=axis)
    tail = lax.slice_in_dim(packed, KV + 192, KV + 256, axis=axis)
    return jnp.concatenate([head, tail], axis=axis)


def unpack_columns(packed, axis):
    def piece(n):
        return lax.slice_in_dim(packed, n * HD, (n + 1) * HD, axis=axis)

    query = jnp.concatenate([piece(7), piece(6), piece(8)], axis=axis)
    key = jnp.concatenate([piece(1), piece(2), piece(5)], axis=axis)
    value = jnp.concatenate([piece(0), piece(3), piece(4)], axis=axis)
    return query, key, value


def per_device(
    dp_size,
    tensor_size,
    inputs,
    cotangent,
    w_query,
    w_key,
    w_value,
    w_output,
    w_up,
    w_down,
    b_query,
    b_value,
    b_output,
    gain_attn,
    bias_attn,
    b_up,
    b_down,
    gain_mlp,
    bias_mlp,
    random_blocks,
):
    width = inputs.shape[1]
    hidden = b_up.shape[0]
    low = jnp.bfloat16
    dp_index = lax.axis_index("dp")
    tensor_index = lax.axis_index("tensor")
    core = dp_index % 2
    half = tensor_index // 2
    rank = 2 * core + tensor_index % 2
    here = core == half
    devices = [(d, t) for d in range(dp_size) for t in range(tensor_size)]
    pair_bits = [bit for bit in range(1, dp_size.bit_length() - 1)]

    def flat(d, t):
        return d * tensor_size + t

    def stays(d, t):
        return d % 2 == t // 2

    def flip(value, d_bits, t_bits, chosen=None):
        pairs = [
            (flat(d, t), flat(d ^ d_bits, t ^ t_bits))
            for d, t in devices
            if chosen is None or chosen(d, t)
        ]
        return lax.ppermute(value, both, pairs)

    def moves(d, t):
        return not stays(d, t)

    def rehome(value):
        return jnp.where(here, value, flip(value, 1, 2, moves))

    def near_of(value):
        return flip(value, 0, 1)

    def side_of(value):
        return flip(value, 1, 0)

    rest = jnp.concatenate([w_up, w_down.T, w_output.T], axis=1)
    below = jnp.concatenate(split_three(b_up))
    below = jnp.pad(below, (0, -below.shape[0] % rest.shape[1])).reshape(-1, rest.shape[1])
    rest = jnp.concatenate([rest, below], axis=0)

    packed = pack_columns(w_query, w_key, w_value, 1)
    columns = packed.shape[1]
    floats = jnp.concatenate([b_query, b_value])
    small = jnp.concatenate(split_three(floats) + [random_blocks.astype(low).reshape(-1)])
    small = jnp.pad(small, (0, -small.shape[0] % columns)).reshape(-1, columns)
    packed = jnp.concatenate([order_halves(core, packed, side_of(packed)), small], axis=0)
    packed_got = flip(packed, 0, 2, stays)

    moved = flip(inputs, 1, 2, moves)
    near_stay = flip(inputs, 0, 1, stays)
    moved, near_stay, packed_got, rest = lax.optimization_barrier(
        (moved, near_stay, packed_got, rest)
    )
    own = jnp.where(here, inputs, moved)
    near_move = flip(own, 0, 1, moves)
    own, packed_got = lax.optimization_barrier((own, packed_got))
    rest = lax.all_gather(rest, "tensor", axis=0)
    packed = jnp.where(here, packed, packed_got)
    small = packed[2 * w_query.shape[0] :].reshape(-1)
    packed = packed[: 2 * w_query.shape[0]]
    for bit in pair_bits:
        packed = order_halves((dp_index >> bit) % 2, packed, flip(packed, 1 << bit, 0))
    w_qkv = insert_zero(packed, 1)
    count = floats.shape[0]
    mine = sum(small[n * count : (n + 1) * count].astype(jnp.float32) for n in range(3))
    my_random = small[3 * count : 3 * count + random_blocks.size]
    my_random = my_random.reshape(HEADS, NB, -1).astype(jnp.int32)
    b_key = jnp.zeros_like(b_query)
    b_qkv = insert_zero(pack_columns(mine[:192], b_key, mine[192:], 0), 0)
    scale = jnp.concatenate([jnp.ones((KV,), jnp.float32), jnp.full((256,), 0.125, jnp.float32)])
    near = jnp.where(here, near_stay, near_move)
    near, own, cotangent, w_qkv, b_qkv, rest = lax.optimization_barrier(
        (near, own, cotangent, w_qkv, b_qkv, rest)
    )
    side, far = side_of(own), side_of(near)
    cot_moved = flip(cotangent, 1, 2, moves)
    below = rest[:, w_up.shape[0] :].reshape(GROUP, -1)
    rest_all = lax.all_gather(
        rest[:, : w_up.shape[0]], "dp", axis=1, tiled=True
    ).reshape(GROUP * width, -1)
    b_up_all = sum(
        below[:, n * hidden : (n + 1) * hidden].astype(jnp.float32) for n in range(3)
    ).reshape(1, -1)
    rows = (own, near, side, far)
    grad_top = jnp.where(here, cotangent, cot_moved)
    block = jnp.arange(NB, dtype=jnp.int32)
    block = block ^ (rank * QB)
    fixed = jnp.clip(
        jnp.stack(
            [
                jnp.zeros_like(block),
                jnp.full_like(block, NB - 1),
                block - 1,
                block,
                block + 1,
            ],
            axis=-1,
        ),
        0,
        NB - 1,
    )
    local_random = jnp.take(my_random, block, axis=1)
    table = jnp.concatenate(
        [jnp.broadcast_to(fixed[None], (HEADS, NB, 5)), local_random], axis=-1
    )
    table = (table ^ (rank * QB)).reshape(-1)

    weights = (w_qkv, b_qkv[None], scale[None])
    out_near, out_far, out_side, probs, qkv = attend_forward((1, 3, 2), rank, table, rows, weights)
    out_own, probs = attend_forward((0,), rank, table, qkv=qkv, probs=probs)
    outs = (out_own, near_of(out_near), side_of(out_side), flip(out_far, 1, 1))

    vectors = jnp.stack([b_output, gain_attn, bias_attn, b_down, gain_mlp, bias_mlp])
    layer_out, n1, g, du, dfr, dar, da, *do, sums = token_block(
        rank, outs, own, grad_top, vectors, b_up_all, rest_all
    )
    grads = (do[0], near_of(do[1]), side_of(do[2]), flip(do[3], 1, 1))
    rest_grad = weight_block(rank, n1, dfr, dar, g, du, outs)
    sums = sums.reshape(-1)
    sums = sums + flip(sums, 0, 1)
    rest_grad, sums, *grads = lax.optimization_barrier((rest_grad, sums, *grads))
    rest_sum = lax.psum_scatter(
        rest_grad.reshape(GROUP, width, -1), "dp", scatter_dimension=1, tiled=True
    )
    layer_sent = flip(layer_out, 1, 2, moves)

    grad_qkv, base, to_near, to_side, to_far, bias_sum = attend_backward(
        table, probs, qkv, grads, (out_own, out_near, out_side, out_far), w_qkv, da
    )
    grad_qkv, base, to_near, to_side, to_far, bias_sum, layer_sent = lax.optimization_barrier(
        (grad_qkv, base, to_near, to_side, to_far, bias_sum, layer_sent)
    )
    side_far = side_of(to_far)
    side_own = side_of(to_side)
    bias_query, _, bias_value = unpack_columns(drop_zero(jnp.sum(bias_sum, axis=0), 0), 0)
    sums = jnp.concatenate([sums, bias_query, bias_value])
    sums = sums + flip(sums, 0, 2)
    to_near = (to_near.astype(jnp.float32) + side_far.astype(jnp.float32)).astype(low)
    to_near, sums = lax.optimization_barrier((to_near, sums))
    near_got = near_of(to_near)
    base = base + side_own.astype(jnp.float32)
    grad_late, to_near = lax.optimization_barrier((grad_qkv, to_near))
    for bit in pair_bits:
        sums = sums + flip(sums, 1 << bit, 0)
    other = side_of(sums)
    grad_late, sums = lax.optimization_barrier((grad_late, sums))
    grad_w = head_weight_block(rows, grad_late)
    rest_sum, base, grad_w = lax.optimization_barrier((rest_sum, base, grad_w))
    rest_sum = lax.psum_scatter(rest_sum, "tensor", scatter_dimension=0, tiled=False).astype(
        jnp.float32
    )
    for bit in reversed(pair_bits[2:]):
        grad_w = halve(flip, (dp_index >> bit) % 2, grad_w, 1 << bit, 0)
    place = (dp_index // 2) % 4
    rows_each = grad_w.shape[0] // 4
    total = lax.dynamic_slice_in_dim(grad_w, place * rows_each, rows_each, 0).astype(jnp.float32)
    for n in (3, 1, 2):
        send = lax.dynamic_slice_in_dim(grad_w, (place ^ n) * rows_each, rows_each, 0)
        total = total + flip(send, 2 * n, 0).astype(jnp.float32)
    grad_w = total.astype(low)
    near_got, grad_w, base, sums, other, layer_sent = lax.optimization_barrier(
        (near_got, grad_w, base, sums, other, layer_sent)
    )
    grad_own = (base + near_got.astype(jnp.float32)).astype(low)
    grad_own, grad_w, layer_sent = lax.optimization_barrier((grad_own, grad_w, layer_sent))
    grad_moved = flip(grad_own, 1, 2, moves)

    grad_got = flip(grad_w, 0, 2, moves)
    grad_w = grad_w.astype(jnp.float32) + grad_got.astype(jnp.float32)
    rows_each = grad_w.shape[0] // 2
    grad_w = grad_w.astype(low)
    keep = lax.dynamic_slice_in_dim(grad_w, core * rows_each, rows_each, 0)
    send = lax.dynamic_slice_in_dim(grad_w, (1 - core) * rows_each, rows_each, 0)
    side_got = side_of(send)
    grad_moved, side_got, rest_sum = lax.optimization_barrier((grad_moved, side_got, rest_sum))
    shard = jnp.where(here, keep, side_got).astype(jnp.float32)
    shard_query, shard_key, shard_value = unpack_columns(shard, 1)
    shard_up = rest_sum[:, :hidden]
    shard_down = rest_sum[:, hidden : 2 * hidden].T
    shard_output = rest_sum[:, 2 * hidden :].T
    layer_out = jnp.where(here, layer_out, layer_sent)
    grad_input = jnp.where(here, grad_own, grad_moved)

    count = 6 * width + GROUP * hidden
    bias_pair = jnp.where(here, sums[count:], other[count:])
    sums = sums + other
    top = sums[: 6 * width].reshape(6, width)
    grad_b_up = lax.dynamic_slice_in_dim(sums, 6 * width + tensor_index * hidden, hidden, 0)
    return (
        layer_out,
        grad_input,
        shard_query,
        shard_key,
        shard_value,
        shard_output,
        shard_up,
        shard_down,
        bias_pair[:192],
        bias_pair[192:],
        top[5],
        top[3],
        top[4],
        grad_b_up,
        top[2],
        top[0],
        top[1],
    )


def order_halves(bit, own, other):
    return jnp.where(
        bit == 0,
        jnp.concatenate([own, other], axis=0),
        jnp.concatenate([other, own], axis=0),
    )


def split_three(values):
    parts = []
    for _ in range(3):
        part = lax.reduce_precision(values, 8, 7)
        parts.append(part.astype(jnp.bfloat16))
        values = values - part
    return parts


def halve(flip, bit, value, d_bits, t_bits):
    rows = value.shape[0] // 2
    keep = lax.dynamic_slice_in_dim(value, bit * rows, rows, 0)
    send = lax.dynamic_slice_in_dim(value, (1 - bit) * rows, rows, 0)
    got = flip(send, d_bits, t_bits)
    return (keep.astype(jnp.float32) + got.astype(jnp.float32)).astype(value.dtype)


def solution(mesh):
    in_specs = (
        P(("dp", "tensor"), None),
        P(("dp", "tensor"), None),
        P("dp", "tensor"),
        P("dp", "tensor"),
        P("dp", "tensor"),
        P("tensor", "dp"),
        P("dp", "tensor"),
        P("tensor", "dp"),
        P("tensor"),
        P("tensor"),
        P(),
        P(),
        P(),
        P("tensor"),
        P(),
        P(),
        P(),
        P("tensor", None, None),
    )
    out_specs = (
        P(("dp", "tensor"), None),
        P(("dp", "tensor"), None),
        P("dp", "tensor"),
        P("dp", "tensor"),
        P("dp", "tensor"),
        P("tensor", "dp"),
        P("dp", "tensor"),
        P("tensor", "dp"),
        P("tensor"),
        P("tensor"),
        P(),
        P(),
        P(),
        P("tensor"),
        P(),
        P(),
        P(),
    )
    body = functools.partial(per_device, mesh.shape["dp"], mesh.shape["tensor"])
    return jax.shard_map(body, mesh=mesh, in_specs=in_specs, out_specs=out_specs, check_vma=False)
```

```python
import functools

import jax
import jax.numpy as jnp
from jax import lax
from jax.experimental import pallas as pl
from jax.experimental.pallas import tpu as pltpu
from jax.sharding import PartitionSpec as P

HD = 64
BLOCK = 64
LENGTH = 4096
NB = LENGTH // BLOCK
GROUP = 4
QROWS = LENGTH // GROUP
QB = QROWS // BLOCK
HEADS = 3
KEYS = 8 * BLOCK
KV = 128 * HEADS
QKV = KV + 256

negative = -1e30
epsilon = 1e-05
both = ("dp", "tensor")
vmem_limit = 56 * 1024 * 1024


def dot_nn(left, right):
    return jnp.dot(left, right, preferred_element_type=jnp.float32)


def dot_tn(left, right):
    return lax.dot_general(
        left, right, (((0,), (0,)), ((), ())), preferred_element_type=jnp.float32
    )


def dot_nt(left, right):
    return lax.dot_general(
        left, right, (((1,), (1,)), ((), ())), preferred_element_type=jnp.float32
    )


def lane_masks(dtype):
    lane = lax.broadcasted_iota(jnp.int32, (1, 128), 1)
    low = (lane < 64).astype(jnp.float32).astype(dtype)
    high = (lane >= 64).astype(jnp.float32).astype(dtype)
    return low, high


def key_bias(block):
    lane = lax.broadcasted_iota(jnp.int32, (1, KEYS), 1)
    entry = lane // BLOCK
    key = jnp.where(entry == 2, block - 1, jnp.where(entry == 3, block, block + 1))
    window = (entry >= 2) & (entry <= 4)
    off = window & ((key < 1) | (key > NB - 2))
    return jnp.where(off, negative, 0.0).astype(jnp.float32)


def gather_keys(table, source, head, block):
    rows = []
    for entry in range(8):
        place = table[(head * NB + block) * 8 + entry]
        rows.append(source[pl.ds(pl.multiple_of(place * BLOCK, BLOCK), BLOCK), head * 128 : head * 128 + 128])
    return jnp.concatenate(rows, axis=0)


def head_queries(first, second, low, high):
    return (first * high, first * low, second)


def forward_kernel(steps, count, project, table, place, *refs):
    step = pl.program_id(0)
    last = step == pl.num_programs(0) - 1
    if project:
        x_refs, (w_ref, add_ref, scale_ref), refs = refs[:4], refs[4:7], refs[7:]
        o_refs, (p_ref, qkv_hbm), refs = refs[:count], refs[count : count + 2], refs[count + 2 :]
        qkv_scr, s_scr, o_scr, x_scr, sems = refs
        out_copy = pltpu.make_async_copy(qkv_scr, qkv_hbm, sems.at[4])

        @pl.when(step == 0)
        def _project():
            copies = [
                pltpu.make_async_copy(src, x_scr.at[pl.ds(n * QROWS, QROWS)], sems.at[n])
                for n, src in enumerate(x_refs)
            ]
            for copy in copies:
                copy.start()
            for copy in copies:
                copy.wait()
            chunk = 512

            def body(n, carry):
                rows = pl.ds(pl.multiple_of(n * chunk, chunk), chunk)
                total = dot_nn(x_scr[rows], w_ref[...]) + add_ref[...]
                qkv_scr[rows] = (total.astype(jnp.bfloat16).astype(jnp.float32) * scale_ref[...]).astype(
                    jnp.bfloat16
                )
                return carry

            lax.fori_loop(0, LENGTH // chunk, body, 0)
            out_copy.start()

        @pl.when(last)
        def _written():
            out_copy.wait()

    else:
        qkv_hbm, _ = refs[:2]
        o_refs, refs = refs[2 : 2 + count], refs[2 + count :]
        p_ref, qkv_scr, s_scr, o_scr, sems = refs

        @pl.when(step == 0)
        def _load():
            copy = pltpu.make_async_copy(qkv_hbm, qkv_scr, sems.at[0])
            copy.start()
            copy.wait()

    low, high = lane_masks(jnp.bfloat16)
    lane = lax.broadcasted_iota(jnp.int32, (1, 128), 1)
    per = QB // steps
    units = [(sub, head) for sub in range(per) for head in range(HEADS)]
    slot = place[1 + step // steps]
    keys = []
    for sub in range(per):
        local = slot * QB + (step % steps) * per + sub
        bias = key_bias(local ^ (place[0] * QB))
        rows = pl.ds(pl.multiple_of(local * BLOCK, BLOCK), BLOCK)
        queries = head_queries(
            qkv_scr[rows, KV : KV + 128], qkv_scr[rows, KV + 128 : KV + 256], low, high
        )
        for head in range(HEADS):
            n = sub * HEADS + head
            keys.append(gather_keys(table, qkv_scr, head, local))
            raw = dot_nt(queries[head], keys[n])
            s_scr[n, :, 0:128] = raw[:, 0:128]
            s_scr[n, :, 128:384] = raw[:, 128:384] + bias[:, 128:384]
            s_scr[n, :, 384:512] = raw[:, 384:512]
    tops = [jnp.max(s_scr[n], axis=1, keepdims=True) for n in range(len(units))]
    sums = []
    for n in range(len(units)):
        expo = jnp.exp(s_scr[n] - tops[n])
        s_scr[n] = expo
        sums.append(jnp.sum(expo, axis=1, keepdims=True))
    for n, (sub, head) in enumerate(units):
        p_ref[sub, head] = (s_scr[n] * (1.0 / sums[n])).astype(jnp.bfloat16)
    for sub in range(per):
        rows = slice(sub * BLOCK, (sub + 1) * BLOCK)
        outs = [dot_nn(p_ref[sub, head], keys[sub * HEADS + head]) for head in range(HEADS)]
        o_scr[rows, 0:128] = jnp.where(lane < 64, outs[0], outs[1]).astype(jnp.bfloat16)
        o_scr[rows, 128:192] = outs[2][:, 0:64].astype(jnp.bfloat16)
    for turn, o_ref in enumerate(o_refs):

        @pl.when(step // steps == turn)
        def _out(o_ref=o_ref):
            o_ref[...] = o_scr[...]


def attend_forward(slots, rank, table, rows=None, weights=None, qkv=None, probs=None):
    steps = 4
    per = QB // steps
    count = len(slots)
    project = rows is not None
    any_spec = pl.BlockSpec(memory_space=pl.ANY)
    place = jnp.stack([rank.astype(jnp.int32)] + [jnp.int32(slot) for slot in slots])
    operands = [table, place] + ([*rows, *weights] if project else [qkv, probs])
    in_specs = [any_spec] * (4 if project else 2)
    if project:
        in_specs += [pl.BlockSpec(each.shape, lambda g, *_: (0, 0)) for each in weights]
    qkv_out = [jax.ShapeDtypeStruct((LENGTH, QKV), jnp.bfloat16)] * project
    extra = [pltpu.VMEM((LENGTH, weights[0].shape[0]), jnp.bfloat16)] if project else []
    return pl.pallas_call(
        functools.partial(forward_kernel, steps, count, project),
        grid_spec=pltpu.PrefetchScalarGridSpec(
            num_scalar_prefetch=2,
            grid=(count * steps,),
            in_specs=in_specs,
            out_specs=[
                pl.BlockSpec(
                    (per * BLOCK, 192),
                    lambda g, *_, turn=turn: (jnp.clip(g - turn * steps, 0, steps - 1), 0),
                )
                for turn in range(count)
            ]
            + [
                pl.BlockSpec(
                    (per, HEADS, BLOCK, KEYS),
                    lambda g, t, pos: (pos[1 + g // steps] * steps + g % steps, 0, 0, 0),
                ),
            ]
            + [any_spec] * project,
            scratch_shapes=[
                pltpu.VMEM((LENGTH, QKV), jnp.bfloat16),
                pltpu.VMEM((per * HEADS, BLOCK, KEYS), jnp.float32),
                pltpu.VMEM((per * BLOCK, 192), jnp.bfloat16),
            ]
            + extra
            + [pltpu.SemaphoreType.DMA((5,))],
        ),
        out_shape=[jax.ShapeDtypeStruct((QROWS, 192), jnp.bfloat16)] * count
        + [jax.ShapeDtypeStruct((NB, HEADS, BLOCK, KEYS), jnp.bfloat16)]
        + qkv_out,
        input_output_aliases={} if project else {3: count},
        compiler_params=pltpu.CompilerParams(
            dimension_semantics=("arbitrary",), vmem_limit_bytes=vmem_limit
        ),
        name="attend_forward",
    )(*operands)


def backward_kernel(
    steps,
    table,
    p_ref,
    qkv_hbm,
    do0,
    do1,
    do2,
    do3,
    o0,
    o1,
    o2,
    o3,
    w_ref,
    da_hbm,
    out_hbm,
    base_hbm,
    near_hbm,
    side_hbm,
    far_hbm,
    sum_ref,
    qkv_scr,
    do_scr,
    o_scr,
    acc,
    st_scr,
    out_ref,
    da_scr,
    share_scr,
    sems,
):
    step = pl.program_id(0)

    @pl.when(step == 0)
    def _load():
        copies = [pltpu.make_async_copy(qkv_hbm, qkv_scr, sems.at[0])] + [
            pltpu.make_async_copy(src, do_scr.at[pl.ds(n * QROWS, QROWS)], sems.at[4 + n])
            for n, src in enumerate((do0, do1, do2, do3))
        ]
        copies += [
            pltpu.make_async_copy(src, o_scr.at[pl.ds(n * QROWS, QROWS)], sems.at[9 + n])
            for n, src in enumerate((o0, o1, o2, o3))
        ]
        for copy in copies:
            copy.start()
        pltpu.make_async_copy(da_hbm, da_scr, sems.at[8]).start()
        acc[...] = jnp.zeros_like(acc)
        for copy in copies:
            copy.wait()

    low, high = lane_masks(jnp.bfloat16)
    lane = lax.broadcasted_iota(jnp.int32, (1, 128), 1)
    per = NB // steps
    units = [(sub, head) for sub in range(per) for head in range(HEADS)]
    keys, right, wide_low, wide_high = [], [], low.astype(jnp.float32), high.astype(jnp.float32)
    for sub in range(per):
        local = step * per + sub
        rows = pl.ds(pl.multiple_of(local * BLOCK, BLOCK), BLOCK)
        queries = head_queries(
            qkv_scr[rows, KV : KV + 128], qkv_scr[rows, KV + 128 : KV + 256], low, high
        )
        g_first = do_scr[rows, 0:128]
        g_second = do_scr[rows, 128:192]
        first = g_first.astype(jnp.float32) * o_scr[rows, 0:128].astype(jnp.float32)
        second = g_second.astype(jnp.float32) * o_scr[rows, 128:192].astype(jnp.float32)
        totals = (
            jnp.sum(first * wide_low, axis=1, keepdims=True),
            jnp.sum(first * wide_high, axis=1, keepdims=True),
            jnp.sum(second, axis=1, keepdims=True),
        )
        grads = (
            g_first * low,
            g_first * high,
            jnp.concatenate([g_second, jnp.zeros_like(g_second)], axis=1),
        )
        for head in range(HEADS):
            n = sub * HEADS + head
            keys.append(gather_keys(table, qkv_scr, head, local))
            right.append(jnp.concatenate([queries[head], grads[head]], axis=0))
            probs = p_ref[sub, head]
            slopes = probs.astype(jnp.float32) * (dot_nt(grads[head], keys[n]) - totals[head])
            st_scr[n, 0:BLOCK] = slopes.astype(jnp.bfloat16)
            st_scr[n, BLOCK:128] = probs
    for sub in range(per):
        local = step * per + sub
        rows = pl.ds(pl.multiple_of(local * BLOCK, BLOCK), BLOCK)
        backs = [
            dot_nn(st_scr[sub * HEADS + head, 0:BLOCK], keys[sub * HEADS + head]) * 0.125
            for head in range(HEADS)
        ]
        out_ref[rows, KV : KV + 128] = jnp.where(lane < 64, backs[1], backs[0]).astype(jnp.bfloat16)
        out_ref[rows, KV + 128 : KV + 256] = jnp.where(lane < 64, 0.0, backs[2]).astype(
            jnp.bfloat16
        )
    for n, (sub, head) in enumerate(units):
        local = step * per + sub
        spread = dot_tn(st_scr[n], right[n])
        for entry in range(8):
            spot = table[(head * NB + local) * 8 + entry]
            where = pl.ds(pl.multiple_of(spot * BLOCK, BLOCK), BLOCK)
            acc[where, head * 128 : head * 128 + 128] += spread[
                entry * BLOCK : (entry + 1) * BLOCK
            ]

    @pl.when(step == steps - 1)
    def _store():
        out_ref[:, 0:KV] = acc[...].astype(jnp.bfloat16)
        total = jnp.zeros((8, QKV), jnp.float32)
        for row in range(0, LENGTH, 128):
            total = total + fold_rows(out_ref[row : row + 128].astype(jnp.float32))
        sum_ref[...] = total
        pltpu.make_async_copy(da_hbm, da_scr, sems.at[8]).wait()
        done = [pltpu.make_async_copy(out_ref, out_hbm, sems.at[0])]
        done[0].start()
        chunk = 512

        def share(n, carry):
            source = (3 - n // (QROWS // chunk)) * QROWS + (n % (QROWS // chunk)) * chunk
            rows = pl.ds(pl.multiple_of(source, chunk), chunk)
            place = pl.ds(pl.multiple_of(n * chunk, chunk), chunk)
            share_scr[place] = dot_nt(out_ref[rows], w_ref[...]).astype(jnp.bfloat16)
            return carry

        lax.fori_loop(0, 3 * QROWS // chunk, share, 0)
        for n, share_hbm in enumerate((far_hbm, side_hbm, near_hbm)):
            rows = pl.ds(n * QROWS, QROWS)
            done.append(pltpu.make_async_copy(share_scr.at[rows], share_hbm, sems.at[1 + n]))
            done[-1].start()

        def base(n, carry):
            rows = pl.ds(pl.multiple_of(n * chunk, chunk), chunk)
            da_scr[rows] += dot_nt(out_ref[rows], w_ref[...])
            return carry

        lax.fori_loop(0, QROWS // chunk, base, 0)
        done.append(pltpu.make_async_copy(da_scr, base_hbm, sems.at[4]))
        done[-1].start()
        for copy in done:
            copy.wait()


def attend_backward(table, probs, qkv, grads, outs, w_qkv, da):
    steps = 8
    per = NB // steps
    width = w_qkv.shape[0]
    any_spec = pl.BlockSpec(memory_space=pl.ANY)
    share = jax.ShapeDtypeStruct((QROWS, width), jnp.bfloat16)
    return pl.pallas_call(
        functools.partial(backward_kernel, steps),
        grid_spec=pltpu.PrefetchScalarGridSpec(
            num_scalar_prefetch=1,
            grid=(steps,),
            in_specs=[pl.BlockSpec((per, HEADS, BLOCK, KEYS), lambda g, *_: (g, 0, 0, 0))]
            + [any_spec] * 9
            + [pl.BlockSpec((width, QKV), lambda g, *_: (0, 0)), any_spec],
            out_specs=[any_spec] * 5 + [pl.BlockSpec((8, QKV), lambda g, *_: (0, 0))],
            scratch_shapes=[
                pltpu.VMEM((LENGTH, QKV), jnp.bfloat16),
                pltpu.VMEM((LENGTH, 192), jnp.bfloat16),
                pltpu.VMEM((LENGTH, 192), jnp.bfloat16),
                pltpu.VMEM((LENGTH, KV), jnp.float32),
                pltpu.VMEM((per * HEADS, 128, KEYS), jnp.bfloat16),
                pltpu.VMEM((LENGTH, QKV), jnp.bfloat16),
                pltpu.VMEM((QROWS, width), jnp.float32),
                pltpu.VMEM((3 * QROWS, width), jnp.bfloat16),
                pltpu.SemaphoreType.DMA((13,)),
            ],
        ),
        out_shape=[
            jax.ShapeDtypeStruct((LENGTH, QKV), jnp.bfloat16),
            jax.ShapeDtypeStruct((QROWS, width), jnp.float32),
            share,
            share,
            share,
            jax.ShapeDtypeStruct((8, QKV), jnp.float32),
        ],
        compiler_params=pltpu.CompilerParams(
            dimension_semantics=("arbitrary",), vmem_limit_bytes=vmem_limit
        ),
        cost_estimate=pl.CostEstimate(
            flops=40 * 10**9, transcendentals=0, bytes_accessed=25 * 10**6
        ),
        name="attend_backward",
    )(table, probs, qkv, *grads, *outs, w_qkv, da)


def head_weight_kernel(x0, x1, x2, x3, grad_ref, out_ref, x_scr, acc, sems):
    slot = pl.program_id(0)

    @pl.when(slot == 0)
    def _load():
        copies = [
            pltpu.make_async_copy(src, x_scr.at[pl.ds(n * QROWS, QROWS)], sems.at[n])
            for n, src in enumerate((x0, x1, x2, x3))
        ]
        for copy in copies:
            copy.start()
        acc[...] = jnp.zeros_like(acc)
        for copy in copies:
            copy.wait()

    rows = pl.ds(pl.multiple_of(slot * QROWS, QROWS), QROWS)
    acc[...] += dot_tn(x_scr[rows], grad_ref[...])

    @pl.when(slot == pl.num_programs(0) - 1)
    def _store():
        out_ref[:, 0 : KV + 128] = acc[:, 0 : KV + 128].astype(jnp.bfloat16)
        out_ref[:, KV + 128 : KV + 192] = acc[:, KV + 192 : KV + 256].astype(jnp.bfloat16)


def head_weight_block(rows, grad_qkv):
    width = rows[0].shape[1]
    any_spec = pl.BlockSpec(memory_space=pl.ANY)
    return pl.pallas_call(
        head_weight_kernel,
        grid=(GROUP,),
        in_specs=[any_spec] * 4 + [pl.BlockSpec((QROWS, QKV), lambda g: (g, 0))],
        out_specs=pl.BlockSpec((width, QKV - 64), lambda g: (0, 0)),
        scratch_shapes=[
            pltpu.VMEM((LENGTH, width), jnp.bfloat16),
            pltpu.VMEM((width, QKV), jnp.float32),
            pltpu.SemaphoreType.DMA((4,)),
        ],
        out_shape=jax.ShapeDtypeStruct((width, QKV - 64), jnp.bfloat16),
        compiler_params=pltpu.CompilerParams(
            dimension_semantics=("arbitrary",), vmem_limit_bytes=vmem_limit
        ),
        cost_estimate=pl.CostEstimate(
            flops=8 * 10**9, transcendentals=0, bytes_accessed=12 * 10**6
        ),
        name="head_weight_block",
    )(*rows, grad_qkv)


def row_mean(values):
    return jnp.mean(values, axis=1, keepdims=True)


def fold_rows(values):
    total = values[0:8]
    for row in range(8, values.shape[0], 8):
        total = total + values[row : row + 8]
    return total


def token_kernel(
    tile,
    width,
    hidden,
    rank_ref,
    o0,
    o1,
    o2,
    o3,
    x_ref,
    cot_ref,
    vec_ref,
    up_bias_ref,
    weights,
    out_ref,
    n1_ref,
    g_ref,
    du_ref,
    dfr_ref,
    dar_ref,
    da_ref,
    do0,
    do1,
    do2,
    do3,
    total_ref,
    w_scr,
    acc,
    u_scr,
    slope_scr,
    xhat_scr,
    m1_scr,
    sum_ref,
    up_sum_ref,
    sem,
):
    step = pl.program_id(0)
    parts = GROUP
    small = 32
    cols = 256
    spans = ((2 * hidden, weights.shape[1] - 2 * hidden), (0, hidden), (hidden, hidden))
    arrivals = [
        pltpu.make_async_copy(
            weights.at[:, pl.ds(*span)], w_scr.at[:, pl.ds(*span)], sem.at[n]
        )
        for n, span in enumerate(spans)
    ]

    @pl.when(step == 0)
    def _load():
        for copy in arrivals:
            copy.start()
        sum_ref[...] = jnp.zeros_like(sum_ref)
        up_sum_ref[...] = jnp.zeros_like(up_sum_ref)
        arrivals[0].wait()

    def vector(n):
        return vec_ref[n : n + 1, :]

    def part_rows(n):
        return slice(n * width, (n + 1) * width)

    def out_weight(n):
        place = pl.multiple_of((rank_ref[0] ^ n) * width, width)
        return w_scr[pl.ds(place, width), 2 * hidden :]

    total = dot_nt(o0[...], out_weight(0))
    for n, piece in ((1, o1), (2, o2), (3, o3)):
        total = total + dot_nt(piece[...], out_weight(n))
    acc[...] = total
    first_scale = []
    for row in range(0, tile, small):
        rows = slice(row, row + small)
        resid = acc[rows] + x_ref[rows].astype(jnp.float32) + vector(0)
        center = resid - row_mean(resid)
        scale = lax.rsqrt(row_mean(center * center) + epsilon)
        xhat = center * scale
        normed = xhat * vector(1) + vector(2)
        first_scale.append(scale)
        xhat_scr[rows] = xhat
        m1_scr[rows] = normed
        n1_ref[rows] = normed.astype(jnp.bfloat16)

    @pl.when(step == 0)
    def _arrived():
        arrivals[1].wait()
        arrivals[2].wait()

    for part in range(parts):
        u_scr[part % 2] = dot_nn(n1_ref[...], w_scr[part_rows(part), 0:hidden])
        for row in range(0, tile, small):
            rows = slice(row, row + small)
            for col in range(0, hidden, cols):
                place = slice(col, col + cols)
                wide = slice(part * hidden + col, part * hidden + col + cols)
                pre = u_scr[part % 2, rows, place] + up_bias_ref[:, wide]
                cdf = 0.5 + 0.5 * lax.erf(pre * 0.7071067811865476)
                g_ref[rows, wide] = (pre * cdf).astype(jnp.bfloat16)
                slope_scr[rows, wide] = (
                    cdf + pre * jnp.exp(-0.5 * pre * pre) * 0.3989422804014327
                )
        lift = dot_nt(
            g_ref[:, part * hidden : (part + 1) * hidden],
            w_scr[part_rows(part), hidden : 2 * hidden],
        )
        if part == 0:
            acc[...] = lift
        else:
            acc[...] += lift
    sums = [jnp.zeros((8, width), jnp.float32) for _ in range(6)]
    for row in range(0, tile, small):
        rows = slice(row, row + small)
        second = m1_scr[rows] + acc[rows] + vector(3)
        center = second - row_mean(second)
        scale = lax.rsqrt(row_mean(center * center) + epsilon)
        xhat = center * scale
        out_ref[rows] = (xhat * vector(4) + vector(5)).astype(jnp.bfloat16)
        top = cot_ref[rows].astype(jnp.float32)
        gained = top * vector(4)
        down = scale * (gained - row_mean(gained) - xhat * row_mean(gained * xhat))
        sums[0] = sums[0] + fold_rows(top * xhat)
        sums[1] = sums[1] + fold_rows(top)
        sums[2] = sums[2] + fold_rows(down)
        m1_scr[rows] = down
        dfr_ref[rows] = down.astype(jnp.bfloat16)
    for part in range(parts):
        whole = slice(part * hidden, (part + 1) * hidden)
        u_scr[part % 2] = dot_nn(dfr_ref[...], w_scr[part_rows(part), hidden : 2 * hidden])
        for col in range(0, hidden, cols):
            place = slice(col, col + cols)
            wide = slice(part * hidden + col, part * hidden + col + cols)
            tally = jnp.zeros((8, cols), jnp.float32)
            for row in range(0, tile, small):
                rows = slice(row, row + small)
                low = (u_scr[part % 2, rows, place] * slope_scr[rows, wide]).astype(jnp.bfloat16)
                du_ref[rows, wide] = low
                tally = tally + fold_rows(low.astype(jnp.float32))
            up_sum_ref[:, wide] += tally
        lift = dot_nt(du_ref[:, whole], w_scr[part_rows(part), 0:hidden])
        if part == 0:
            acc[...] = lift
        else:
            acc[...] += lift
    for n, row in enumerate(range(0, tile, small)):
        rows = slice(row, row + small)
        back = m1_scr[rows] + acc[rows]
        xhat = xhat_scr[rows]
        sums[3] = sums[3] + fold_rows(back * xhat)
        sums[4] = sums[4] + fold_rows(back)
        gained = back * vector(1)
        down = first_scale[n] * (gained - row_mean(gained) - xhat * row_mean(gained * xhat))
        sums[5] = sums[5] + fold_rows(down)
        da_ref[rows] = down
        dar_ref[rows] = down.astype(jnp.bfloat16)
    for n in range(6):
        sum_ref[n] += sums[n]
    for n, do_ref in enumerate((do0, do1, do2, do3)):
        do_ref[...] = dot_nn(dar_ref[...], out_weight(n)).astype(jnp.bfloat16)

    @pl.when(step == pl.num_programs(0) - 1)
    def _totals():
        for n in range(6):
            total_ref[:, n * width : (n + 1) * width] = jnp.sum(
                sum_ref[n], axis=0, keepdims=True
            )
        total_ref[:, 6 * width :] = jnp.sum(up_sum_ref[...], axis=0, keepdims=True)


def token_block(rank, outs, own, cot, vectors, up_bias, weights):
    count, width = own.shape
    total_hidden = up_bias.shape[1]
    hidden = total_hidden // GROUP
    tile = 256

    def rows_of(columns):
        return pl.BlockSpec((tile, columns), lambda g, *_: (g, 0))

    def whole(shape):
        return pl.BlockSpec(shape, lambda g, *_: (0,) * len(shape))

    low = jnp.bfloat16
    head = outs[0].shape[1]
    return pl.pallas_call(
        functools.partial(token_kernel, tile, width, hidden),
        grid_spec=pltpu.PrefetchScalarGridSpec(
            num_scalar_prefetch=1,
            grid=(count // tile,),
            in_specs=[rows_of(head)] * 4
            + [rows_of(width)] * 2
            + [whole(vectors.shape), whole(up_bias.shape)] + [pl.BlockSpec(memory_space=pl.ANY)],
            out_specs=[
                rows_of(width),
                rows_of(width),
                rows_of(total_hidden),
                rows_of(total_hidden),
                rows_of(width),
                rows_of(width),
                rows_of(width),
                rows_of(head),
                rows_of(head),
                rows_of(head),
                rows_of(head),
                whole((1, 6 * width + total_hidden)),
            ],
            scratch_shapes=[
                pltpu.VMEM(weights.shape, low),
                pltpu.VMEM((tile, width), jnp.float32),
                pltpu.VMEM((2, tile, hidden), jnp.float32),
                pltpu.VMEM((tile, total_hidden), jnp.float32),
                pltpu.VMEM((tile, width), jnp.float32),
                pltpu.VMEM((tile, width), jnp.float32),
                pltpu.VMEM((6, 8, width), jnp.float32),
                pltpu.VMEM((8, total_hidden), jnp.float32),
                pltpu.SemaphoreType.DMA((3,)),
            ],
        ),
        out_shape=[
            jax.ShapeDtypeStruct((count, width), low),
            jax.ShapeDtypeStruct((count, width), low),
            jax.ShapeDtypeStruct((count, total_hidden), low),
            jax.ShapeDtypeStruct((count, total_hidden), low),
            jax.ShapeDtypeStruct((count, width), low),
            jax.ShapeDtypeStruct((count, width), low),
            jax.ShapeDtypeStruct((count, width), jnp.float32),
            jax.ShapeDtypeStruct((count, head), low),
            jax.ShapeDtypeStruct((count, head), low),
            jax.ShapeDtypeStruct((count, head), low),
            jax.ShapeDtypeStruct((count, head), low),
            jax.ShapeDtypeStruct((1, 6 * width + total_hidden), jnp.float32),
        ],
        compiler_params=pltpu.CompilerParams(
            dimension_semantics=("arbitrary",), vmem_limit_bytes=vmem_limit
        ),
        cost_estimate=pl.CostEstimate(
            flops=46 * 10**9, transcendentals=0, bytes_accessed=40 * 10**6
        ),
        name="token_block",
    )(rank.astype(jnp.int32).reshape(1), *outs, own, cot, vectors, up_bias, weights)


def weight_kernel(width, hidden, rank_ref, n1, dfr, dar, g, du, o0, o1, o2, o3, out_ref, n1_t, dfr_t, dar_t):
    part = pl.program_id(0)

    @pl.when(part == 0)
    def _turn():
        n1_t[...] = n1[...].T
        dfr_t[...] = dfr[...].T
        dar_t[...] = dar[...].T

    chunk = 384

    def product(n, carry):
        rows = pl.ds(pl.multiple_of(n * chunk, chunk), chunk)
        out_ref[rows, 0:hidden] = dot_nn(n1_t[rows], du[...]).astype(jnp.bfloat16)
        out_ref[rows, hidden : 2 * hidden] = dot_nn(dfr_t[rows], g[...]).astype(jnp.bfloat16)
        return carry

    lax.fori_loop(0, width // chunk, product, 0)
    for n, piece in enumerate((o0, o1, o2, o3)):

        @pl.when(part == rank_ref[0] ^ n)
        def _out(piece=piece):
            out_ref[:, 2 * hidden :] = dot_nn(dar_t[...], piece[...]).astype(jnp.bfloat16)


def weight_block(rank, n1, dfr, dar, g, du, outs):
    count, width = n1.shape
    hidden = g.shape[1] // GROUP
    head = outs[0].shape[1]
    columns = 2 * hidden + head
    low = jnp.bfloat16

    def whole(shape):
        return pl.BlockSpec(shape, lambda g, *_: (0,) * len(shape))

    return pl.pallas_call(
        functools.partial(weight_kernel, width, hidden),
        grid_spec=pltpu.PrefetchScalarGridSpec(
            num_scalar_prefetch=1,
            grid=(GROUP,),
            in_specs=[whole((count, width))] * 3
            + [pl.BlockSpec((count, hidden), lambda g, *_: (0, g))] * 2
            + [whole((count, head))] * 4,
            out_specs=pl.BlockSpec((width, columns), lambda g, *_: (g, 0)),
            scratch_shapes=[pltpu.VMEM((width, count), low)] * 3,
        ),
        out_shape=jax.ShapeDtypeStruct((GROUP * width, columns), low),
        compiler_params=pltpu.CompilerParams(
            dimension_semantics=("arbitrary",), vmem_limit_bytes=vmem_limit
        ),
        cost_estimate=pl.CostEstimate(
            flops=22 * 10**9, transcendentals=0, bytes_accessed=30 * 10**6
        ),
        name="weight_block",
    )(rank.astype(jnp.int32).reshape(1), n1, dfr, dar, g, du, *outs)


def pack_columns(query, key, value, axis):
    def piece(matrix, head):
        return lax.slice_in_dim(matrix, head * HD, (head + 1) * HD, axis=axis)

    return jnp.concatenate(
        [
            piece(value, 0),
            piece(key, 0),
            piece(key, 1),
            piece(value, 1),
            piece(value, 2),
            piece(key, 2),
            piece(query, 1),
            piece(query, 0),
            piece(query, 2),
        ],
        axis=axis,
    )


def insert_zero(packed, axis):
    head = lax.slice_in_dim(packed, 0, KV + 128, axis=axis)
    tail = lax.slice_in_dim(packed, KV + 128, KV + 192, axis=axis)
    return jnp.concatenate([head, jnp.zeros_like(tail), tail], axis=axis)


def drop_zero(packed, axis):
    head = lax.slice_in_dim(packed, 0, KV + 128, axis=axis)
    tail = lax.slice_in_dim(packed, KV + 192, KV + 256, axis=axis)
    return jnp.concatenate([head, tail], axis=axis)


def unpack_columns(packed, axis):
    def piece(n):
        return lax.slice_in_dim(packed, n * HD, (n + 1) * HD, axis=axis)

    query = jnp.concatenate([piece(7), piece(6), piece(8)], axis=axis)
    key = jnp.concatenate([piece(1), piece(2), piece(5)], axis=axis)
    value = jnp.concatenate([piece(0), piece(3), piece(4)], axis=axis)
    return query, key, value


def per_device(
    dp_size,
    tensor_size,
    inputs,
    cotangent,
    w_query,
    w_key,
    w_value,
    w_output,
    w_up,
    w_down,
    b_query,
    b_value,
    b_output,
    gain_attn,
    bias_attn,
    b_up,
    b_down,
    gain_mlp,
    bias_mlp,
    random_blocks,
):
    width = inputs.shape[1]
    hidden = b_up.shape[0]
    low = jnp.bfloat16
    dp_index = lax.axis_index("dp")
    tensor_index = lax.axis_index("tensor")
    core = dp_index % 2
    half = tensor_index // 2
    rank = 2 * core + tensor_index % 2
    here = core == half
    devices = [(d, t) for d in range(dp_size) for t in range(tensor_size)]
    pair_bits = [bit for bit in range(1, dp_size.bit_length() - 1)]

    def flat(d, t):
        return d * tensor_size + t

    def stays(d, t):
        return d % 2 == t // 2

    def flip(value, d_bits, t_bits, chosen=None):
        pairs = [
            (flat(d, t), flat(d ^ d_bits, t ^ t_bits))
            for d, t in devices
            if chosen is None or chosen(d, t)
        ]
        return lax.ppermute(value, both, pairs)

    def moves(d, t):
        return not stays(d, t)

    def rehome(value):
        return jnp.where(here, value, flip(value, 1, 2, moves))

    def near_of(value):
        return flip(value, 0, 1)

    def side_of(value):
        return flip(value, 1, 0)

    rest = jnp.concatenate([w_up, w_down.T, w_output.T], axis=1)
    below = jnp.concatenate(split_three(b_up))
    below = jnp.pad(below, (0, -below.shape[0] % rest.shape[1])).reshape(-1, rest.shape[1])
    rest = jnp.concatenate([rest, below], axis=0)

    packed = pack_columns(w_query, w_key, w_value, 1)
    columns = packed.shape[1]
    floats = jnp.concatenate([b_query, b_value])
    small = jnp.concatenate(split_three(floats) + [random_blocks.astype(low).reshape(-1)])
    small = jnp.pad(small, (0, -small.shape[0] % columns)).reshape(-1, columns)
    packed = jnp.concatenate([order_halves(core, packed, side_of(packed)), small], axis=0)
    packed_got = flip(packed, 0, 2, stays)

    moved = flip(inputs, 1, 2, moves)
    near_stay = flip(inputs, 0, 1, stays)
    moved, near_stay, packed_got, rest = lax.optimization_barrier(
        (moved, near_stay, packed_got, rest)
    )
    own = jnp.where(here, inputs, moved)
    near_move = flip(own, 0, 1, moves)
    own, packed_got = lax.optimization_barrier((own, packed_got))
    rest = lax.all_gather(rest, "tensor", axis=0)
    packed = jnp.where(here, packed, packed_got)
    small = packed[2 * w_query.shape[0] :].reshape(-1)
    packed = packed[: 2 * w_query.shape[0]]
    for bit in pair_bits:
        packed = order_halves((dp_index >> bit) % 2, packed, flip(packed, 1 << bit, 0))
    w_qkv = insert_zero(packed, 1)
    count = floats.shape[0]
    mine = sum(small[n * count : (n + 1) * count].astype(jnp.float32) for n in range(3))
    my_random = small[3 * count : 3 * count + random_blocks.size]
    my_random = my_random.reshape(HEADS, NB, -1).astype(jnp.int32)
    b_key = jnp.zeros_like(b_query)
    b_qkv = insert_zero(pack_columns(mine[:192], b_key, mine[192:], 0), 0)
    scale = jnp.concatenate([jnp.ones((KV,), jnp.float32), jnp.full((256,), 0.125, jnp.float32)])
    near = jnp.where(here, near_stay, near_move)
    near, own, cotangent, w_qkv, b_qkv = lax.optimization_barrier(
        (near, own, cotangent, w_qkv, b_qkv)
    )
    side, far = side_of(own), side_of(near)
    cot_moved = flip(cotangent, 1, 2, moves)
    side, far, rest = lax.optimization_barrier((side, far, rest))
    below = rest[:, w_up.shape[0] :].reshape(GROUP, -1)
    rest_all = lax.all_gather(
        rest[:, : w_up.shape[0]], "dp", axis=1, tiled=True
    ).reshape(GROUP * width, -1)
    b_up_all = sum(
        below[:, n * hidden : (n + 1) * hidden].astype(jnp.float32) for n in range(3)
    ).reshape(1, -1)
    rows = (own, near, side, far)
    grad_top = jnp.where(here, cotangent, cot_moved)
    block = jnp.arange(NB, dtype=jnp.int32)
    block = block ^ (rank * QB)
    fixed = jnp.clip(
        jnp.stack(
            [
                jnp.zeros_like(block),
                jnp.full_like(block, NB - 1),
                block - 1,
                block,
                block + 1,
            ],
            axis=-1,
        ),
        0,
        NB - 1,
    )
    local_random = jnp.take(my_random, block, axis=1)
    table = jnp.concatenate(
        [jnp.broadcast_to(fixed[None], (HEADS, NB, 5)), local_random], axis=-1
    )
    table = (table ^ (rank * QB)).reshape(-1)

    weights = (w_qkv, b_qkv[None], scale[None])
    out_near, out_far, out_side, probs, qkv = attend_forward((1, 3, 2), rank, table, rows, weights)
    out_own, probs = attend_forward((0,), rank, table, qkv=qkv, probs=probs)
    outs = (out_own, near_of(out_near), side_of(out_side), flip(out_far, 1, 1))

    vectors = jnp.stack([b_output, gain_attn, bias_attn, b_down, gain_mlp, bias_mlp])
    layer_out, n1, g, du, dfr, dar, da, *do, sums = token_block(
        rank, outs, own, grad_top, vectors, b_up_all, rest_all
    )
    grads = (do[0], near_of(do[1]), side_of(do[2]), flip(do[3], 1, 1))
    rest_grad = weight_block(rank, n1, dfr, dar, g, du, outs)
    sums = sums.reshape(-1)
    sums = sums + flip(sums, 0, 1)
    rest_grad, sums, *grads = lax.optimization_barrier((rest_grad, sums, *grads))
    rest_sum = lax.psum_scatter(
        rest_grad.reshape(GROUP, width, -1), "dp", scatter_dimension=1, tiled=True
    )
    layer_sent = flip(layer_out, 1, 2, moves)

    grad_qkv, base, to_near, to_side, to_far, bias_sum = attend_backward(
        table, probs, qkv, grads, (out_own, out_near, out_side, out_far), w_qkv, da
    )
    grad_qkv, base, to_near, to_side, to_far, bias_sum, layer_sent = lax.optimization_barrier(
        (grad_qkv, base, to_near, to_side, to_far, bias_sum, layer_sent)
    )
    side_far = side_of(to_far)
    side_own = side_of(to_side)
    bias_query, _, bias_value = unpack_columns(drop_zero(jnp.sum(bias_sum, axis=0), 0), 0)
    sums = jnp.concatenate([sums, bias_query, bias_value])
    sums = sums + flip(sums, 0, 2)
    to_near = (to_near.astype(jnp.float32) + side_far.astype(jnp.float32)).astype(low)
    to_near, sums = lax.optimization_barrier((to_near, sums))
    near_got = near_of(to_near)
    base = base + side_own.astype(jnp.float32)
    grad_late, to_near = lax.optimization_barrier((grad_qkv, to_near))
    for bit in pair_bits:
        sums = sums + flip(sums, 1 << bit, 0)
    other = side_of(sums)
    grad_late, sums = lax.optimization_barrier((grad_late, sums))
    grad_w = head_weight_block(rows, grad_late)
    rest_sum, base, grad_w = lax.optimization_barrier((rest_sum, base, grad_w))
    rest_sum = lax.psum_scatter(rest_sum, "tensor", scatter_dimension=0, tiled=False).astype(
        jnp.float32
    )
    for bit in reversed(pair_bits[2:]):
        grad_w = halve(flip, (dp_index >> bit) % 2, grad_w, 1 << bit, 0)
    place = (dp_index // 2) % 4
    rows_each = grad_w.shape[0] // 4
    total = lax.dynamic_slice_in_dim(grad_w, place * rows_each, rows_each, 0).astype(jnp.float32)
    for n in (3, 1, 2):
        send = lax.dynamic_slice_in_dim(grad_w, (place ^ n) * rows_each, rows_each, 0)
        total = total + flip(send, 2 * n, 0).astype(jnp.float32)
    grad_w = total.astype(low)
    near_got, grad_w, base, sums, other, layer_sent = lax.optimization_barrier(
        (near_got, grad_w, base, sums, other, layer_sent)
    )
    grad_own = (base + near_got.astype(jnp.float32)).astype(low)
    grad_own, grad_w, layer_sent = lax.optimization_barrier((grad_own, grad_w, layer_sent))
    grad_moved = flip(grad_own, 1, 2, moves)

    grad_got = flip(grad_w, 0, 2, moves)
    grad_w = grad_w.astype(jnp.float32) + grad_got.astype(jnp.float32)
    rows_each = grad_w.shape[0] // 2
    grad_w = grad_w.astype(low)
    keep = lax.dynamic_slice_in_dim(grad_w, core * rows_each, rows_each, 0)
    send = lax.dynamic_slice_in_dim(grad_w, (1 - core) * rows_each, rows_each, 0)
    side_got = side_of(send)
    grad_moved, side_got, rest_sum = lax.optimization_barrier((grad_moved, side_got, rest_sum))
    shard = jnp.where(here, keep, side_got).astype(jnp.float32)
    shard_query, shard_key, shard_value = unpack_columns(shard, 1)
    shard_up = rest_sum[:, :hidden]
    shard_down = rest_sum[:, hidden : 2 * hidden].T
    shard_output = rest_sum[:, 2 * hidden :].T
    layer_out = jnp.where(here, layer_out, layer_sent)
    grad_input = jnp.where(here, grad_own, grad_moved)

    count = 6 * width + GROUP * hidden
    bias_pair = jnp.where(here, sums[count:], other[count:])
    sums = sums + other
    top = sums[: 6 * width].reshape(6, width)
    grad_b_up = lax.dynamic_slice_in_dim(sums, 6 * width + tensor_index * hidden, hidden, 0)
    return (
        layer_out,
        grad_input,
        shard_query,
        shard_key,
        shard_value,
        shard_output,
        shard_up,
        shard_down,
        bias_pair[:192],
        bias_pair[192:],
        top[5],
        top[3],
        top[4],
        grad_b_up,
        top[2],
        top[0],
        top[1],
    )


def order_halves(bit, own, other):
    return jnp.where(
        bit == 0,
        jnp.concatenate([own, other], axis=0),
        jnp.concatenate([other, own], axis=0),
    )


def split_three(values):
    parts = []
    for _ in range(3):
        part = lax.reduce_precision(values, 8, 7)
        parts.append(part.astype(jnp.bfloat16))
        values = values - part
    return parts


def halve(flip, bit, value, d_bits, t_bits):
    rows = value.shape[0] // 2
    keep = lax.dynamic_slice_in_dim(value, bit * rows, rows, 0)
    send = lax.dynamic_slice_in_dim(value, (1 - bit) * rows, rows, 0)
    got = flip(send, d_bits, t_bits)
    return (keep.astype(jnp.float32) + got.astype(jnp.float32)).astype(value.dtype)


def solution(mesh):
    in_specs = (
        P(("dp", "tensor"), None),
        P(("dp", "tensor"), None),
        P("dp", "tensor"),
        P("dp", "tensor"),
        P("dp", "tensor"),
        P("tensor", "dp"),
        P("dp", "tensor"),
        P("tensor", "dp"),
        P("tensor"),
        P("tensor"),
        P(),
        P(),
        P(),
        P("tensor"),
        P(),
        P(),
        P(),
        P("tensor", None, None),
    )
    out_specs = (
        P(("dp", "tensor"), None),
        P(("dp", "tensor"), None),
        P("dp", "tensor"),
        P("dp", "tensor"),
        P("dp", "tensor"),
        P("tensor", "dp"),
        P("dp", "tensor"),
        P("tensor", "dp"),
        P("tensor"),
        P("tensor"),
        P(),
        P(),
        P(),
        P("tensor"),
        P(),
        P(),
        P(),
    )
    body = functools.partial(per_device, mesh.shape["dp"], mesh.shape["tensor"])
    return jax.shard_map(body, mesh=mesh, in_specs=in_specs, out_specs=out_specs, check_vma=False)
```

```python
import functools

import jax
import jax.numpy as jnp
from jax import lax
from jax.experimental import pallas as pl
from jax.experimental.pallas import tpu as pltpu
from jax.sharding import PartitionSpec as P

HD = 64
BLOCK = 64
LENGTH = 4096
NB = LENGTH // BLOCK
GROUP = 4
QROWS = LENGTH // GROUP
QB = QROWS // BLOCK
HEADS = 3
KEYS = 8 * BLOCK
KV = 128 * HEADS
QKV = KV + 256

negative = -1e30
epsilon = 1e-05
both = ("dp", "tensor")
vmem_limit = 56 * 1024 * 1024


def dot_nn(left, right):
    return jnp.dot(left, right, preferred_element_type=jnp.float32)


def dot_tn(left, right):
    return lax.dot_general(
        left, right, (((0,), (0,)), ((), ())), preferred_element_type=jnp.float32
    )


def dot_nt(left, right):
    return lax.dot_general(
        left, right, (((1,), (1,)), ((), ())), preferred_element_type=jnp.float32
    )


def lane_masks(dtype):
    lane = lax.broadcasted_iota(jnp.int32, (1, 128), 1)
    low = (lane < 64).astype(jnp.float32).astype(dtype)
    high = (lane >= 64).astype(jnp.float32).astype(dtype)
    return low, high


def key_bias(block):
    lane = lax.broadcasted_iota(jnp.int32, (1, KEYS), 1)
    entry = lane // BLOCK
    key = jnp.where(entry == 2, block - 1, jnp.where(entry == 3, block, block + 1))
    window = (entry >= 2) & (entry <= 4)
    off = window & ((key < 1) | (key > NB - 2))
    return jnp.where(off, negative, 0.0).astype(jnp.float32)


def gather_keys(table, source, head, block):
    rows = []
    for entry in range(8):
        place = table[(head * NB + block) * 8 + entry]
        rows.append(source[pl.ds(pl.multiple_of(place * BLOCK, BLOCK), BLOCK), head * 128 : head * 128 + 128])
    return jnp.concatenate(rows, axis=0)


def head_queries(first, second, low, high):
    return (first * high, first * low, second)


def forward_kernel(steps, count, project, table, place, *refs):
    step = pl.program_id(0)
    last = step == pl.num_programs(0) - 1
    if project:
        x_refs, (w_ref, add_ref, scale_ref), refs = refs[:4], refs[4:7], refs[7:]
        o_refs, (p_ref, qkv_hbm), refs = refs[:count], refs[count : count + 2], refs[count + 2 :]
        qkv_scr, s_scr, o_scr, x_scr, sems = refs
        out_copy = pltpu.make_async_copy(qkv_scr, qkv_hbm, sems.at[4])

        @pl.when(step == 0)
        def _project():
            copies = [
                pltpu.make_async_copy(src, x_scr.at[pl.ds(n * QROWS, QROWS)], sems.at[n])
                for n, src in enumerate(x_refs)
            ]
            for copy in copies:
                copy.start()
            for copy in copies:
                copy.wait()
            chunk = 512

            def body(n, carry):
                rows = pl.ds(pl.multiple_of(n * chunk, chunk), chunk)
                total = dot_nn(x_scr[rows], w_ref[...]) + add_ref[...]
                qkv_scr[rows] = (total.astype(jnp.bfloat16).astype(jnp.float32) * scale_ref[...]).astype(
                    jnp.bfloat16
                )
                return carry

            lax.fori_loop(0, LENGTH // chunk, body, 0)
            out_copy.start()

        @pl.when(last)
        def _written():
            out_copy.wait()

    else:
        qkv_hbm, _ = refs[:2]
        o_refs, refs = refs[2 : 2 + count], refs[2 + count :]
        p_ref, qkv_scr, s_scr, o_scr, sems = refs

        @pl.when(step == 0)
        def _load():
            copy = pltpu.make_async_copy(qkv_hbm, qkv_scr, sems.at[0])
            copy.start()
            copy.wait()

    low, high = lane_masks(jnp.bfloat16)
    lane = lax.broadcasted_iota(jnp.int32, (1, 128), 1)
    per = QB // steps
    units = [(sub, head) for sub in range(per) for head in range(HEADS)]
    slot = place[1 + step // steps]
    keys = []
    for sub in range(per):
        local = slot * QB + (step % steps) * per + sub
        bias = key_bias(local ^ (place[0] * QB))
        rows = pl.ds(pl.multiple_of(local * BLOCK, BLOCK), BLOCK)
        queries = head_queries(
            qkv_scr[rows, KV : KV + 128], qkv_scr[rows, KV + 128 : KV + 256], low, high
        )
        for head in range(HEADS):
            n = sub * HEADS + head
            keys.append(gather_keys(table, qkv_scr, head, local))
            raw = dot_nt(queries[head], keys[n])
            s_scr[n, :, 0:128] = raw[:, 0:128]
            s_scr[n, :, 128:384] = raw[:, 128:384] + bias[:, 128:384]
            s_scr[n, :, 384:512] = raw[:, 384:512]
    tops = [jnp.max(s_scr[n], axis=1, keepdims=True) for n in range(len(units))]
    sums = []
    for n in range(len(units)):
        expo = jnp.exp(s_scr[n] - tops[n])
        s_scr[n] = expo
        sums.append(jnp.sum(expo, axis=1, keepdims=True))
    for n, (sub, head) in enumerate(units):
        p_ref[sub, head] = (s_scr[n] * (1.0 / sums[n])).astype(jnp.bfloat16)
    for sub in range(per):
        rows = slice(sub * BLOCK, (sub + 1) * BLOCK)
        outs = [dot_nn(p_ref[sub, head], keys[sub * HEADS + head]) for head in range(HEADS)]
        o_scr[rows, 0:128] = jnp.where(lane < 64, outs[0], outs[1]).astype(jnp.bfloat16)
        o_scr[rows, 128:192] = outs[2][:, 0:64].astype(jnp.bfloat16)
    for turn, o_ref in enumerate(o_refs):

        @pl.when(step // steps == turn)
        def _out(o_ref=o_ref):
            o_ref[...] = o_scr[...]


def attend_forward(slots, rank, table, rows=None, weights=None, qkv=None, probs=None):
    steps = 4
    per = QB // steps
    count = len(slots)
    project = rows is not None
    any_spec = pl.BlockSpec(memory_space=pl.ANY)
    place = jnp.stack([rank.astype(jnp.int32)] + [jnp.int32(slot) for slot in slots])
    operands = [table, place] + ([*rows, *weights] if project else [qkv, probs])
    in_specs = [any_spec] * (4 if project else 2)
    if project:
        in_specs += [pl.BlockSpec(each.shape, lambda g, *_: (0, 0)) for each in weights]
    qkv_out = [jax.ShapeDtypeStruct((LENGTH, QKV), jnp.bfloat16)] * project
    extra = [pltpu.VMEM((LENGTH, weights[0].shape[0]), jnp.bfloat16)] if project else []
    return pl.pallas_call(
        functools.partial(forward_kernel, steps, count, project),
        grid_spec=pltpu.PrefetchScalarGridSpec(
            num_scalar_prefetch=2,
            grid=(count * steps,),
            in_specs=in_specs,
            out_specs=[
                pl.BlockSpec(
                    (per * BLOCK, 192),
                    lambda g, *_, turn=turn: (jnp.clip(g - turn * steps, 0, steps - 1), 0),
                )
                for turn in range(count)
            ]
            + [
                pl.BlockSpec(
                    (per, HEADS, BLOCK, KEYS),
                    lambda g, t, pos: (pos[1 + g // steps] * steps + g % steps, 0, 0, 0),
                ),
            ]
            + [any_spec] * project,
            scratch_shapes=[
                pltpu.VMEM((LENGTH, QKV), jnp.bfloat16),
                pltpu.VMEM((per * HEADS, BLOCK, KEYS), jnp.float32),
                pltpu.VMEM((per * BLOCK, 192), jnp.bfloat16),
            ]
            + extra
            + [pltpu.SemaphoreType.DMA((5,))],
        ),
        out_shape=[jax.ShapeDtypeStruct((QROWS, 192), jnp.bfloat16)] * count
        + [jax.ShapeDtypeStruct((NB, HEADS, BLOCK, KEYS), jnp.bfloat16)]
        + qkv_out,
        input_output_aliases={} if project else {3: count},
        compiler_params=pltpu.CompilerParams(
            dimension_semantics=("arbitrary",), vmem_limit_bytes=vmem_limit
        ),
        name="attend_forward",
    )(*operands)


def backward_kernel(
    steps,
    table,
    p_ref,
    qkv_hbm,
    do0,
    do1,
    do2,
    do3,
    o0,
    o1,
    o2,
    o3,
    w_ref,
    da_hbm,
    out_hbm,
    base_hbm,
    near_hbm,
    side_hbm,
    far_hbm,
    sum_ref,
    qkv_scr,
    do_scr,
    o_scr,
    acc,
    st_scr,
    out_ref,
    da_scr,
    share_scr,
    sems,
):
    step = pl.program_id(0)

    @pl.when(step == 0)
    def _load():
        copies = [pltpu.make_async_copy(qkv_hbm, qkv_scr, sems.at[0])] + [
            pltpu.make_async_copy(src, do_scr.at[pl.ds(n * QROWS, QROWS)], sems.at[4 + n])
            for n, src in enumerate((do0, do1, do2, do3))
        ]
        copies += [
            pltpu.make_async_copy(src, o_scr.at[pl.ds(n * QROWS, QROWS)], sems.at[9 + n])
            for n, src in enumerate((o0, o1, o2, o3))
        ]
        for copy in copies:
            copy.start()
        pltpu.make_async_copy(da_hbm, da_scr, sems.at[8]).start()
        acc[...] = jnp.zeros_like(acc)
        for copy in copies:
            copy.wait()

    low, high = lane_masks(jnp.bfloat16)
    lane = lax.broadcasted_iota(jnp.int32, (1, 128), 1)
    per = NB // steps
    units = [(sub, head) for sub in range(per) for head in range(HEADS)]
    keys, right, wide_low, wide_high = [], [], low.astype(jnp.float32), high.astype(jnp.float32)
    for sub in range(per):
        local = step * per + sub
        rows = pl.ds(pl.multiple_of(local * BLOCK, BLOCK), BLOCK)
        queries = head_queries(
            qkv_scr[rows, KV : KV + 128], qkv_scr[rows, KV + 128 : KV + 256], low, high
        )
        g_first = do_scr[rows, 0:128]
        g_second = do_scr[rows, 128:192]
        first = g_first.astype(jnp.float32) * o_scr[rows, 0:128].astype(jnp.float32)
        second = g_second.astype(jnp.float32) * o_scr[rows, 128:192].astype(jnp.float32)
        totals = (
            jnp.sum(first * wide_low, axis=1, keepdims=True),
            jnp.sum(first * wide_high, axis=1, keepdims=True),
            jnp.sum(second, axis=1, keepdims=True),
        )
        grads = (
            g_first * low,
            g_first * high,
            jnp.concatenate([g_second, jnp.zeros_like(g_second)], axis=1),
        )
        for head in range(HEADS):
            n = sub * HEADS + head
            keys.append(gather_keys(table, qkv_scr, head, local))
            right.append(jnp.concatenate([queries[head], grads[head]], axis=0))
            probs = p_ref[sub, head]
            slopes = probs.astype(jnp.float32) * (dot_nt(grads[head], keys[n]) - totals[head])
            st_scr[n, 0:BLOCK] = slopes.astype(jnp.bfloat16)
            st_scr[n, BLOCK:128] = probs
    for sub in range(per):
        local = step * per + sub
        rows = pl.ds(pl.multiple_of(local * BLOCK, BLOCK), BLOCK)
        backs = [
            dot_nn(st_scr[sub * HEADS + head, 0:BLOCK], keys[sub * HEADS + head]) * 0.125
            for head in range(HEADS)
        ]
        out_ref[rows, KV : KV + 128] = jnp.where(lane < 64, backs[1], backs[0]).astype(jnp.bfloat16)
        out_ref[rows, KV + 128 : KV + 256] = jnp.where(lane < 64, 0.0, backs[2]).astype(
            jnp.bfloat16
        )
    for n, (sub, head) in enumerate(units):
        local = step * per + sub
        spread = dot_tn(st_scr[n], right[n])
        for entry in range(8):
            spot = table[(head * NB + local) * 8 + entry]
            where = pl.ds(pl.multiple_of(spot * BLOCK, BLOCK), BLOCK)
            acc[where, head * 128 : head * 128 + 128] += spread[
                entry * BLOCK : (entry + 1) * BLOCK
            ]

    @pl.when(step == steps - 1)
    def _store():
        out_ref[:, 0:KV] = acc[...].astype(jnp.bfloat16)
        total = jnp.zeros((8, QKV), jnp.float32)
        for row in range(0, LENGTH, 128):
            total = total + fold_rows(out_ref[row : row + 128].astype(jnp.float32))
        sum_ref[...] = total
        pltpu.make_async_copy(da_hbm, da_scr, sems.at[8]).wait()
        done = [pltpu.make_async_copy(out_ref, out_hbm, sems.at[0])]
        done[0].start()
        chunk = 512

        def share(n, carry):
            source = (3 - n // (QROWS // chunk)) * QROWS + (n % (QROWS // chunk)) * chunk
            rows = pl.ds(pl.multiple_of(source, chunk), chunk)
            place = pl.ds(pl.multiple_of(n * chunk, chunk), chunk)
            share_scr[place] = dot_nt(out_ref[rows], w_ref[...]).astype(jnp.bfloat16)
            return carry

        lax.fori_loop(0, 3 * QROWS // chunk, share, 0)
        for n, share_hbm in enumerate((far_hbm, side_hbm, near_hbm)):
            rows = pl.ds(n * QROWS, QROWS)
            done.append(pltpu.make_async_copy(share_scr.at[rows], share_hbm, sems.at[1 + n]))
            done[-1].start()

        def base(n, carry):
            rows = pl.ds(pl.multiple_of(n * chunk, chunk), chunk)
            da_scr[rows] += dot_nt(out_ref[rows], w_ref[...])
            return carry

        lax.fori_loop(0, QROWS // chunk, base, 0)
        done.append(pltpu.make_async_copy(da_scr, base_hbm, sems.at[4]))
        done[-1].start()
        for copy in done:
            copy.wait()


def attend_backward(table, probs, qkv, grads, outs, w_qkv, da):
    steps = 8
    per = NB // steps
    width = w_qkv.shape[0]
    any_spec = pl.BlockSpec(memory_space=pl.ANY)
    share = jax.ShapeDtypeStruct((QROWS, width), jnp.bfloat16)
    return pl.pallas_call(
        functools.partial(backward_kernel, steps),
        grid_spec=pltpu.PrefetchScalarGridSpec(
            num_scalar_prefetch=1,
            grid=(steps,),
            in_specs=[pl.BlockSpec((per, HEADS, BLOCK, KEYS), lambda g, *_: (g, 0, 0, 0))]
            + [any_spec] * 9
            + [pl.BlockSpec((width, QKV), lambda g, *_: (0, 0)), any_spec],
            out_specs=[any_spec] * 5 + [pl.BlockSpec((8, QKV), lambda g, *_: (0, 0))],
            scratch_shapes=[
                pltpu.VMEM((LENGTH, QKV), jnp.bfloat16),
                pltpu.VMEM((LENGTH, 192), jnp.bfloat16),
                pltpu.VMEM((LENGTH, 192), jnp.bfloat16),
                pltpu.VMEM((LENGTH, KV), jnp.float32),
                pltpu.VMEM((per * HEADS, 128, KEYS), jnp.bfloat16),
                pltpu.VMEM((LENGTH, QKV), jnp.bfloat16),
                pltpu.VMEM((QROWS, width), jnp.float32),
                pltpu.VMEM((3 * QROWS, width), jnp.bfloat16),
                pltpu.SemaphoreType.DMA((13,)),
            ],
        ),
        out_shape=[
            jax.ShapeDtypeStruct((LENGTH, QKV), jnp.bfloat16),
            jax.ShapeDtypeStruct((QROWS, width), jnp.float32),
            share,
            share,
            share,
            jax.ShapeDtypeStruct((8, QKV), jnp.float32),
        ],
        compiler_params=pltpu.CompilerParams(
            dimension_semantics=("arbitrary",), vmem_limit_bytes=vmem_limit
        ),
        cost_estimate=pl.CostEstimate(
            flops=40 * 10**9, transcendentals=0, bytes_accessed=25 * 10**6
        ),
        name="attend_backward",
    )(table, probs, qkv, *grads, *outs, w_qkv, da)


def head_weight_kernel(x0, x1, x2, x3, grad_ref, out_ref, x_scr, acc, sems):
    slot = pl.program_id(0)

    @pl.when(slot == 0)
    def _load():
        copies = [
            pltpu.make_async_copy(src, x_scr.at[pl.ds(n * QROWS, QROWS)], sems.at[n])
            for n, src in enumerate((x0, x1, x2, x3))
        ]
        for copy in copies:
            copy.start()
        acc[...] = jnp.zeros_like(acc)
        for copy in copies:
            copy.wait()

    rows = pl.ds(pl.multiple_of(slot * QROWS, QROWS), QROWS)
    acc[...] += dot_tn(x_scr[rows], grad_ref[...])

    @pl.when(slot == pl.num_programs(0) - 1)
    def _store():
        out_ref[:, 0 : KV + 128] = acc[:, 0 : KV + 128].astype(jnp.bfloat16)
        out_ref[:, KV + 128 : KV + 192] = acc[:, KV + 192 : KV + 256].astype(jnp.bfloat16)


def head_weight_block(rows, grad_qkv):
    width = rows[0].shape[1]
    any_spec = pl.BlockSpec(memory_space=pl.ANY)
    return pl.pallas_call(
        head_weight_kernel,
        grid=(GROUP,),
        in_specs=[any_spec] * 4 + [pl.BlockSpec((QROWS, QKV), lambda g: (g, 0))],
        out_specs=pl.BlockSpec((width, QKV - 64), lambda g: (0, 0)),
        scratch_shapes=[
            pltpu.VMEM((LENGTH, width), jnp.bfloat16),
            pltpu.VMEM((width, QKV), jnp.float32),
            pltpu.SemaphoreType.DMA((4,)),
        ],
        out_shape=jax.ShapeDtypeStruct((width, QKV - 64), jnp.bfloat16),
        compiler_params=pltpu.CompilerParams(
            dimension_semantics=("arbitrary",), vmem_limit_bytes=vmem_limit
        ),
        cost_estimate=pl.CostEstimate(
            flops=8 * 10**9, transcendentals=0, bytes_accessed=12 * 10**6
        ),
        name="head_weight_block",
    )(*rows, grad_qkv)


def row_mean(values):
    return jnp.mean(values, axis=1, keepdims=True)


def fold_rows(values):
    total = values[0:8]
    for row in range(8, values.shape[0], 8):
        total = total + values[row : row + 8]
    return total


def token_kernel(
    tile,
    width,
    hidden,
    rank_ref,
    o0,
    o1,
    o2,
    o3,
    x_ref,
    cot_ref,
    vec_ref,
    up_bias_ref,
    weights,
    out_ref,
    n1_ref,
    g_ref,
    du_ref,
    dfr_ref,
    dar_ref,
    da_ref,
    do0,
    do1,
    do2,
    do3,
    total_ref,
    w_scr,
    acc,
    u_scr,
    slope_scr,
    xhat_scr,
    m1_scr,
    sum_ref,
    up_sum_ref,
    sem,
):
    step = pl.program_id(0)
    parts = GROUP
    small = 32
    cols = 256
    spans = ((2 * hidden, weights.shape[1] - 2 * hidden), (0, hidden), (hidden, hidden))
    arrivals = [
        pltpu.make_async_copy(
            weights.at[:, pl.ds(*span)], w_scr.at[:, pl.ds(*span)], sem.at[n]
        )
        for n, span in enumerate(spans)
    ]

    @pl.when(step == 0)
    def _load():
        for copy in arrivals:
            copy.start()
        sum_ref[...] = jnp.zeros_like(sum_ref)
        up_sum_ref[...] = jnp.zeros_like(up_sum_ref)
        arrivals[0].wait()

    def vector(n):
        return vec_ref[n : n + 1, :]

    def part_rows(n):
        return slice(n * width, (n + 1) * width)

    def out_weight(n):
        place = pl.multiple_of((rank_ref[0] ^ n) * width, width)
        return w_scr[pl.ds(place, width), 2 * hidden :]

    total = dot_nt(o0[...], out_weight(0))
    for n, piece in ((1, o1), (2, o2), (3, o3)):
        total = total + dot_nt(piece[...], out_weight(n))
    acc[...] = total
    first_scale = []
    for row in range(0, tile, small):
        rows = slice(row, row + small)
        resid = acc[rows] + x_ref[rows].astype(jnp.float32) + vector(0)
        center = resid - row_mean(resid)
        scale = lax.rsqrt(row_mean(center * center) + epsilon)
        xhat = center * scale
        normed = xhat * vector(1) + vector(2)
        first_scale.append(scale)
        xhat_scr[rows] = xhat
        m1_scr[rows] = normed
        n1_ref[rows] = normed.astype(jnp.bfloat16)

    @pl.when(step == 0)
    def _arrived():
        arrivals[1].wait()
        arrivals[2].wait()

    for part in range(parts):
        u_scr[part % 2] = dot_nn(n1_ref[...], w_scr[part_rows(part), 0:hidden])
        for row in range(0, tile, small):
            rows = slice(row, row + small)
            for col in range(0, hidden, cols):
                place = slice(col, col + cols)
                wide = slice(part * hidden + col, part * hidden + col + cols)
                pre = u_scr[part % 2, rows, place] + up_bias_ref[:, wide]
                cdf = 0.5 + 0.5 * lax.erf(pre * 0.7071067811865476)
                g_ref[rows, wide] = (pre * cdf).astype(jnp.bfloat16)
                slope_scr[rows, wide] = (
                    cdf + pre * jnp.exp(-0.5 * pre * pre) * 0.3989422804014327
                )
        lift = dot_nt(
            g_ref[:, part * hidden : (part + 1) * hidden],
            w_scr[part_rows(part), hidden : 2 * hidden],
        )
        if part == 0:
            acc[...] = lift
        else:
            acc[...] += lift
    sums = [jnp.zeros((8, width), jnp.float32) for _ in range(6)]
    for row in range(0, tile, small):
        rows = slice(row, row + small)
        second = m1_scr[rows] + acc[rows] + vector(3)
        center = second - row_mean(second)
        scale = lax.rsqrt(row_mean(center * center) + epsilon)
        xhat = center * scale
        out_ref[rows] = (xhat * vector(4) + vector(5)).astype(jnp.bfloat16)
        top = cot_ref[rows].astype(jnp.float32)
        gained = top * vector(4)
        down = scale * (gained - row_mean(gained) - xhat * row_mean(gained * xhat))
        sums[0] = sums[0] + fold_rows(top * xhat)
        sums[1] = sums[1] + fold_rows(top)
        sums[2] = sums[2] + fold_rows(down)
        m1_scr[rows] = down
        dfr_ref[rows] = down.astype(jnp.bfloat16)
    for part in range(parts):
        whole = slice(part * hidden, (part + 1) * hidden)
        u_scr[part % 2] = dot_nn(dfr_ref[...], w_scr[part_rows(part), hidden : 2 * hidden])
        for col in range(0, hidden, cols):
            place = slice(col, col + cols)
            wide = slice(part * hidden + col, part * hidden + col + cols)
            tally = jnp.zeros((8, cols), jnp.float32)
            for row in range(0, tile, small):
                rows = slice(row, row + small)
                low = (u_scr[part % 2, rows, place] * slope_scr[rows, wide]).astype(jnp.bfloat16)
                du_ref[rows, wide] = low
                tally = tally + fold_rows(low.astype(jnp.float32))
            up_sum_ref[:, wide] += tally
        lift = dot_nt(du_ref[:, whole], w_scr[part_rows(part), 0:hidden])
        if part == 0:
            acc[...] = lift
        else:
            acc[...] += lift
    for n, row in enumerate(range(0, tile, small)):
        rows = slice(row, row + small)
        back = m1_scr[rows] + acc[rows]
        xhat = xhat_scr[rows]
        sums[3] = sums[3] + fold_rows(back * xhat)
        sums[4] = sums[4] + fold_rows(back)
        gained = back * vector(1)
        down = first_scale[n] * (gained - row_mean(gained) - xhat * row_mean(gained * xhat))
        sums[5] = sums[5] + fold_rows(down)
        da_ref[rows] = down
        dar_ref[rows] = down.astype(jnp.bfloat16)
    for n in range(6):
        sum_ref[n] += sums[n]
    for n, do_ref in enumerate((do0, do1, do2, do3)):
        do_ref[...] = dot_nn(dar_ref[...], out_weight(n)).astype(jnp.bfloat16)

    @pl.when(step == pl.num_programs(0) - 1)
    def _totals():
        for n in range(6):
            total_ref[:, n * width : (n + 1) * width] = jnp.sum(
                sum_ref[n], axis=0, keepdims=True
            )
        total_ref[:, 6 * width :] = jnp.sum(up_sum_ref[...], axis=0, keepdims=True)


def token_block(rank, outs, own, cot, vectors, up_bias, weights):
    count, width = own.shape
    total_hidden = up_bias.shape[1]
    hidden = total_hidden // GROUP
    tile = 256

    def rows_of(columns):
        return pl.BlockSpec((tile, columns), lambda g, *_: (g, 0))

    def whole(shape):
        return pl.BlockSpec(shape, lambda g, *_: (0,) * len(shape))

    low = jnp.bfloat16
    head = outs[0].shape[1]
    return pl.pallas_call(
        functools.partial(token_kernel, tile, width, hidden),
        grid_spec=pltpu.PrefetchScalarGridSpec(
            num_scalar_prefetch=1,
            grid=(count // tile,),
            in_specs=[rows_of(head)] * 4
            + [rows_of(width)] * 2
            + [whole(vectors.shape), whole(up_bias.shape)] + [pl.BlockSpec(memory_space=pl.ANY)],
            out_specs=[
                rows_of(width),
                rows_of(width),
                rows_of(total_hidden),
                rows_of(total_hidden),
                rows_of(width),
                rows_of(width),
                rows_of(width),
                rows_of(head),
                rows_of(head),
                rows_of(head),
                rows_of(head),
                whole((1, 6 * width + total_hidden)),
            ],
            scratch_shapes=[
                pltpu.VMEM(weights.shape, low),
                pltpu.VMEM((tile, width), jnp.float32),
                pltpu.VMEM((2, tile, hidden), jnp.float32),
                pltpu.VMEM((tile, total_hidden), jnp.float32),
                pltpu.VMEM((tile, width), jnp.float32),
                pltpu.VMEM((tile, width), jnp.float32),
                pltpu.VMEM((6, 8, width), jnp.float32),
                pltpu.VMEM((8, total_hidden), jnp.float32),
                pltpu.SemaphoreType.DMA((3,)),
            ],
        ),
        out_shape=[
            jax.ShapeDtypeStruct((count, width), low),
            jax.ShapeDtypeStruct((count, width), low),
            jax.ShapeDtypeStruct((count, total_hidden), low),
            jax.ShapeDtypeStruct((count, total_hidden), low),
            jax.ShapeDtypeStruct((count, width), low),
            jax.ShapeDtypeStruct((count, width), low),
            jax.ShapeDtypeStruct((count, width), jnp.float32),
            jax.ShapeDtypeStruct((count, head), low),
            jax.ShapeDtypeStruct((count, head), low),
            jax.ShapeDtypeStruct((count, head), low),
            jax.ShapeDtypeStruct((count, head), low),
            jax.ShapeDtypeStruct((1, 6 * width + total_hidden), jnp.float32),
        ],
        compiler_params=pltpu.CompilerParams(
            dimension_semantics=("arbitrary",), vmem_limit_bytes=vmem_limit
        ),
        cost_estimate=pl.CostEstimate(
            flops=46 * 10**9, transcendentals=0, bytes_accessed=40 * 10**6
        ),
        name="token_block",
    )(rank.astype(jnp.int32).reshape(1), *outs, own, cot, vectors, up_bias, weights)


def weight_kernel(width, hidden, rank_ref, n1, dfr, dar, g, du, o0, o1, o2, o3, out_ref, n1_t, dfr_t, dar_t):
    part = pl.program_id(0)

    @pl.when(part == 0)
    def _turn():
        n1_t[...] = n1[...].T
        dfr_t[...] = dfr[...].T
        dar_t[...] = dar[...].T

    chunk = 384

    def product(n, carry):
        rows = pl.ds(pl.multiple_of(n * chunk, chunk), chunk)
        out_ref[rows, 0:hidden] = dot_nn(n1_t[rows], du[...]).astype(jnp.bfloat16)
        out_ref[rows, hidden : 2 * hidden] = dot_nn(dfr_t[rows], g[...]).astype(jnp.bfloat16)
        return carry

    lax.fori_loop(0, width // chunk, product, 0)
    for n, piece in enumerate((o0, o1, o2, o3)):

        @pl.when(part == rank_ref[0] ^ n)
        def _out(piece=piece):
            out_ref[:, 2 * hidden :] = dot_nn(dar_t[...], piece[...]).astype(jnp.bfloat16)


def weight_block(rank, n1, dfr, dar, g, du, outs):
    count, width = n1.shape
    hidden = g.shape[1] // GROUP
    head = outs[0].shape[1]
    columns = 2 * hidden + head
    low = jnp.bfloat16

    def whole(shape):
        return pl.BlockSpec(shape, lambda g, *_: (0,) * len(shape))

    return pl.pallas_call(
        functools.partial(weight_kernel, width, hidden),
        grid_spec=pltpu.PrefetchScalarGridSpec(
            num_scalar_prefetch=1,
            grid=(GROUP,),
            in_specs=[whole((count, width))] * 3
            + [pl.BlockSpec((count, hidden), lambda g, *_: (0, g))] * 2
            + [whole((count, head))] * 4,
            out_specs=pl.BlockSpec((width, columns), lambda g, *_: (g, 0)),
            scratch_shapes=[pltpu.VMEM((width, count), low)] * 3,
        ),
        out_shape=jax.ShapeDtypeStruct((GROUP * width, columns), low),
        compiler_params=pltpu.CompilerParams(
            dimension_semantics=("arbitrary",), vmem_limit_bytes=vmem_limit
        ),
        cost_estimate=pl.CostEstimate(
            flops=22 * 10**9, transcendentals=0, bytes_accessed=30 * 10**6
        ),
        name="weight_block",
    )(rank.astype(jnp.int32).reshape(1), n1, dfr, dar, g, du, *outs)


def pack_columns(query, key, value, axis):
    def piece(matrix, head):
        return lax.slice_in_dim(matrix, head * HD, (head + 1) * HD, axis=axis)

    return jnp.concatenate(
        [
            piece(value, 0),
            piece(key, 0),
            piece(key, 1),
            piece(value, 1),
            piece(value, 2),
            piece(key, 2),
            piece(query, 1),
            piece(query, 0),
            piece(query, 2),
        ],
        axis=axis,
    )


def insert_zero(packed, axis):
    head = lax.slice_in_dim(packed, 0, KV + 128, axis=axis)
    tail = lax.slice_in_dim(packed, KV + 128, KV + 192, axis=axis)
    return jnp.concatenate([head, jnp.zeros_like(tail), tail], axis=axis)


def drop_zero(packed, axis):
    head = lax.slice_in_dim(packed, 0, KV + 128, axis=axis)
    tail = lax.slice_in_dim(packed, KV + 192, KV + 256, axis=axis)
    return jnp.concatenate([head, tail], axis=axis)


def unpack_columns(packed, axis):
    def piece(n):
        return lax.slice_in_dim(packed, n * HD, (n + 1) * HD, axis=axis)

    query = jnp.concatenate([piece(7), piece(6), piece(8)], axis=axis)
    key = jnp.concatenate([piece(1), piece(2), piece(5)], axis=axis)
    value = jnp.concatenate([piece(0), piece(3), piece(4)], axis=axis)
    return query, key, value


def per_device(
    dp_size,
    tensor_size,
    inputs,
    cotangent,
    w_query,
    w_key,
    w_value,
    w_output,
    w_up,
    w_down,
    b_query,
    b_value,
    b_output,
    gain_attn,
    bias_attn,
    b_up,
    b_down,
    gain_mlp,
    bias_mlp,
    random_blocks,
):
    width = inputs.shape[1]
    hidden = b_up.shape[0]
    low = jnp.bfloat16
    dp_index = lax.axis_index("dp")
    tensor_index = lax.axis_index("tensor")
    core = dp_index % 2
    half = tensor_index // 2
    rank = 2 * core + tensor_index % 2
    here = core == half
    devices = [(d, t) for d in range(dp_size) for t in range(tensor_size)]
    pair_bits = [bit for bit in range(1, dp_size.bit_length() - 1)]

    def flat(d, t):
        return d * tensor_size + t

    def stays(d, t):
        return d % 2 == t // 2

    def flip(value, d_bits, t_bits, chosen=None):
        pairs = [
            (flat(d, t), flat(d ^ d_bits, t ^ t_bits))
            for d, t in devices
            if chosen is None or chosen(d, t)
        ]
        return lax.ppermute(value, both, pairs)

    def moves(d, t):
        return not stays(d, t)

    def rehome(value):
        return jnp.where(here, value, flip(value, 1, 2, moves))

    def near_of(value):
        return flip(value, 0, 1)

    def side_of(value):
        return flip(value, 1, 0)

    rest = jnp.concatenate([w_up, w_down.T, w_output.T], axis=1)

    packed = pack_columns(w_query, w_key, w_value, 1)
    columns = packed.shape[1]
    floats = jnp.concatenate([b_query, b_value])
    small = jnp.concatenate(split_three(floats) + [random_blocks.astype(low).reshape(-1)])
    small = jnp.pad(small, (0, -small.shape[0] % columns)).reshape(-1, columns)
    packed = jnp.concatenate([order_halves(core, packed, side_of(packed)), small], axis=0)
    packed_got = flip(packed, 0, 2, stays)

    moved = flip(inputs, 1, 2, moves)
    near_stay = flip(inputs, 0, 1, stays)
    moved, near_stay, packed_got, rest = lax.optimization_barrier(
        (moved, near_stay, packed_got, rest)
    )
    own = jnp.where(here, inputs, moved)
    near_move = flip(own, 0, 1, moves)
    own, packed_got, b_up = lax.optimization_barrier((own, packed_got, b_up))
    up_bias = jnp.stack([b_up] + [flip(b_up, 0, n) for n in (1, 2, 3)])
    rest = lax.all_gather(rest, "tensor", axis=0)
    packed = jnp.where(here, packed, packed_got)
    small = packed[2 * w_query.shape[0] :].reshape(-1)
    packed = packed[: 2 * w_query.shape[0]]
    for bit in pair_bits:
        packed = order_halves((dp_index >> bit) % 2, packed, flip(packed, 1 << bit, 0))
    w_qkv = insert_zero(packed, 1)
    count = floats.shape[0]
    mine = sum(small[n * count : (n + 1) * count].astype(jnp.float32) for n in range(3))
    my_random = small[3 * count : 3 * count + random_blocks.size]
    my_random = my_random.reshape(HEADS, NB, -1).astype(jnp.int32)
    b_key = jnp.zeros_like(b_query)
    b_qkv = insert_zero(pack_columns(mine[:192], b_key, mine[192:], 0), 0)
    scale = jnp.concatenate([jnp.ones((KV,), jnp.float32), jnp.full((256,), 0.125, jnp.float32)])
    near = jnp.where(here, near_stay, near_move)
    block = jnp.arange(NB, dtype=jnp.int32)
    block = block ^ (rank * QB)
    fixed = jnp.clip(
        jnp.stack(
            [
                jnp.zeros_like(block),
                jnp.full_like(block, NB - 1),
                block - 1,
                block,
                block + 1,
            ],
            axis=-1,
        ),
        0,
        NB - 1,
    )
    local_random = jnp.take(my_random, block, axis=1)
    table = jnp.concatenate(
        [jnp.broadcast_to(fixed[None], (HEADS, NB, 5)), local_random], axis=-1
    )
    table = (table ^ (rank * QB)).reshape(-1)

    b_up_all = jnp.concatenate(
        [lax.dynamic_index_in_dim(up_bias, tensor_index ^ n, 0) for n in range(GROUP)], axis=1
    )
    near, own, cotangent, w_qkv, b_qkv, table, b_up_all = lax.optimization_barrier(
        (near, own, cotangent, w_qkv, b_qkv, table, b_up_all)
    )
    side, far = side_of(own), side_of(near)
    cot_moved = flip(cotangent, 1, 2, moves)
    side, far, rest = lax.optimization_barrier((side, far, rest))
    rest_all = lax.all_gather(rest, "dp", axis=1, tiled=True).reshape(GROUP * width, -1)
    rows = (own, near, side, far)
    grad_top = jnp.where(here, cotangent, cot_moved)
    weights = (w_qkv, b_qkv[None], scale[None])
    out_near, out_far, out_side, probs, qkv = attend_forward((1, 3, 2), rank, table, rows, weights)
    out_own, probs = attend_forward((0,), rank, table, qkv=qkv, probs=probs)
    outs = (out_own, near_of(out_near), side_of(out_side), flip(out_far, 1, 1))

    vectors = jnp.stack([b_output, gain_attn, bias_attn, b_down, gain_mlp, bias_mlp])
    layer_out, n1, g, du, dfr, dar, da, *do, sums = token_block(
        rank, outs, own, grad_top, vectors, b_up_all, rest_all
    )
    grads = (do[0], near_of(do[1]), side_of(do[2]), flip(do[3], 1, 1))
    rest_grad = weight_block(rank, n1, dfr, dar, g, du, outs)
    sums = sums.reshape(-1)
    sums = sums + flip(sums, 0, 1)
    rest_grad, sums, *grads = lax.optimization_barrier((rest_grad, sums, *grads))
    rest_sum = lax.psum_scatter(
        rest_grad.reshape(GROUP, width, -1), "dp", scatter_dimension=1, tiled=True
    )
    layer_sent = flip(layer_out, 1, 2, moves)

    grad_qkv, base, to_near, to_side, to_far, bias_sum = attend_backward(
        table, probs, qkv, grads, (out_own, out_near, out_side, out_far), w_qkv, da
    )
    grad_qkv, base, to_near, to_side, to_far, bias_sum, layer_sent = lax.optimization_barrier(
        (grad_qkv, base, to_near, to_side, to_far, bias_sum, layer_sent)
    )
    side_far = side_of(to_far)
    side_own = side_of(to_side)
    bias_query, _, bias_value = unpack_columns(drop_zero(jnp.sum(bias_sum, axis=0), 0), 0)
    sums = jnp.concatenate([sums, bias_query, bias_value])
    sums = sums + flip(sums, 0, 2)
    to_near = (to_near.astype(jnp.float32) + side_far.astype(jnp.float32)).astype(low)
    to_near, sums = lax.optimization_barrier((to_near, sums))
    near_got = near_of(to_near)
    base = base + side_own.astype(jnp.float32)
    grad_late, to_near = lax.optimization_barrier((grad_qkv, to_near))
    for bit in pair_bits:
        sums = sums + flip(sums, 1 << bit, 0)
    other = side_of(sums)
    grad_late, sums = lax.optimization_barrier((grad_late, sums))
    grad_w = head_weight_block(rows, grad_late)
    rest_sum, base, grad_w = lax.optimization_barrier((rest_sum, base, grad_w))
    rest_sum = lax.psum_scatter(rest_sum, "tensor", scatter_dimension=0, tiled=False).astype(
        jnp.float32
    )
    for bit in reversed(pair_bits[2:]):
        grad_w = halve(flip, (dp_index >> bit) % 2, grad_w, 1 << bit, 0)
    place = (dp_index // 2) % 4
    rows_each = grad_w.shape[0] // 4
    total = lax.dynamic_slice_in_dim(grad_w, place * rows_each, rows_each, 0).astype(jnp.float32)
    for n in (3, 1, 2):
        send = lax.dynamic_slice_in_dim(grad_w, (place ^ n) * rows_each, rows_each, 0)
        total = total + flip(send, 2 * n, 0).astype(jnp.float32)
    grad_w = total.astype(low)
    near_got, grad_w, base, sums, other, layer_sent = lax.optimization_barrier(
        (near_got, grad_w, base, sums, other, layer_sent)
    )
    grad_own = (base + near_got.astype(jnp.float32)).astype(low)
    grad_own, grad_w, layer_sent = lax.optimization_barrier((grad_own, grad_w, layer_sent))
    grad_moved = flip(grad_own, 1, 2, moves)

    grad_got = flip(grad_w, 0, 2, moves)
    grad_w = grad_w.astype(jnp.float32) + grad_got.astype(jnp.float32)
    rows_each = grad_w.shape[0] // 2
    grad_w = grad_w.astype(low)
    keep = lax.dynamic_slice_in_dim(grad_w, core * rows_each, rows_each, 0)
    send = lax.dynamic_slice_in_dim(grad_w, (1 - core) * rows_each, rows_each, 0)
    side_got = side_of(send)
    grad_moved, side_got, rest_sum = lax.optimization_barrier((grad_moved, side_got, rest_sum))
    shard = jnp.where(here, keep, side_got).astype(jnp.float32)
    shard_query, shard_key, shard_value = unpack_columns(shard, 1)
    shard_up = rest_sum[:, :hidden]
    shard_down = rest_sum[:, hidden : 2 * hidden].T
    shard_output = rest_sum[:, 2 * hidden :].T
    layer_out = jnp.where(here, layer_out, layer_sent)
    grad_input = jnp.where(here, grad_own, grad_moved)

    count = 6 * width + GROUP * hidden
    bias_pair = jnp.where(here, sums[count:], other[count:])
    sums = sums + other
    top = sums[: 6 * width].reshape(6, width)
    grad_b_up = lax.dynamic_slice_in_dim(sums, 6 * width + tensor_index * hidden, hidden, 0)
    return (
        layer_out,
        grad_input,
        shard_query,
        shard_key,
        shard_value,
        shard_output,
        shard_up,
        shard_down,
        bias_pair[:192],
        bias_pair[192:],
        top[5],
        top[3],
        top[4],
        grad_b_up,
        top[2],
        top[0],
        top[1],
    )


def order_halves(bit, own, other):
    return jnp.where(
        bit == 0,
        jnp.concatenate([own, other], axis=0),
        jnp.concatenate([other, own], axis=0),
    )


def split_three(values):
    parts = []
    for _ in range(3):
        part = lax.reduce_precision(values, 8, 7)
        parts.append(part.astype(jnp.bfloat16))
        values = values - part
    return parts


def halve(flip, bit, value, d_bits, t_bits):
    rows = value.shape[0] // 2
    keep = lax.dynamic_slice_in_dim(value, bit * rows, rows, 0)
    send = lax.dynamic_slice_in_dim(value, (1 - bit) * rows, rows, 0)
    got = flip(send, d_bits, t_bits)
    return (keep.astype(jnp.float32) + got.astype(jnp.float32)).astype(value.dtype)


def solution(mesh):
    in_specs = (
        P(("dp", "tensor"), None),
        P(("dp", "tensor"), None),
        P("dp", "tensor"),
        P("dp", "tensor"),
        P("dp", "tensor"),
        P("tensor", "dp"),
        P("dp", "tensor"),
        P("tensor", "dp"),
        P("tensor"),
        P("tensor"),
        P(),
        P(),
        P(),
        P("tensor"),
        P(),
        P(),
        P(),
        P("tensor", None, None),
    )
    out_specs = (
        P(("dp", "tensor"), None),
        P(("dp", "tensor"), None),
        P("dp", "tensor"),
        P("dp", "tensor"),
        P("dp", "tensor"),
        P("tensor", "dp"),
        P("dp", "tensor"),
        P("tensor", "dp"),
        P("tensor"),
        P("tensor"),
        P(),
        P(),
        P(),
        P("tensor"),
        P(),
        P(),
        P(),
    )
    body = functools.partial(per_device, mesh.shape["dp"], mesh.shape["tensor"])
    return jax.shard_map(body, mesh=mesh, in_specs=in_specs, out_specs=out_specs, check_vma=False)
```
